128 devices in a mesh: member: 8 (over y, core), dp: 16 (over z, x).
Axes of the slice: x: 4, y: 4, z: 4, core: 2. Of those that a mesh axis runs over, the one named last changes fastest.
Arguments:
- observations: bfloat16 [4096, 1152], P(('member', 'dp')), may hold values from -6 to 6
- rollout: bfloat16 [4096, 384], P(('member', 'dp')), as said below
- done_flags: int32 [4096, 24], P(('member', 'dp')), may hold values 0 or 1
- member_ids: int32 [4096, 1], P(('member', 'dp')), may hold values from 0 to 15; in each aligned block of 32 rows (0 to 31, 32 to 63, ...) at most 6 rows name the same one
- embed_weight: float32 [16, 48, 256], P('member'), may hold values from -0.875 to 0.875
- conv_weight: float32 [16, 3, 2, 256, 256], P('member'), may hold values from -0.25 to 0.25
- trunk_in: float32 [16, 256, 512], P('member'), may hold values from -0.375 to 0.375
- trunk_mid: float32 [16, 512, 512], P('member'), may hold values from -0.25 to 0.25
- head_weight: float32 [16, 512, 13], P('member'), may hold values from -0.15625 to 0.15625
- log_std: float32 [16, 12], P('member'), may hold values from -0.1 to 0.1
Outputs:
- embed_dir: float32 [16, 48, 256], P('member', 'dp')
- conv_dir: float32 [16, 3, 2, 256, 256], P('member', None, None, 'dp')
- in_dir: float32 [16, 256, 512], P('member', 'dp')
- mid_dir: float32 [16, 512, 512], P('member', 'dp')
- head_dir: float32 [16, 512, 13], P('member', 'dp')
- std_dir: float32 [16, 12], P('member')
The draws below stay inside these ranges and needn't reach their ends.
Inputs may be any that keep to these rules, and one draw needn't show every extreme that they name: `member_ids`: in each shard's 32 rows no member is named more than 6 times, a bound that some block reaches. `rollout`: per step: 12 action values, reward, old value, next value, old log-probability.
All inputs are finite; a program needn't handle non-finite values. No bound on the sum of `done_flags` on one device may be relied on, other than what follows from the above.
Results may differ from the reference program's by a relative error of at most 0.023.
Values may be sent and summed in bfloat16 or wider, within the bound.
No kernel may reach another device: no remote copies, remote signals or barrier semaphores. Data moves between devices by JAX's collectives and lax.ppermute only.
A program may use at most 128 MiB of HBM per device.

```python
import math
from functools import partial
import jax
import jax.numpy as jnp
import numpy as np
from jax import lax

OBS = 48
STEPS = 24
ACT = 12
CHANNELS = 256
UNITS = 512
LAYERS = 3
CH_DEV = 32
MEMBERS = 16
CAP = 6
ENVS = 4096
PARAMS = 805388
N_MEMBER = 8
N_DP = 16


def draw_rollout(key, part):
    shape = (ENVS, STEPS, ACT + 4)
    base_draw = jax.random.normal(key, shape, jnp.float32)
    actions = base_draw[:, :, :ACT]
    reward = 0.5 * base_draw[:, :, ACT:ACT + 1]
    old_value = base_draw[:, :, ACT + 1:ACT + 2]
    next_value = base_draw[:, :, ACT + 2:ACT + 3]
    old_logp = -0.5 * jnp.sum(actions * actions, axis=2, keepdims=True) - ACT * 0.9189385332046727 + 0.3 * base_draw[:, :, ACT + 3:ACT + 4]
    joined = jnp.concatenate([actions, reward, old_value, next_value, old_logp], axis=2)
    return joined.reshape(ENVS, STEPS * (ACT + 4)).astype(jnp.bfloat16)


def set_ends(array, own_key, least, high):
    index_at = [jax.random.randint(jax.random.fold_in(own_key, axis), (), 0, length) for axis, length in enumerate(array.shape)]
    longest = array.shape.index(max(array.shape))
    next_to = index_at[:longest] + [(index_at[longest] + 1) % array.shape[longest]] + index_at[longest + 1:]
    return array.at[tuple(index_at)].set(least).at[tuple(next_to)].set(high)


def block_scale(stream_key, shape, shards, smallest, largest):
    level, own = 1.0, jax.random.fold_in(stream_key, 6)
    for dim, shards_of in shards:
        steps = jnp.exp(jax.random.uniform(jax.random.fold_in(own, dim), (shards_of,), jnp.float32, smallest / len(shards), largest / len(shards)))
        level = level * jnp.repeat(steps, shape[dim] // shards_of).reshape([-1 if axis == dim else 1 for axis in range(len(shape))])
    return level


def shared_out(key, own, number, rows, count, top, reach, lean):
    ranking = jax.random.permutation(key, count)
    heavy_load, common = load_shares(count, rows * top, reach, lean, True), load_shares(count, rows * top, reach, lean, False)
    places = jnp.arange(count)

    def named(tallies, turn):
        used = int((tallies > 0).sum())
        fixed = max(1, used // 4)
        moved = fixed + (places - fixed + turn * (used - fixed)) % max(1, count - fixed)
        return jnp.zeros((count,), jnp.int32).at[ranking[jnp.where(places < fixed, places, moved)]].set(jnp.asarray(tallies, jnp.int32))

    tallies = jnp.where(number % 4 == 0, named(heavy_load, number // 4), named(common, number - number // 4 - 1))
    mixed = jax.random.permutation(jax.random.fold_in(own, 3), count)
    source_of, receiver = mixed[0:count // 2 * 2:2], mixed[1:count // 2 * 2:2]
    room = jnp.minimum(tallies[source_of] - 1, reach - tallies[receiver]) // 2
    room = jnp.where((source_of == ranking[0]) | (receiver == ranking[0]) | (tallies[receiver] == 0), 0, jnp.maximum(room, 0))
    moved = jax.random.randint(jax.random.fold_in(own, 4), (count // 2,), 0, 1 << 20) % (room + 1)
    tallies = tallies.at[source_of].add(-moved).at[receiver].add(moved)
    members = jnp.searchsorted(jnp.cumsum(tallies), jnp.arange(rows * top), side="right").astype(jnp.int32)
    grid = members.reshape(top, rows).T
    grid = grid[jax.random.permutation(jax.random.fold_in(own, 1), rows)]
    turn = jax.random.randint(jax.random.fold_in(own, 2), (rows, 1), 0, top)
    return jnp.take_along_axis(grid, (jnp.arange(top)[None, :] + turn) % top, axis=1)


def load_shares(count, total, most, slope, full):
    portions = [(1 << 20) // math.isqrt(rank ** slope) + 1 for rank in range(1, count + 1)]
    largest = most if full else min(most, max(-(-total // count), total * portions[0] // sum(portions)))
    least = 1 if total - largest >= count - 1 else 0
    counts, rest = [largest] + [least] * (count - 1), total - largest - least * (count - 1)
    while rest > 0:
        candidates = [i for i in range(1, count) if counts[i] < largest] or [i for i in range(1, count) if counts[i] < most]
        whole, remaining = sum([portions[i] for i in candidates]), rest
        for i in candidates:
            addition = min(most - counts[i], max(1, remaining * portions[i] // whole), rest)
            counts[i] = counts[i] + addition
            rest = rest - addition
    return np.array(counts)


def scatter_about(stream_key, dims, width, most, cuts=(), held_as=jnp.bfloat16):
    values = width * jax.random.normal(stream_key, dims, jnp.float32)
    if cuts:
        values = values * block_scale(stream_key, dims, cuts, -0.22, 0.18)
    return jnp.clip(values, -most, most).astype(held_as)


def setup_inputs(seed: int = 0) -> dict:
    splits = jax.random.split(jax.random.key(seed), 11)
    observations = scatter_about(splits[0], (ENVS, STEPS * OBS), 1.0, 6.0, ((0, 128),))
    rollout = draw_rollout(jax.random.fold_in(splits[10], 71), 0)
    done_flags = set_ends((jax.random.randint(splits[2], (ENVS, STEPS), 0, STEPS) < 1).astype(jnp.int32), jax.random.fold_in(splits[2], 1), 0, 1)
    member_ids_keys = jax.random.split(jax.random.fold_in(splits[3], 1), ENVS // CH_DEV)
    member_ids_turns = jax.random.permutation(jax.random.fold_in(splits[3], 3), ENVS // CH_DEV)
    member_ids = jax.vmap(lambda own, number: shared_out(jax.random.fold_in(splits[3], 2), own, number, CH_DEV, MEMBERS, 1, CAP, 2))(member_ids_keys, member_ids_turns).reshape((ENVS, 1))
    embed_weight = scatter_about(splits[4], (MEMBERS, OBS, CHANNELS), OBS ** -0.5, 0.875, ((0, 8),), jnp.float32)
    conv_weight = scatter_about(splits[5], (MEMBERS, LAYERS, 2, CHANNELS, CHANNELS), (2 * CHANNELS) ** -0.5, 0.25, ((0, 8),), jnp.float32)
    trunk_in = scatter_about(splits[6], (MEMBERS, CHANNELS, UNITS), CHANNELS ** -0.5, 0.375, ((0, 8),), jnp.float32)
    trunk_mid = scatter_about(splits[7], (MEMBERS, UNITS, UNITS), UNITS ** -0.5, 0.25, ((0, 8),), jnp.float32)
    head_weight = scatter_about(splits[8], (MEMBERS, UNITS, ACT + 1), 0.01, 0.15625, ((0, 8),), jnp.float32)
    log_std = jnp.clip(jax.random.uniform(splits[9], (MEMBERS, ACT), jnp.float32, -0.1, 0.1) * block_scale(splits[9], (MEMBERS, ACT), ((0, 8),), -0.4, 0.0), -0.1, 0.1)
    return {"observations": observations, "rollout": rollout, "done_flags": done_flags, "member_ids": member_ids, "embed_weight": embed_weight, "conv_weight": conv_weight, "trunk_in": trunk_in, "trunk_mid": trunk_mid, "head_weight": head_weight, "log_std": log_std}


gamma_rate = 0.99
trace_rate = 0.95
penalty_weight = 0.5
value_weight = 0.5
half_log_tau = 0.9189385332046727

def advantages(reward, old_value, next_value, done_mask):
    alive = 1.0 - done_mask
    td_error = reward + gamma_rate * alive * next_value - old_value
    step_count = td_error.shape[1]
    running = td_error[:, step_count - 1]
    columns = [running]
    for step_index in range(step_count - 2, -1, -1):
        running = td_error[:, step_index] + gamma_rate * trace_rate * alive[:, step_index] * running
        columns.append(running)
    advantage = jnp.stack(columns[::-1], axis=1)
    return (advantage, advantage + old_value)

def policy_loss(weights, observations, rollout, done_mask, live_mask):
    embedding, conv_stack, trunk_first, trunk_second, head_mat, log_scale = weights
    row_count, step_count = done_mask.shape
    channels = embedding.shape[1]
    action_count = log_scale.shape[0]
    features = observations.reshape(row_count * step_count, embedding.shape[0])
    hidden = jnp.dot(features, embedding.astype(jnp.bfloat16), preferred_element_type=jnp.float32)
    for conv_layer in range(conv_stack.shape[0]):
        dilation = 2 ** conv_layer
        current = hidden.astype(jnp.bfloat16)
        shaped = current.reshape(row_count, step_count, channels)
        earlier = jnp.pad(shaped[:, :step_count - dilation], ((0, 0), (dilation, 0), (0, 0)))
        earlier = earlier.reshape(row_count * step_count, channels)
        mixing = jnp.dot(current, conv_stack[conv_layer, 0].astype(jnp.bfloat16), preferred_element_type=jnp.float32)
        mixing = mixing + jnp.dot(earlier, conv_stack[conv_layer, 1].astype(jnp.bfloat16), preferred_element_type=jnp.float32)
        hidden = hidden + jax.nn.elu(mixing)
    trunk_input = hidden.astype(jnp.bfloat16)
    first_units = jax.nn.elu(jnp.dot(trunk_input, trunk_first.astype(jnp.bfloat16), preferred_element_type=jnp.float32)).astype(jnp.bfloat16)
    second = jax.nn.elu(jnp.dot(first_units, trunk_second.astype(jnp.bfloat16), preferred_element_type=jnp.float32)).astype(jnp.bfloat16)
    head_out = jnp.dot(second, head_mat.astype(jnp.bfloat16), preferred_element_type=jnp.float32)
    action_mean = head_out[:, :action_count]
    value_pred = head_out[:, action_count]
    record = rollout.astype(jnp.float32).reshape(row_count, step_count, -1)
    action = record[:, :, :action_count].reshape(row_count * step_count, action_count)
    advantage, target_value = advantages(record[:, :, action_count], record[:, :, action_count + 1], record[:, :, action_count + 2], done_mask)
    old_logp = record[:, :, action_count + 3].reshape(-1)
    scaled = (action - action_mean) * jnp.exp(-log_scale)
    log_prob = lax.optimization_barrier(jnp.sum(-0.5 * scaled * scaled - log_scale, axis=1)) - action_count * half_log_tau
    log_ratio = log_prob - old_logp
    prob_ratio = jnp.exp(log_ratio)
    value_gap = value_pred - target_value.reshape(-1)
    per_step = -prob_ratio * advantage.reshape(-1) + penalty_weight * (prob_ratio - 1.0 - log_ratio) + 0.5 * value_weight * value_gap * value_gap
    weight = (live_mask[:, None] * jnp.ones((1, step_count), jnp.float32)).reshape(-1)
    return jnp.sum(per_step * weight)

def member_grad(weights, observations, rollout, done_mask, live_mask):
    total_loss, pullback = jax.vjp(partial(policy_loss, observations=observations, rollout=rollout, done_mask=done_mask, live_mask=live_mask), weights)
    return pullback(jnp.ones((), jnp.float32))[0]

def reference(observations, rollout, done_flags, member_ids, embed_weight, conv_weight, trunk_in, trunk_mid, head_weight, log_std):
    slot_count = N_MEMBER * CAP
    width_all = N_MEMBER * CH_DEV
    owner_table = member_ids[:, 0].reshape(N_MEMBER, N_DP, CH_DEV).transpose(1, 0, 2).reshape(N_DP, width_all)
    obs_table = observations.reshape(N_MEMBER, N_DP, CH_DEV, -1).transpose(1, 0, 2, 3).reshape(N_DP, width_all, -1)
    record_table = rollout.reshape(N_MEMBER, N_DP, CH_DEV, -1).transpose(1, 0, 2, 3).reshape(N_DP, width_all, -1)
    done_table = done_flags.reshape(N_MEMBER, N_DP, CH_DEV, -1).transpose(1, 0, 2, 3).reshape(N_DP, width_all, -1)
    position = jnp.arange(width_all, dtype=jnp.int32)

    def one_member(member_data):
        member, weights = member_data

        def one_shard(running_sum, shard_data):
            shard_owner, shard_obs, shard_record, shard_done = shard_data
            matches = shard_owner == member
            sort_key = jnp.where(matches, position, position + width_all).astype(jnp.int32)
            ordering = jnp.argsort(sort_key)[:slot_count].astype(jnp.int32)
            live_mask = matches[ordering].astype(jnp.float32)
            grads = member_grad(weights, shard_obs[ordering], shard_record[ordering], shard_done[ordering].astype(jnp.float32), live_mask)
            return (jax.tree.map(lambda running, adding: running + adding, running_sum, grads), None)
        zero_grads = jax.tree.map(jnp.zeros_like, weights)
        summed, unused = lax.scan(one_shard, zero_grads, (owner_table, obs_table, record_table, done_table))
        return summed
    all_weights = (embed_weight, conv_weight, trunk_in, trunk_mid, head_weight, log_std)
    gradients = lax.map(one_member, (jnp.arange(MEMBERS, dtype=jnp.int32), all_weights))
    squares = sum((lax.optimization_barrier(jnp.sum(grad_part * grad_part, axis=tuple(range(1, grad_part.ndim)))) for grad_part in gradients))
    root_mean = jnp.sqrt(squares / PARAMS + 1e-06)
    return tuple((grad_part / root_mean.reshape((-1,) + (1,) * (grad_part.ndim - 1)) for grad_part in gradients))
```

```python
import jax
import jax.numpy as jnp
from jax import lax
from jax.experimental import pallas as pl
from jax.experimental.pallas import tpu as pltpu
from jax.sharding import Mesh, PartitionSpec as P

gamma_rate = 0.99
trace_rate = 0.95
half_log_tau = 0.9189385332046727

OBS = 48
STEPS = 24
ACT = 12
CH = 256
UNITS = 512
MEMBERS = 16
CAP = 6
SLOT = 8
REC = 64
WIDTH = STEPS * REC
ENTRIES = 805388
SOURCES = 16
SPANS = SOURCES * CAP
CHUNK_STEPS = 8
CHUNKS = STEPS // CHUNK_STEPS
ROWS = CHUNK_STEPS * SPANS
ALL_ROWS = STEPS * SPANS
PAD = 4 * SPANS
SHARDS = 16
BLOCK = 208
FIRST_LANE = 3
f32 = jnp.float32
bf16 = jnp.bfloat16


def iota(shape, dim):
    return lax.broadcasted_iota(jnp.int32, shape, dim)


def dot(a, b):
    return jnp.dot(a, b, preferred_element_type=f32)


def dot_tn(a, b):
    return lax.dot_general(a, b, (((0,), (0,)), ((), ())), preferred_element_type=f32)


def dot_nt(a, b):
    return lax.dot_general(a, b, (((1,), (1,)), ((), ())), preferred_element_type=f32)


def onehot(cond):
    return jnp.where(cond, 1.0, 0.0).astype(bf16)


def pack_kernel(obs_ref, roll_ref, done_ref, ids_ref, out_ref):
    spans = obs_ref.shape[0]
    row, col = iota((STEPS * 16, 512), 0), iota((STEPS * 16, 512), 1)
    step = col & 127
    pick = onehot((row == 16 * step + 12 + (col >> 7)) & (step < STEPS))
    parts = dot(roll_ref[...], pick)
    reward, old_value = parts[:, 0:128], parts[:, 128:256]
    next_value, old_logp = parts[:, 256:384], parts[:, 384:512]
    widen = onehot(iota((STEPS, 128), 0) == iota((STEPS, 128), 1))
    done = dot(done_ref[...].astype(f32).astype(bf16), widen)
    lane = iota((spans, 128), 1)
    alive = jnp.where(lane < STEPS, 1.0 - done, 0.0)
    advantage = reward + gamma_rate * alive * next_value - old_value
    carry = gamma_rate * trace_rate * alive
    for shift in (1, 2, 4, 8, 16):
        advantage = advantage + carry * pltpu.roll(advantage, 128 - shift, 1)
        carry = carry * pltpu.roll(carry, 128 - shift, 1)
    target = jnp.where(lane < STEPS, advantage + old_value, 0.0)
    advantage = jnp.where(lane < STEPS, advantage, 0.0)
    scalars = jnp.concatenate([target.astype(bf16), advantage.astype(bf16), old_logp.astype(bf16)], axis=1)

    col = iota((384, 512), 1)
    row = iota((384, 512), 0)
    spot, within = col & 63, col >> 6
    place_obs = onehot((row == 48 * within + spot) & (spot < 48))
    place_act = onehot((row == 16 * within + spot - 48) & (spot >= 48) & (spot < 60))[0:128]
    live = jnp.where((iota((spans, 512), 1) & 63) == 63, 1.0, 0.0)
    groups = []
    for g in range(3):
        place_scal = onehot((spot >= 60) & (spot < 63) & (row == (spot - 60) * 128 + 8 * g + within))
        placed = dot(obs_ref[:, 384 * g : 384 * g + 384], place_obs)
        placed = placed + dot(roll_ref[:, 128 * g : 128 * g + 128], place_act)
        placed = placed + dot(scalars, place_scal) + live
        groups.append(placed.astype(bf16))

    ids = ids_ref[...]
    named = (lane == ids).astype(f32)
    lower = onehot(iota((spans, spans), 0) > iota((spans, spans), 1))
    before = dot(lower, named.astype(bf16))
    rank = jnp.sum(before * named, axis=1, keepdims=True)
    slot = ids * SLOT + rank.astype(jnp.int32)
    dispatch = onehot(lane == slot)
    for g in range(3):
        out_ref[:, 512 * g : 512 * g + 512] = dot_tn(dispatch, groups[g]).astype(bf16)


def pack(observations, rollout, done_flags, member_ids):
    return pl.pallas_call(
        pack_kernel,
        out_shape=jax.ShapeDtypeStruct((MEMBERS * SLOT, WIDTH), bf16),
        name="pack",
    )(observations, rollout, done_flags, member_ids)


def weights_kernel(which_ref, embed_ref, conv_ref, in_ref, mid_ref, head_ref, embed_out, conv_out, in_out, mid_out, head_out):
    row, col = iota((128, 256), 0), iota((128, 256), 1)
    embed = embed_ref[0].astype(bf16)
    r, k = iota((128, OBS), 0), iota((128, OBS), 1)
    for half in range(2):
        spread = onehot(r == k + REC * half)
        embed_out[:, 256 * half : 256 * half + 256] = dot(spread, embed).astype(bf16)
    even = (row - 48 == col - FIRST_LANE) & (row >= 48) & (row < 64)
    odd = (row - 112 == col - 128 - FIRST_LANE) & (row >= 112)
    embed_out[:, 512:768] = onehot(even | odd)
    for layer in range(3):
        for tap in range(2):
            conv_out[2 * layer + tap] = conv_ref[0, layer, tap].astype(bf16)
    in_out[...] = in_ref[0].astype(bf16)
    mid_out[...] = mid_ref[0].astype(bf16)
    a, lane = iota((ACT + 1, 128), 0), iota((ACT + 1, 128), 1)
    head_out[...] = dot(head_ref[0].astype(bf16), onehot(a + FIRST_LANE == lane)).astype(bf16)


def prepare(which, embed, conv, trunk_in, trunk_mid, head):
    def one(shape):
        return pl.BlockSpec((1,) + shape, lambda i, w: (w[0],) + (0,) * len(shape))

    def whole(shape):
        return pl.BlockSpec(shape, lambda i, w: (0,) * len(shape))

    outs = ((128, 768), (6, CH, CH), (CH, UNITS), (UNITS, UNITS), (UNITS, 128))
    return pl.pallas_call(
        weights_kernel,
        grid_spec=pltpu.PrefetchScalarGridSpec(
            num_scalar_prefetch=1,
            grid=(1,),
            in_specs=[one(x.shape[1:]) for x in (embed, conv, trunk_in, trunk_mid, head)],
            out_specs=[whole(s) for s in outs],
        ),
        out_shape=[jax.ShapeDtypeStruct(s, bf16) for s in outs],
        cost_estimate=pl.CostEstimate(flops=0, bytes_accessed=5_000_000, transcendentals=0),
        name="weights",
    )(which, embed, conv, trunk_in, trunk_mid, head)


def grad_kernel(
    recv_ref, embed_ref, conv_ref, in_ref, mid_ref, head_ref, scale_ref,
    send_ref, stat_ref,
    xc, hid, rec, c0, c1, c2, c3, g0, g1, g2, first, second, dout, dp2, dp1, dhid, dm0, dm1, dm2, dpair,
    acc_conv, acc_in, acc_mid, acc_head,
):
    cs, gs, dms = (c0, c1, c2), (g0, g1, g2), (dm0, dm1, dm2)
    for ref in cs:
        ref[0:PAD, :] = jnp.zeros((PAD, CH), bf16)
    for ref in dms:
        ref[ALL_ROWS : ALL_ROWS + PAD, :] = jnp.zeros((PAD, CH), bf16)
    acc_conv[...] = jnp.zeros_like(acc_conv)
    acc_in[...] = jnp.zeros_like(acc_in)
    acc_mid[...] = jnp.zeros_like(acc_mid)
    acc_head[...] = jnp.zeros_like(acc_head)
    stat_ref[...] = jnp.zeros_like(stat_ref)

    r, k = iota((SPANS, SOURCES * SLOT), 0), iota((SPANS, SOURCES * SLOT), 1)
    compact = onehot(((k & 7) < CAP) & (r == (k >> 3) * CAP + (k & 7)))
    lane1 = iota((1, 128), 1)
    is_act = (lane1 >= FIRST_LANE) & (lane1 < FIRST_LANE + ACT)
    log_scale = scale_ref[0:1, :]
    inverse = jnp.where(is_act, jnp.exp(-log_scale), 0.0)
    offset = jnp.sum(jnp.where(is_act, log_scale, 0.0), axis=1, keepdims=True) + ACT * half_log_tau

    @pl.loop(0, CHUNKS)
    def _(i):
        base = i * ROWS
        for p in range(CHUNK_STEPS // 2):
            pair = i * (CHUNK_STEPS // 2) + p
            x = recv_ref[:, pl.ds(pl.multiple_of(pair * 128, 128), 128)]
            x = dot(compact, x).astype(bf16)
            xc[pl.ds(pl.multiple_of(pair * SPANS, 16), SPANS), :] = x
            y = dot(x, embed_ref[...])
            for half in range(2):
                at = (2 * p + half) * SPANS
                h = y[:, 256 * half : 256 * half + 256]
                hid[at : at + SPANS, :] = h
                c0[pl.ds(pl.multiple_of(base + PAD + at, 16), SPANS), :] = h.astype(bf16)
                rec[at : at + SPANS, :] = y[:, 512 + 128 * half : 640 + 128 * half]
        for layer in range(3):
            c, g = cs[layer], gs[layer]
            lag = SPANS * 2**layer
            mix = dot(c[pl.ds(pl.multiple_of(base + PAD, 16), ROWS), :], conv_ref[2 * layer])
            mix = mix + dot(c[pl.ds(pl.multiple_of(base + PAD - lag, 16), ROWS), :], conv_ref[2 * layer + 1])
            grown = jnp.exp(jnp.minimum(mix, 0.0))
            h = hid[...] + jnp.where(mix > 0, mix, grown - 1.0)
            g[pl.ds(pl.multiple_of(base, 16), ROWS), :] = grown.astype(bf16)
            if layer < 2:
                hid[...] = h
                cs[layer + 1][pl.ds(pl.multiple_of(base + PAD, 16), ROWS), :] = h.astype(bf16)
            else:
                c3[...] = h.astype(bf16)

        def elu(x):
            return jnp.where(x > 0, x, jnp.exp(jnp.minimum(x, 0.0)) - 1.0).astype(bf16)

        def slope(y):
            return jnp.minimum(y.astype(f32), 0.0) + 1.0

        for n in range(0, UNITS, 256):
            first[:, n : n + 256] = elu(dot(c3[...], in_ref[:, n : n + 256]))
        for n in range(0, UNITS, 256):
            second[:, n : n + 256] = elu(dot(first[...], mid_ref[:, n : n + 256]))
        out = dot(second[...], head_ref[...])
        record = rec[...]
        diff = record - out
        scaled = diff * inverse
        square = scaled * scaled
        advantage = record[:, FIRST_LANE + 13 : FIRST_LANE + 14]
        old_logp = record[:, FIRST_LANE + 14 : FIRST_LANE + 15]
        live = record[:, FIRST_LANE + 15 : FIRST_LANE + 16]
        log_ratio = -0.5 * jnp.sum(square, axis=1, keepdims=True) - offset - old_logp
        ratio = jnp.exp(log_ratio)
        dlog = live * (0.5 * (ratio - 1.0) - ratio * advantage)
        dvalue = -0.5 * live * diff
        d = jnp.where(lane1 == FIRST_LANE + ACT, dvalue, dlog * scaled * inverse)
        dout[...] = d.astype(bf16)
        stat_ref[0:1, :] += jnp.where(is_act, jnp.sum(dlog * (square - 1.0), axis=0, keepdims=True), 0.0)
        for n in range(0, UNITS, 256):
            ds = dot_nt(dout[...], head_ref[n : n + 256, :])
            dp2[:, n : n + 256] = (ds * slope(second[:, n : n + 256])).astype(bf16)
        for n in range(0, UNITS, 256):
            df = dot_nt(dp2[...], mid_ref[n : n + 256, :])
            dp1[:, n : n + 256] = (df * slope(first[:, n : n + 256])).astype(bf16)
        dhid[pl.ds(pl.multiple_of(base, 16), ROWS), :] = dot_nt(dp1[...], in_ref[...])
        acc_head[...] += dot_tn(dout[...], second[...])
        for n in range(0, UNITS, 256):
            acc_mid[n : n + 256, :] += dot_tn(first[:, n : n + 256], dp2[...])
        acc_in[...] += dot_tn(c3[...], dp1[...])

    @pl.loop(0, CHUNKS)
    def _(j):
        i = CHUNKS - 1 - j
        base = i * ROWS
        here = pl.ds(pl.multiple_of(base, 16), ROWS)
        for layer in (2, 1, 0):
            c, g, dm = cs[layer], gs[layer], dms[layer]
            lag = SPANS * 2**layer
            dh = dhid[here, :]
            dm[here, :] = (dh * g[here, :].astype(f32)).astype(bf16)
            dc = dot_nt(dm[here, :], conv_ref[2 * layer])
            dc = dc + dot_nt(dm[pl.ds(pl.multiple_of(base + lag, 16), ROWS), :], conv_ref[2 * layer + 1])
            dh = dh + dc
            if layer > 0:
                dhid[here, :] = dh
            else:
                for s in range(CHUNK_STEPS):
                    at = pl.ds(pl.multiple_of(i * (ROWS // 2) + (s // 2) * SPANS, 16), SPANS)
                    dpair[at, 256 * (s % 2) : 256 * (s % 2) + 256] = dh[s * SPANS : s * SPANS + SPANS].astype(bf16)
            acc_conv[2 * layer] += dot_tn(c[pl.ds(pl.multiple_of(base + PAD, 16), ROWS), :], dm[here, :])
            acc_conv[2 * layer + 1] += dot_tn(c[pl.ds(pl.multiple_of(base + PAD - lag, 16), ROWS), :], dm[here, :])

    dembed = dot_tn(xc[...], dpair[...])
    dembed = (dembed[0:OBS, 0:256] + dembed[REC : REC + OBS, 256:512]).astype(bf16)
    r, k = iota((SHARDS * 16, OBS), 0), iota((SHARDS * 16, OBS), 1)
    spread = onehot(((r & 15) < 3) & (k == (r >> 4) * 3 + (r & 15)))
    extra = dot(spread, dembed).astype(bf16)
    dhead = acc_head[0:16, :]
    for s in range(SHARDS):
        for q in range(6):
            send_ref[s, 16 * q : 16 * q + 16, :] = acc_conv[q, 16 * s : 16 * s + 16, :].astype(bf16)
        for n in range(2):
            send_ref[s, 96 + 16 * n : 112 + 16 * n, :] = acc_in[16 * s : 16 * s + 16, 256 * n : 256 * n + 256].astype(bf16)
            send_ref[s, 128 + 32 * n : 160 + 32 * n, :] = acc_mid[32 * s : 32 * s + 32, 256 * n : 256 * n + 256].astype(bf16)
        send_ref[s, 192:208, :] = extra[16 * s : 16 * s + 16, :]
        moved = jnp.where(iota((16, 32), 0) >= FIRST_LANE, dhead[:, 32 * s : 32 * s + 32].astype(bf16).astype(f32), extra[16 * s : 16 * s + 16, 0:32].astype(f32))
        send_ref[s, 192:208, 0:32] = moved.astype(bf16)


def member_grad(recv, embed, conv, trunk_in, trunk_mid, head, scale):
    v = pltpu.VMEM
    half = ALL_ROWS // 2
    return pl.pallas_call(
        grad_kernel,
        out_shape=(
            jax.ShapeDtypeStruct((SHARDS, BLOCK, 256), bf16),
            jax.ShapeDtypeStruct((8, 128), f32),
        ),
        scratch_shapes=[
            v((half, 128), bf16), v((ROWS, CH), f32), v((ROWS, 128), f32),
            v((PAD + ALL_ROWS, CH), bf16), v((PAD + ALL_ROWS, CH), bf16), v((PAD + ALL_ROWS, CH), bf16),
            v((ROWS, CH), bf16),
            v((ALL_ROWS, CH), bf16), v((ALL_ROWS, CH), bf16), v((ALL_ROWS, CH), bf16),
            v((ROWS, UNITS), bf16), v((ROWS, UNITS), bf16), v((ROWS, 128), bf16),
            v((ROWS, UNITS), bf16), v((ROWS, UNITS), bf16),
            v((ALL_ROWS, CH), f32),
            v((ALL_ROWS + PAD, CH), bf16), v((ALL_ROWS + PAD, CH), bf16), v((ALL_ROWS + PAD, CH), bf16),
            v((half, 512), bf16),
            v((6, CH, CH), f32), v((CH, UNITS), f32), v((UNITS, UNITS), f32), v((128, UNITS), f32),
        ],
        cost_estimate=pl.CostEstimate(flops=11_200_000_000, bytes_accessed=4_000_000, transcendentals=4_000_000),
        compiler_params=pltpu.CompilerParams(vmem_limit_bytes=56 * 1024 * 1024),
        name="grad",
    )(recv, embed, conv, trunk_in, trunk_mid, head, scale)


def reduce_kernel(recv_ref, stat_ref, sum_ref, cast_ref):
    row, lane = iota((16, 256), 0), iota((16, 256), 1)
    ok = (row < FIRST_LANE) | (lane < 32)
    squares = []
    for member in range(2):
        total = recv_ref[member].astype(f32)
        for source in range(member + 2, SHARDS, 2):
            total = total + recv_ref[source].astype(f32)
        sum_ref[member] = total
        square = jnp.sum(total[0:192] * total[0:192]) + jnp.sum(jnp.where(ok, total[192:208] * total[192:208], 0.0))
        squares.append(square)
    lane1 = iota((1, 128), 1)
    line = jnp.where(lane1 == 0, squares[0], jnp.where(lane1 == 1, squares[1], 0.0)) + pltpu.roll(stat_ref[0:1, :], 32, 1)
    for s in range(SHARDS):
        cast_ref[8 * s : 8 * s + 8, :] = jnp.broadcast_to(line, (8, 128))


def reduce_parts(recv, stat):
    return pl.pallas_call(
        reduce_kernel,
        out_shape=(jax.ShapeDtypeStruct((2, BLOCK, 256), f32), jax.ShapeDtypeStruct((SHARDS * 8, 128), f32)),
        name="reduce",
    )(recv, stat)


def finish_kernel(sum_ref, cast_ref, embed_ref, conv_ref, in_ref, mid_ref, head_ref, std_ref):
    lines = [cast_ref[8 * s : 8 * s + 1, :] for s in range(SHARDS)]
    lane1 = iota((1, 128), 1)
    total = sum(lines[1:], lines[0])
    for member in range(2):
        mine = lines[member]
        for s in range(member + 2, SHARDS, 2):
            mine = mine + lines[s]
        lo = 32 + FIRST_LANE
        std = jnp.where((lane1 >= lo) & (lane1 < lo + ACT), mine, 0.0)
        square = jnp.sum(std * std, axis=1, keepdims=True) + total[:, member : member + 1]
        scale = 1.0 / jnp.sqrt(square / ENTRIES + 1e-06)
        std_ref[member : member + 1, :] = (std * scale)[:, lo : lo + ACT]
        part = sum_ref.at[member]
        for q in range(6):
            conv_ref[member, q // 2, q % 2] = part[16 * q : 16 * q + 16, :] * scale
        for n in range(2):
            in_ref[member, :, 256 * n : 256 * n + 256] = part[96 + 16 * n : 112 + 16 * n, :] * scale
            mid_ref[member, :, 256 * n : 256 * n + 256] = part[128 + 32 * n : 160 + 32 * n, :] * scale
        embed_ref[member] = part[192:195, :] * scale
        head = (part[192:208, 0:128] * scale).T
        head_ref[member] = head[0:32, FIRST_LANE:16]


def finish(sums, cast):
    shapes = ((2, 3, 256), (2, 3, 2, 16, 256), (2, 16, 512), (2, 32, 512), (2, 32, 13), (2, 12))
    return pl.pallas_call(
        finish_kernel,
        out_shape=tuple(jax.ShapeDtypeStruct(s, f32) for s in shapes),
        name="finish",
    )(sums, cast)


def local(observations, rollout, done_flags, member_ids, embed_weight, conv_weight, trunk_in, trunk_mid, head_weight, log_std):
    which = lax.axis_index("xl").astype(jnp.int32)
    packed = pack(observations, rollout, done_flags, member_ids)
    recv = lax.all_to_all(packed, ("member", "xl"), split_axis=0, concat_axis=0, tiled=True)
    prepared = prepare(which.reshape(1), embed_weight, conv_weight, trunk_in, trunk_mid, head_weight)
    scale = jnp.pad(lax.dynamic_index_in_dim(log_std, which, 0), ((0, 7), (FIRST_LANE, 128 - ACT - FIRST_LANE)))
    send, stat = member_grad(recv, *prepared, scale)
    parts = lax.all_to_all(send, ("z", "xh", "xl"), split_axis=0, concat_axis=0, tiled=True)
    sums, cast = reduce_parts(parts, stat)
    cast = lax.all_to_all(cast, ("z", "xh", "xl"), split_axis=0, concat_axis=0, tiled=True)
    return finish(sums, cast)


def solution(mesh):
    fine = Mesh(mesh.devices.reshape(8, 4, 2, 2), ("member", "z", "xh", "xl"))
    dp = ("z", "xh", "xl")
    every = ("member",) + dp
    return jax.shard_map(
        local,
        mesh=fine,
        in_specs=(P(every), P(every), P(every), P(every)) + (P("member"),) * 6,
        out_specs=(
            P("member", dp),
            P("member", None, None, dp),
            P("member", dp),
            P("member", dp),
            P("member", dp),
            P("member"),
        ),
        check_vma=False,
    )
```

```python
import jax
import jax.numpy as jnp
from jax import lax
from jax.experimental import pallas as pl
from jax.experimental.pallas import tpu as pltpu
from jax.sharding import Mesh, PartitionSpec as P

gamma_rate = 0.99
trace_rate = 0.95
half_log_tau = 0.9189385332046727

OBS = 48
STEPS = 24
ACT = 12
CH = 256
UNITS = 512
MEMBERS = 16
CAP = 6
SLOT = 8
REC = 64
WIDTH = STEPS * REC
ENTRIES = 805388
SOURCES = 16
SPANS = SOURCES * CAP
CHUNK_STEPS = 8
CHUNKS = STEPS // CHUNK_STEPS
ROWS = CHUNK_STEPS * SPANS
ALL_ROWS = STEPS * SPANS
PAD = 4 * SPANS
SHARDS = 16
BLOCK = 208
FIRST_LANE = 3
f32 = jnp.float32
bf16 = jnp.bfloat16


def iota(shape, dim):
    return lax.broadcasted_iota(jnp.int32, shape, dim)


def dot(a, b):
    return jnp.dot(a, b, preferred_element_type=f32)


def dot_tn(a, b):
    return lax.dot_general(a, b, (((0,), (0,)), ((), ())), preferred_element_type=f32)


def dot_nt(a, b):
    return lax.dot_general(a, b, (((1,), (1,)), ((), ())), preferred_element_type=f32)


def onehot(cond):
    return jnp.where(cond, 1.0, 0.0).astype(bf16)


def pack_kernel(obs_ref, roll_ref, done_ref, ids_ref, out_ref):
    spans = obs_ref.shape[0]
    row, col = iota((STEPS * 16, 512), 0), iota((STEPS * 16, 512), 1)
    step = col & 127
    pick = onehot((row == 16 * step + 12 + (col >> 7)) & (step < STEPS))
    parts = dot(roll_ref[...], pick)
    reward, old_value = parts[:, 0:128], parts[:, 128:256]
    next_value, old_logp = parts[:, 256:384], parts[:, 384:512]
    widen = onehot(iota((STEPS, 128), 0) == iota((STEPS, 128), 1))
    done = dot_tn(done_ref[...].astype(f32).astype(bf16), widen)
    lane = iota((spans, 128), 1)
    alive = jnp.where(lane < STEPS, 1.0 - done, 0.0)
    advantage = reward + gamma_rate * alive * next_value - old_value
    carry = gamma_rate * trace_rate * alive
    for shift in (1, 2, 4, 8, 16):
        advantage = advantage + carry * pltpu.roll(advantage, 128 - shift, 1)
        carry = carry * pltpu.roll(carry, 128 - shift, 1)
    target = jnp.where(lane < STEPS, advantage + old_value, 0.0)
    advantage = jnp.where(lane < STEPS, advantage, 0.0)
    scalars = jnp.concatenate([target.astype(bf16), advantage.astype(bf16), old_logp.astype(bf16)], axis=1)

    col = iota((384, 512), 1)
    row = iota((384, 512), 0)
    spot, within = col & 63, col >> 6
    place_obs = onehot((row == 48 * within + spot) & (spot < 48))
    place_act = onehot((row == 16 * within + spot - 48) & (spot >= 48) & (spot < 60))[0:128]
    live = jnp.where((iota((spans, 512), 1) & 63) == 63, 1.0, 0.0)
    groups = []
    for g in range(3):
        place_scal = onehot((spot >= 60) & (spot < 63) & (row == (spot - 60) * 128 + 8 * g + within))
        placed = dot(obs_ref[:, 384 * g : 384 * g + 384], place_obs)
        placed = placed + dot(roll_ref[:, 128 * g : 128 * g + 128], place_act)
        placed = placed + dot(scalars, place_scal) + live
        groups.append(placed.astype(bf16))

    slots = MEMBERS * SLOT
    ids = ids_ref[...]
    slot, span = iota((slots, spans), 0), iota((slots, spans), 1)
    named = onehot(iota((MEMBERS, spans), 0) == ids)
    earlier = onehot(iota((spans, spans), 0) < iota((spans, spans), 1))
    rank = jnp.sum(dot(named, earlier) * named.astype(f32), axis=0, keepdims=True)
    dispatch = onehot(slot == ids * SLOT + rank.astype(jnp.int32))
    for g in range(3):
        out_ref[:, 512 * g : 512 * g + 512] = dot(dispatch, groups[g]).astype(bf16)


def pack(observations, rollout, done_flags, member_ids):
    return pl.pallas_call(
        pack_kernel,
        out_shape=jax.ShapeDtypeStruct((MEMBERS * SLOT, WIDTH), bf16),
        name="pack",
    )(observations, rollout, done_flags.T, member_ids.T)


def weights_kernel(
    which_ref, embed_ref, conv_ref, in_ref, mid_ref, head_ref, scale_ref,
    embed_out, conv_out, in_out, mid_out, head_out, scale_out,
):
    embed = embed_ref[0].astype(bf16)
    r, k = iota((128, OBS), 0), iota((128, OBS), 1)
    for half in range(2):
        spread = onehot(r == k + REC * half)
        embed_out[:, 256 * half : 256 * half + 256] = dot(spread, embed).astype(bf16)
    for layer in range(3):
        for tap in range(2):
            conv_out[layer, 256 * tap : 256 * tap + 256, :] = conv_ref[0, layer, tap].astype(bf16)
    in_out[...] = in_ref[0].astype(bf16)
    mid_out[...] = mid_ref[0].astype(bf16)
    first = which_ref[0] == 0
    head = jnp.where(first, head_ref[:, 0, :], head_ref[:, 1, :]).astype(bf16)
    spread = onehot(iota((16, ACT + 1), 0) == iota((16, ACT + 1), 1) + FIRST_LANE)
    head_out[...] = dot(spread, head).astype(bf16)
    scale = jnp.where(first, scale_ref[0:1, :], scale_ref[1:2, :])
    at = iota((16, ACT), 0) == iota((16, ACT), 1) + FIRST_LANE
    column = jnp.sum(jnp.where(at, scale, 0.0), axis=1, keepdims=True)
    scale_out[...] = jnp.broadcast_to(column, (16, 128))


def prepare(which, embed, conv, trunk_in, trunk_mid, head, log_std):
    def one(shape):
        return pl.BlockSpec((1,) + shape, lambda i, w: (w[0],) + (0,) * len(shape))

    def whole(shape):
        return pl.BlockSpec(shape, lambda i, w: (0,) * len(shape))

    head = head.transpose(2, 0, 1)
    outs = ((128, 512), (3, 2 * CH, CH), (CH, UNITS), (UNITS, UNITS), (16, UNITS))
    return pl.pallas_call(
        weights_kernel,
        grid_spec=pltpu.PrefetchScalarGridSpec(
            num_scalar_prefetch=1,
            grid=(1,),
            in_specs=[one(x.shape[1:]) for x in (embed, conv, trunk_in, trunk_mid)] + [whole(head.shape), whole(log_std.shape)],
            out_specs=[whole(s) for s in outs] + [whole((16, 128))],
        ),
        out_shape=[jax.ShapeDtypeStruct(s, bf16) for s in outs] + [jax.ShapeDtypeStruct((16, 128), f32)],
        cost_estimate=pl.CostEstimate(flops=0, bytes_accessed=5_000_000, transcendentals=0),
        compiler_params=pltpu.CompilerParams(vmem_limit_bytes=16 * 1024 * 1024),
        name="weights",
    )(which, embed, conv, trunk_in, trunk_mid, head, log_std)


def grad_kernel(
    recv_ref, embed_ref, conv_ref, in_ref, mid_ref, head_ref, scale_ref,
    send_ref, stat_ref,
    xc, xt, hid, c0, c1, c2, c3, g0, g1, g2, first, second, dout, dp2, dp1, dhid, dm0, dm1, dm2, dpair,
    acc_conv, acc_in, acc_mid, acc_head, acc_stat,
):
    cs, gs, dms = (c0, c1, c2), (g0, g1, g2), (dm0, dm1, dm2)
    for ref in cs:
        ref[0:PAD, :] = jnp.zeros((PAD, CH), bf16)
    for ref in dms:
        ref[ALL_ROWS : ALL_ROWS + PAD, :] = jnp.zeros((PAD, CH), bf16)
    for ref in (acc_conv, acc_in, acc_mid, acc_head, acc_stat):
        ref[...] = jnp.zeros_like(ref)

    r, k = iota((SPANS, SOURCES * SLOT), 0), iota((SPANS, SOURCES * SLOT), 1)
    compact = onehot(((k & 7) < CAP) & (r == (k >> 3) * CAP + (k & 7)))
    r, k = iota((64, 128), 0), iota((64, 128), 1)
    entry = r & 31
    select = onehot((entry >= FIRST_LANE) & (entry < FIRST_LANE + 16) & (k == entry + 48 - FIRST_LANE + (r >> 5) * REC))
    sub = iota((16, 1), 0)
    is_act = (sub >= FIRST_LANE) & (sub < FIRST_LANE + ACT)
    log_scale = scale_ref[:, 0:1]
    inverse = jnp.where(is_act, jnp.exp(-log_scale), 0.0)
    offset = jnp.sum(jnp.where(is_act, log_scale, 0.0), axis=0, keepdims=True) + ACT * half_log_tau
    lane = iota((1, ROWS), 1)
    odd = lane < 0
    for s in range(1, CHUNK_STEPS, 2):
        odd = odd | ((lane >= s * SPANS) & (lane < (s + 1) * SPANS))

    @pl.loop(0, CHUNKS)
    def _(i):
        base = i * ROWS
        pairs = CHUNK_STEPS // 2
        x = recv_ref[:, pl.ds(pl.multiple_of(i * (pairs * 128), 128), pairs * 128)]
        x = dot(compact, x).astype(bf16)
        half_rows = pl.ds(pl.multiple_of(i * (ROWS // 2), 16), ROWS // 2)
        for p in range(pairs):
            part = x[:, 128 * p : 128 * p + 128]
            xc[pl.ds(pl.multiple_of(i * (ROWS // 2) + p * SPANS, 16), SPANS), :] = part
            xt[2 * p * SPANS : (2 * p + 1) * SPANS, :] = part
            xt[(2 * p + 1) * SPANS : (2 * p + 2) * SPANS, :] = part
        y = dot(xc[half_rows, :], embed_ref[...])
        for p in range(pairs):
            for half in range(2):
                at = (2 * p + half) * SPANS
                h = y[p * SPANS : (p + 1) * SPANS, 256 * half : 256 * half + 256]
                hid[at : at + SPANS, :] = h
                c0[pl.ds(pl.multiple_of(base + PAD + at, 16), SPANS), :] = h.astype(bf16)
        for layer in range(3):
            c, g = cs[layer], gs[layer]
            lag = SPANS * 2**layer
            both = jnp.concatenate(
                [c[pl.ds(pl.multiple_of(base + PAD, 16), ROWS), :], c[pl.ds(pl.multiple_of(base + PAD - lag, 16), ROWS), :]],
                axis=1,
            )
            mix = dot(both, conv_ref[layer])
            grown = jnp.exp(mix)
            h = hid[...] + jnp.maximum(mix, jnp.minimum(grown - 1.0, 0.0))
            g[pl.ds(pl.multiple_of(base, 16), ROWS), :] = jnp.minimum(grown.astype(bf16), jnp.ones((), bf16))
            if layer < 2:
                hid[...] = h
                cs[layer + 1][pl.ds(pl.multiple_of(base + PAD, 16), ROWS), :] = h.astype(bf16)
            else:
                c3[...] = h.astype(bf16)

        def elu(x):
            below = jnp.minimum((jnp.exp(x) - 1.0).astype(bf16), jnp.zeros((), bf16))
            return jnp.maximum(x.astype(bf16), below)

        def slope(y):
            return jnp.minimum(y, jnp.zeros((), bf16)) + jnp.ones((), bf16)

        for n in range(0, UNITS, 256):
            first[:, n : n + 256] = elu(dot(c3[...], in_ref[:, n : n + 256]))
        for n in range(0, UNITS, 256):
            second[:, n : n + 256] = elu(dot(first[...], mid_ref[:, n : n + 256]))
        out = dot_nt(head_ref[...], second[...])
        record = dot_nt(select, xt[...])
        record = jnp.where(odd, record[32:64], record[0:32])
        diff = record[0:16] - out
        scaled = diff * inverse
        square = scaled * scaled
        advantage = record[FIRST_LANE + 13 : FIRST_LANE + 14]
        old_logp = record[FIRST_LANE + 14 : FIRST_LANE + 15]
        live = record[FIRST_LANE + 15 : FIRST_LANE + 16]
        log_ratio = -0.5 * jnp.sum(square, axis=0, keepdims=True) - offset - old_logp
        ratio = jnp.exp(log_ratio)
        dlog = live * (0.5 * (ratio - 1.0) - ratio * advantage)
        dvalue = -0.5 * live * diff
        d = jnp.where(sub == FIRST_LANE + ACT, dvalue, dlog * scaled * inverse)
        dout[...] = d.astype(bf16)
        acc_stat[...] += jnp.sum(dlog * (square - 1.0), axis=1, keepdims=True)
        acc_head[...] += dot(dout[...], second[...])
        for n in range(0, UNITS, 256):
            ds = dot_tn(dout[...], head_ref[:, n : n + 256])
            dp2[:, n : n + 256] = ds.astype(bf16) * slope(second[:, n : n + 256])
        for n in range(0, UNITS, 256):
            df = dot_nt(dp2[...], mid_ref[n : n + 256, :])
            dp1[:, n : n + 256] = df.astype(bf16) * slope(first[:, n : n + 256])
        dhid[pl.ds(pl.multiple_of(base, 16), ROWS), :] = dot_nt(dp1[...], in_ref[...])
        for n in range(0, UNITS, 256):
            acc_mid[n : n + 256, :] += dot_tn(first[:, n : n + 256], dp2[...])
        acc_in[...] += dot_tn(c3[...], dp1[...])

    @pl.loop(0, CHUNKS)
    def _(j):
        i = CHUNKS - 1 - j
        base = i * ROWS
        here = pl.ds(pl.multiple_of(base, 16), ROWS)
        for layer in (2, 1, 0):
            c, g, dm = cs[layer], gs[layer], dms[layer]
            lag = SPANS * 2**layer
            dh = dhid[here, :]
            dm[here, :] = dh.astype(bf16) * g[here, :]
            dc = dot_nt(dm[here, :], conv_ref[layer, 0:256, :])
            dc = dc + dot_nt(dm[pl.ds(pl.multiple_of(base + lag, 16), ROWS), :], conv_ref[layer, 256:512, :])
            dh = dh + dc
            if layer > 0:
                dhid[here, :] = dh
            else:
                for s in range(CHUNK_STEPS):
                    at = pl.ds(pl.multiple_of(i * (ROWS // 2) + (s // 2) * SPANS, 16), SPANS)
                    dpair[at, 256 * (s % 2) : 256 * (s % 2) + 256] = dh[s * SPANS : s * SPANS + SPANS].astype(bf16)
            acc_conv[2 * layer] += dot_tn(c[pl.ds(pl.multiple_of(base + PAD, 16), ROWS), :], dm[here, :])
            acc_conv[2 * layer + 1] += dot_tn(c[pl.ds(pl.multiple_of(base + PAD - lag, 16), ROWS), :], dm[here, :])

    dembed = dot_tn(xc[...], dpair[...])
    dembed = (dembed[0:OBS, 0:256] + dembed[REC : REC + OBS, 256:512]).astype(bf16)
    r, k = iota((SHARDS * 16, OBS), 0), iota((SHARDS * 16, OBS), 1)
    spread = onehot(((r & 15) < 3) & (k == (r >> 4) * 3 + (r & 15)))
    extra = dot(spread, dembed).astype(bf16)
    dhead = acc_head[...]
    for s in range(SHARDS):
        for q in range(6):
            send_ref[s, 16 * q : 16 * q + 16, :] = acc_conv[q, 16 * s : 16 * s + 16, :].astype(bf16)
        for n in range(2):
            send_ref[s, 96 + 16 * n : 112 + 16 * n, :] = acc_in[16 * s : 16 * s + 16, 256 * n : 256 * n + 256].astype(bf16)
            send_ref[s, 128 + 32 * n : 160 + 32 * n, :] = acc_mid[32 * s : 32 * s + 32, 256 * n : 256 * n + 256].astype(bf16)
        send_ref[s, 192:208, :] = extra[16 * s : 16 * s + 16, :]
        moved = jnp.where(iota((16, 32), 0) >= FIRST_LANE, dhead[:, 32 * s : 32 * s + 32].astype(bf16).astype(f32), extra[16 * s : 16 * s + 16, 0:32].astype(f32))
        send_ref[s, 192:208, 0:32] = moved.astype(bf16)
    at = (iota((16, 128), 0) == iota((16, 128), 1)) & is_act
    line = jnp.sum(jnp.where(at, acc_stat[...], 0.0), axis=0, keepdims=True)
    stat_ref[...] = jnp.broadcast_to(line, (8, 128))


def member_grad(recv, embed, conv, trunk_in, trunk_mid, head, scale):
    v = pltpu.VMEM
    half = ALL_ROWS // 2
    return pl.pallas_call(
        grad_kernel,
        out_shape=(
            jax.ShapeDtypeStruct((SHARDS, BLOCK, 256), bf16),
            jax.ShapeDtypeStruct((8, 128), f32),
        ),
        scratch_shapes=[
            v((half, 128), bf16), v((ROWS, 128), bf16), v((ROWS, CH), f32),
            v((PAD + ALL_ROWS, CH), bf16), v((PAD + ALL_ROWS, CH), bf16), v((PAD + ALL_ROWS, CH), bf16),
            v((ROWS, CH), bf16),
            v((ALL_ROWS, CH), bf16), v((ALL_ROWS, CH), bf16), v((ALL_ROWS, CH), bf16),
            v((ROWS, UNITS), bf16), v((ROWS, UNITS), bf16), v((16, ROWS), bf16),
            v((ROWS, UNITS), bf16), v((ROWS, UNITS), bf16),
            v((ALL_ROWS, CH), f32),
            v((ALL_ROWS + PAD, CH), bf16), v((ALL_ROWS + PAD, CH), bf16), v((ALL_ROWS + PAD, CH), bf16),
            v((half, 512), bf16),
            v((6, CH, CH), f32), v((CH, UNITS), f32), v((UNITS, UNITS), f32), v((16, UNITS), f32), v((16, 128), f32),
        ],
        cost_estimate=pl.CostEstimate(flops=11_200_000_000, bytes_accessed=4_000_000, transcendentals=4_000_000),
        compiler_params=pltpu.CompilerParams(vmem_limit_bytes=36 * 1024 * 1024),
        name="grad",
    )(recv, embed, conv, trunk_in, trunk_mid, head, scale)


def reduce_kernel(recv_ref, stat_ref, sum_ref, cast_ref):
    row, lane = iota((16, 256), 0), iota((16, 256), 1)
    ok = (row < FIRST_LANE) | (lane < 32)
    squares = []
    for member in range(2):
        total = recv_ref[member].astype(f32)
        for source in range(member + 2, SHARDS, 2):
            total = total + recv_ref[source].astype(f32)
        sum_ref[member] = total
        square = jnp.sum(total[0:192] * total[0:192]) + jnp.sum(jnp.where(ok, total[192:208] * total[192:208], 0.0))
        squares.append(square)
    lane1 = iota((1, 128), 1)
    line = jnp.where(lane1 == 0, squares[0], jnp.where(lane1 == 1, squares[1], 0.0)) + pltpu.roll(stat_ref[0:1, :], 32, 1)
    for s in range(SHARDS):
        cast_ref[8 * s : 8 * s + 8, :] = jnp.broadcast_to(line, (8, 128))


def reduce_parts(recv, stat):
    return pl.pallas_call(
        reduce_kernel,
        out_shape=(jax.ShapeDtypeStruct((2, BLOCK, 256), f32), jax.ShapeDtypeStruct((SHARDS * 8, 128), f32)),
        name="reduce",
    )(recv, stat)


def finish_kernel(sum_ref, cast_ref, embed_ref, conv_ref, in_ref, mid_ref, head_ref, std_ref):
    lines = [cast_ref[8 * s : 8 * s + 1, :] for s in range(SHARDS)]
    lane1 = iota((1, 128), 1)
    total = sum(lines[1:], lines[0])
    for member in range(2):
        mine = lines[member]
        for s in range(member + 2, SHARDS, 2):
            mine = mine + lines[s]
        lo = 32 + FIRST_LANE
        std = jnp.where((lane1 >= lo) & (lane1 < lo + ACT), mine, 0.0)
        square = jnp.sum(std * std, axis=1, keepdims=True) + total[:, member : member + 1]
        scale = 1.0 / jnp.sqrt(square / ENTRIES + 1e-06)
        std_ref[member : member + 1, :] = (std * scale)[:, lo : lo + ACT]
        part = sum_ref.at[member]
        for q in range(6):
            conv_ref[member, q // 2, q % 2] = part[16 * q : 16 * q + 16, :] * scale
        for n in range(2):
            in_ref[member, :, 256 * n : 256 * n + 256] = part[96 + 16 * n : 112 + 16 * n, :] * scale
            mid_ref[member, :, 256 * n : 256 * n + 256] = part[128 + 32 * n : 160 + 32 * n, :] * scale
        embed_ref[:, member, :] = part[192:195, :] * scale
        head_ref[:, member, :] = part[192 + FIRST_LANE : 208, 0:32] * scale


def finish(sums, cast):
    shapes = ((3, 2, 256), (2, 3, 2, 16, 256), (2, 16, 512), (2, 32, 512), (13, 2, 32), (2, 12))
    embed, conv, first, second, head, std = pl.pallas_call(
        finish_kernel,
        out_shape=tuple(jax.ShapeDtypeStruct(s, f32) for s in shapes),
        name="finish",
    )(sums, cast)
    return embed.transpose(1, 0, 2), conv, first, second, head.transpose(1, 2, 0), std


def local(observations, rollout, done_flags, member_ids, embed_weight, conv_weight, trunk_in, trunk_mid, head_weight, log_std):
    which = lax.axis_index("xl").astype(jnp.int32)
    packed = pack(observations, rollout, done_flags, member_ids)
    recv = lax.all_to_all(packed, ("member", "xl"), split_axis=0, concat_axis=0, tiled=True)
    prepared = prepare(which.reshape(1), embed_weight, conv_weight, trunk_in, trunk_mid, head_weight, log_std)
    send, stat = member_grad(recv, *prepared)
    parts = lax.all_to_all(send, ("z", "xh", "xl"), split_axis=0, concat_axis=0, tiled=True)
    sums, cast = reduce_parts(parts, stat)
    cast = lax.all_to_all(cast, ("z", "xh", "xl"), split_axis=0, concat_axis=0, tiled=True)
    return finish(sums, cast)


def solution(mesh):
    fine = Mesh(mesh.devices.reshape(8, 4, 2, 2), ("member", "z", "xh", "xl"))
    dp = ("z", "xh", "xl")
    every = ("member",) + dp
    return jax.shard_map(
        local,
        mesh=fine,
        in_specs=(P(every), P(every), P(every), P(every)) + (P("member"),) * 6,
        out_specs=(
            P("member", dp),
            P("member", None, None, dp),
            P("member", dp),
            P("member", dp),
            P("member", dp),
            P("member"),
        ),
        check_vma=False,
    )
```

```python
import jax
import jax.numpy as jnp
from jax import lax
from jax.experimental import pallas as pl
from jax.experimental.pallas import tpu as pltpu
from jax.sharding import Mesh, PartitionSpec as P

gamma_rate = 0.99
trace_rate = 0.95
half_log_tau = 0.9189385332046727

OBS = 48
STEPS = 24
ACT = 12
CH = 256
UNITS = 512
MEMBERS = 16
CAP = 6
SLOT = 8
REC = 64
WIDTH = STEPS * REC
ENTRIES = 805388
SOURCES = 16
SPANS = SOURCES * CAP
CHUNK_STEPS = 8
CHUNKS = STEPS // CHUNK_STEPS
ROWS = CHUNK_STEPS * SPANS
ALL_ROWS = STEPS * SPANS
PAD = 4 * SPANS
SHARDS = 16
HALF = 104
W_IN, W_MID, W_EMBED, W_HEAD, W_ROWS = 1536, 2048, 3072, 3328, 3360
f32 = jnp.float32
bf16 = jnp.bfloat16


def iota(shape, dim):
    return lax.broadcasted_iota(jnp.int32, shape, dim)


def dot(a, b):
    return jnp.dot(a, b, preferred_element_type=f32)


def dot_tn(a, b):
    return lax.dot_general(a, b, (((0,), (0,)), ((), ())), preferred_element_type=f32)


def dot_nt(a, b):
    return lax.dot_general(a, b, (((1,), (1,)), ((), ())), preferred_element_type=f32)


def onehot(cond):
    return jnp.where(cond, 1.0, 0.0).astype(bf16)


def pack_kernel(obs_ref, roll_ref, done_ref, ids_ref, out_ref):
    spans = obs_ref.shape[0]
    row, col = iota((STEPS * 16, 512), 0), iota((STEPS * 16, 512), 1)
    step = col & 127
    pick = onehot((row == 16 * step + 12 + (col >> 7)) & (step < STEPS))
    parts = dot(roll_ref[...], pick)
    reward, old_value = parts[:, 0:128], parts[:, 128:256]
    next_value, old_logp = parts[:, 256:384], parts[:, 384:512]
    widen = onehot(iota((STEPS, 128), 0) == iota((STEPS, 128), 1))
    done = dot_tn(done_ref[...].astype(f32).astype(bf16), widen)
    lane = iota((spans, 128), 1)
    alive = jnp.where(lane < STEPS, 1.0 - done, 0.0)
    advantage = reward + gamma_rate * alive * next_value - old_value
    carry = gamma_rate * trace_rate * alive
    for shift in (1, 2, 4, 8, 16):
        advantage = advantage + carry * pltpu.roll(advantage, 128 - shift, 1)
        carry = carry * pltpu.roll(carry, 128 - shift, 1)
    target = jnp.where(lane < STEPS, advantage + old_value, 0.0)
    advantage = jnp.where(lane < STEPS, advantage, 0.0)
    scalars = jnp.concatenate([target.astype(bf16), advantage.astype(bf16), old_logp.astype(bf16)], axis=1)

    col = iota((384, 512), 1)
    row = iota((384, 512), 0)
    spot, within = col & 63, col >> 6
    place_obs = onehot((row == 48 * within + spot) & (spot < 48))
    place_act = onehot((row == 16 * within + spot - 48) & (spot >= 48) & (spot < 60))[0:128]
    live = jnp.where((iota((spans, 512), 1) & 63) == 63, 1.0, 0.0)
    groups = []
    for g in range(3):
        place_scal = onehot((spot >= 60) & (spot < 63) & (row == (spot - 60) * 128 + 8 * g + within))
        placed = dot(obs_ref[:, 384 * g : 384 * g + 384], place_obs)
        placed = placed + dot(roll_ref[:, 128 * g : 128 * g + 128], place_act)
        placed = placed + dot(scalars, place_scal) + live
        groups.append(placed.astype(bf16))

    slots = MEMBERS * SLOT
    ids = ids_ref[...]
    slot, span = iota((slots, spans), 0), iota((slots, spans), 1)
    named = onehot(iota((MEMBERS, spans), 0) == ids)
    earlier = onehot(iota((spans, spans), 0) < iota((spans, spans), 1))
    rank = jnp.sum(dot(named, earlier) * named.astype(f32), axis=0, keepdims=True)
    dispatch = onehot(slot == ids * SLOT + rank.astype(jnp.int32))
    for g in range(3):
        out_ref[:, 512 * g : 512 * g + 512] = dot(dispatch, groups[g]).astype(bf16)


def pack(observations, rollout, done_flags, member_ids):
    return pl.pallas_call(
        pack_kernel,
        out_shape=jax.ShapeDtypeStruct((MEMBERS * SLOT, WIDTH), bf16),
        name="pack",
    )(observations, rollout, done_flags.T, member_ids.T)


def weights_kernel(which_ref, embed_ref, conv_ref, in_ref, mid_ref, head_ref, out_ref):
    for layer in range(3):
        for tap in range(2):
            at = CH * (2 * layer + tap)
            out_ref[at : at + CH, :] = conv_ref[0, layer, tap].astype(bf16)
    head = jnp.where(which_ref[0] == 0, head_ref[:, 0, :], head_ref[:, 1, :]).astype(bf16)
    head = dot(onehot(iota((16, ACT + 1), 0) == iota((16, ACT + 1), 1)), head).astype(bf16)
    embed = embed_ref[0].astype(bf16)
    r, k = iota((128, OBS), 0), iota((128, OBS), 1)
    for n in range(2):
        cols = slice(256 * n, 256 * n + 256)
        out_ref[W_IN + CH * n : W_IN + CH * n + CH, :] = in_ref[0, :, cols].astype(bf16)
        out_ref[W_MID + UNITS * n : W_MID + UNITS * n + UNITS, :] = mid_ref[0, :, cols].astype(bf16)
        out_ref[W_EMBED + 128 * n : W_EMBED + 128 * n + 128, :] = dot(onehot(r == k + REC * n), embed).astype(bf16)
        out_ref[W_HEAD + 16 * n : W_HEAD + 16 * n + 16, :] = head[:, cols]


def prepare(which, embed, conv, trunk_in, trunk_mid, head):
    def one(shape):
        return pl.BlockSpec((1,) + shape, lambda i, w: (w[0],) + (0,) * len(shape))

    def whole(shape):
        return pl.BlockSpec(shape, lambda i, w: (0,) * len(shape))

    head = head.transpose(2, 0, 1)
    return pl.pallas_call(
        weights_kernel,
        grid_spec=pltpu.PrefetchScalarGridSpec(
            num_scalar_prefetch=1,
            grid=(1,),
            in_specs=[one(x.shape[1:]) for x in (embed, conv, trunk_in, trunk_mid)] + [whole(head.shape)],
            out_specs=whole((W_ROWS, CH)),
        ),
        out_shape=jax.ShapeDtypeStruct((W_ROWS, CH), bf16),
        cost_estimate=pl.CostEstimate(flops=0, bytes_accessed=5_000_000, transcendentals=0),
        compiler_params=pltpu.CompilerParams(vmem_limit_bytes=60 * 1024 * 1024),
        name="weights",
    )(which, embed, conv, trunk_in, trunk_mid, head)


def grad_kernel(
    flags_ref, recv_ref, w_ref, scale_ref, other_ref,
    keep_ref, give_ref, stat_ref,
    xc, xt, hid, c0, c1, c2, c3, g0, g1, g2, first, second, dout, dp2, dp1, dhid, dm0, dm1, dm2, dpair,
    acc_conv, acc_in, acc_mid, acc_head, acc_stat,
):
    cs, gs, dms = (c0, c1, c2), (g0, g1, g2), (dm0, dm1, dm2)
    for ref in cs:
        ref[0:PAD, :] = jnp.zeros((PAD, CH), bf16)
    for ref in dms:
        ref[ALL_ROWS : ALL_ROWS + PAD, :] = jnp.zeros((PAD, CH), bf16)
    for ref in (acc_conv, acc_in, acc_mid, acc_head, acc_stat):
        ref[...] = jnp.zeros_like(ref)

    r, k = iota((SPANS, SOURCES * SLOT), 0), iota((SPANS, SOURCES * SLOT), 1)
    compact = onehot(((k & 7) < CAP) & (r == (k >> 3) * CAP + (k & 7)))
    r, k = iota((64, 128), 0), iota((64, 128), 1)
    entry = r & 31
    select = onehot((entry < 16) & (k == entry + OBS + (r >> 5) * REC))
    sub = iota((16, 1), 0)
    is_act = sub < ACT
    scale = jnp.where(flags_ref[1] == 1, scale_ref[...], other_ref[...])
    scale = jnp.where(flags_ref[0] == 0, scale[0:1, :], scale[1:2, :])
    log_scale = jnp.sum(jnp.where(iota((16, ACT), 0) == iota((16, ACT), 1), scale, 0.0), axis=1, keepdims=True)
    conv = [w_ref.at[2 * CH * layer : 2 * CH * layer + 2 * CH] for layer in range(3)]
    in_half = [w_ref.at[W_IN + CH * n : W_IN + CH * n + CH] for n in range(2)]
    mid_half = [w_ref.at[W_MID + UNITS * n : W_MID + UNITS * n + UNITS] for n in range(2)]
    embed_half = [w_ref.at[W_EMBED + 128 * n : W_EMBED + 128 * n + 128] for n in range(2)]
    head_half = [w_ref.at[W_HEAD + 16 * n : W_HEAD + 16 * n + 16] for n in range(2)]

    def across(halves, rows):
        return jnp.concatenate([half[rows, :] for half in halves], axis=1)
    inverse = jnp.where(is_act, jnp.exp(-log_scale), 0.0)
    offset = jnp.sum(jnp.where(is_act, log_scale, 0.0), axis=0, keepdims=True) + ACT * half_log_tau
    lane = iota((1, ROWS), 1)
    odd = lane < 0
    for s in range(1, CHUNK_STEPS, 2):
        odd = odd | ((lane >= s * SPANS) & (lane < (s + 1) * SPANS))

    @pl.loop(0, CHUNKS)
    def _(i):
        base = i * ROWS
        pairs = CHUNK_STEPS // 2
        x = recv_ref[:, pl.ds(pl.multiple_of(i * (pairs * 128), 128), pairs * 128)]
        x = dot(compact, x).astype(bf16)
        half_rows = pl.ds(pl.multiple_of(i * (ROWS // 2), 16), ROWS // 2)
        for p in range(pairs):
            part = x[:, 128 * p : 128 * p + 128]
            xc[pl.ds(pl.multiple_of(i * (ROWS // 2) + p * SPANS, 16), SPANS), :] = part
            xt[2 * p * SPANS : (2 * p + 1) * SPANS, :] = part
            xt[(2 * p + 1) * SPANS : (2 * p + 2) * SPANS, :] = part
        y = [dot(xc[half_rows, :], half[...]) for half in embed_half]
        for p in range(pairs):
            for half in range(2):
                at = (2 * p + half) * SPANS
                h = y[half][p * SPANS : (p + 1) * SPANS, :]
                hid[at : at + SPANS, :] = h
                c0[pl.ds(pl.multiple_of(base + PAD + at, 16), SPANS), :] = h.astype(bf16)
        for layer in range(3):
            c, g = cs[layer], gs[layer]
            lag = SPANS * 2**layer
            both = jnp.concatenate(
                [c[pl.ds(pl.multiple_of(base + PAD, 16), ROWS), :], c[pl.ds(pl.multiple_of(base + PAD - lag, 16), ROWS), :]],
                axis=1,
            )
            mix = dot(both, conv[layer][...])
            grown = jnp.exp(mix)
            h = hid[...] + jnp.maximum(mix, jnp.minimum(grown - 1.0, 0.0))
            g[pl.ds(pl.multiple_of(base, 16), ROWS), :] = jnp.minimum(grown.astype(bf16), jnp.ones((), bf16))
            if layer < 2:
                hid[...] = h
                cs[layer + 1][pl.ds(pl.multiple_of(base + PAD, 16), ROWS), :] = h.astype(bf16)
            else:
                c3[...] = h.astype(bf16)

        def elu(x):
            below = jnp.minimum((jnp.exp(x) - 1.0).astype(bf16), jnp.zeros((), bf16))
            return jnp.maximum(x.astype(bf16), below)

        def slope(y):
            return jnp.minimum(y, jnp.zeros((), bf16)) + jnp.ones((), bf16)

        for n in range(0, UNITS, 256):
            first[:, n : n + 256] = elu(dot(c3[...], in_half[n // 256][...]))
        for n in range(0, UNITS, 256):
            second[:, n : n + 256] = elu(dot(first[...], mid_half[n // 256][...]))
        out = dot_nt(across(head_half, slice(0, 16)), second[...])
        record = dot_nt(select, xt[...])
        record = jnp.where(odd, record[32:64], record[0:32])
        diff = record[0:16] - out
        scaled = diff * inverse
        square = scaled * scaled
        advantage = record[13:14]
        old_logp = record[14:15]
        live = record[15:16]
        log_ratio = -0.5 * jnp.sum(square, axis=0, keepdims=True) - offset - old_logp
        ratio = jnp.exp(log_ratio)
        dlog = live * (0.5 * (ratio - 1.0) - ratio * advantage)
        dvalue = -0.5 * live * diff
        d = jnp.where(sub == ACT, dvalue, dlog * scaled * inverse)
        dout[...] = d.astype(bf16)
        acc_stat[...] += jnp.sum(dlog * (square - 1.0), axis=1, keepdims=True)
        acc_head[...] += dot(dout[...], second[...])
        for n in range(0, UNITS, 256):
            ds = dot_tn(dout[...], head_half[n // 256][...])
            dp2[:, n : n + 256] = ds.astype(bf16) * slope(second[:, n : n + 256])
        for n in range(0, UNITS, 256):
            df = dot_nt(dp2[...], across(mid_half, slice(n, n + 256)))
            dp1[:, n : n + 256] = df.astype(bf16) * slope(first[:, n : n + 256])
        dhid[pl.ds(pl.multiple_of(base, 16), ROWS), :] = dot_nt(dp1[...], across(in_half, slice(0, CH)))
        for n in range(0, UNITS, 256):
            acc_mid[n : n + 256, :] += dot_tn(first[:, n : n + 256], dp2[...])
        acc_in[...] += dot_tn(c3[...], dp1[...])

    @pl.loop(0, CHUNKS)
    def _(j):
        i = CHUNKS - 1 - j
        base = i * ROWS
        here = pl.ds(pl.multiple_of(base, 16), ROWS)
        for layer in (2, 1, 0):
            c, g, dm = cs[layer], gs[layer], dms[layer]
            lag = SPANS * 2**layer
            dh = dhid[here, :]
            dm[here, :] = dh.astype(bf16) * g[here, :]
            dc = dot_nt(dm[here, :], conv[layer][0:256, :])
            dc = dc + dot_nt(dm[pl.ds(pl.multiple_of(base + lag, 16), ROWS), :], conv[layer][256:512, :])
            dh = dh + dc
            if layer > 0:
                dhid[here, :] = dh
            else:
                for s in range(CHUNK_STEPS):
                    at = pl.ds(pl.multiple_of(i * (ROWS // 2) + (s // 2) * SPANS, 16), SPANS)
                    dpair[at, 256 * (s % 2) : 256 * (s % 2) + 256] = dh[s * SPANS : s * SPANS + SPANS].astype(bf16)
            acc_conv[2 * layer] += dot_tn(c[pl.ds(pl.multiple_of(base + PAD, 16), ROWS), :], dm[here, :])
            acc_conv[2 * layer + 1] += dot_tn(c[pl.ds(pl.multiple_of(base + PAD - lag, 16), ROWS), :], dm[here, :])

    dembed = dot_tn(xc[...], dpair[...])
    dembed = (dembed[0:OBS, 0:256] + dembed[REC : REC + OBS, 256:512]).astype(bf16)
    r, k = iota((SHARDS * 8, OBS), 0), iota((SHARDS * 8, OBS), 1)
    spread = onehot(((r & 7) < 3) & (k == (r >> 3) * 3 + (r & 7)))
    extra = dot(spread, dembed).astype(bf16)
    dhead = acc_head[...].astype(bf16)

    def write(encoder_ref, trunk_ref):
        for s in range(SHARDS):
            for q in range(6):
                encoder_ref[s, 16 * q : 16 * q + 16, :] = acc_conv[q, 16 * s : 16 * s + 16, :].astype(bf16)
            encoder_ref[s, 96:104, :] = extra[8 * s : 8 * s + 8, :]
            for n in range(2):
                cols = slice(256 * n, 256 * n + 256)
                trunk_ref[s, 16 * n : 16 * n + 16, :] = acc_in[16 * s : 16 * s + 16, cols].astype(bf16)
                trunk_ref[s, 32 + 32 * n : 64 + 32 * n, :] = acc_mid[32 * s : 32 * s + 32, cols].astype(bf16)
            trunk_ref[s, 96:104, :] = jnp.zeros((8, 256), bf16)
            for n in range(2):
                trunk_ref[s, 96:104, 32 * n : 32 * n + 32] = dhead[8 * n : 8 * n + 8, 32 * s : 32 * s + 32]

    @pl.when(flags_ref[2] == 0)
    def _():
        write(keep_ref, give_ref)

    @pl.when(flags_ref[2] == 1)
    def _():
        write(give_ref, keep_ref)

    at = (iota((16, 128), 0) == iota((16, 128), 1)) & is_act
    line = jnp.sum(jnp.where(at, acc_stat[...], 0.0), axis=0, keepdims=True)
    stat_ref[...] = jnp.broadcast_to(line, (8, 128))


def member_grad(flags, recv, weights, scale, other):
    v = pltpu.VMEM
    half = ALL_ROWS // 2
    return pl.pallas_call(
        grad_kernel,
        out_shape=(
            jax.ShapeDtypeStruct((SHARDS, HALF, 256), bf16),
            jax.ShapeDtypeStruct((SHARDS, HALF, 256), bf16),
            jax.ShapeDtypeStruct((8, 128), f32),
        ),
        in_specs=[pl.BlockSpec(memory_space=pltpu.SMEM)] + [pl.BlockSpec(memory_space=v)] * 4,
        scratch_shapes=[
            v((half, 128), bf16), v((ROWS, 128), bf16), v((ROWS, CH), f32),
            v((PAD + ALL_ROWS, CH), bf16), v((PAD + ALL_ROWS, CH), bf16), v((PAD + ALL_ROWS, CH), bf16),
            v((ROWS, CH), bf16),
            v((ALL_ROWS, CH), bf16), v((ALL_ROWS, CH), bf16), v((ALL_ROWS, CH), bf16),
            v((ROWS, UNITS), bf16), v((ROWS, UNITS), bf16), v((16, ROWS), bf16),
            v((ROWS, UNITS), bf16), v((ROWS, UNITS), bf16),
            v((ALL_ROWS, CH), f32),
            v((ALL_ROWS + PAD, CH), bf16), v((ALL_ROWS + PAD, CH), bf16), v((ALL_ROWS + PAD, CH), bf16),
            v((half, 512), bf16),
            v((6, CH, CH), f32), v((CH, UNITS), f32), v((UNITS, UNITS), f32), v((16, UNITS), f32), v((16, 128), f32),
        ],
        cost_estimate=pl.CostEstimate(flops=11_200_000_000, bytes_accessed=4_000_000, transcendentals=4_000_000),
        compiler_params=pltpu.CompilerParams(vmem_limit_bytes=36 * 1024 * 1024),
        name="grad",
    )(flags, recv, weights, scale, other)


def reduce_kernel(flags_ref, recv_ref, stat_ref, mine_ref, theirs_ref, cast_ref):
    lane1 = iota((1, 128), 1)
    line = pltpu.roll(stat_ref[0:1, :], 32, 1)
    for whose, out_ref in ((flags_ref[2], mine_ref), (1 - flags_ref[2], theirs_ref)):
        for j in range(2):
            kind = 2 * whose + j
            total = recv_ref[kind].astype(f32)
            for z in range(1, 4):
                total = total + recv_ref[4 * z + kind].astype(f32)
            out_ref[j] = total
            line = line + jnp.where(lane1 == kind, jnp.sum(total * total), 0.0)
    for s in range(SHARDS):
        cast_ref[8 * s : 8 * s + 8, :] = jnp.broadcast_to(line, (8, 128))


def reduce_parts(flags, recv, stat):
    part = jax.ShapeDtypeStruct((2, HALF, 256), f32)
    return pl.pallas_call(
        reduce_kernel,
        out_shape=(part, part, jax.ShapeDtypeStruct((SHARDS * 8, 128), f32)),
        in_specs=[pl.BlockSpec(memory_space=pltpu.SMEM)] + [pl.BlockSpec(memory_space=pltpu.VMEM)] * 2,
        compiler_params=pltpu.CompilerParams(vmem_limit_bytes=16 * 1024 * 1024),
        name="reduce",
    )(flags, recv, stat)


def finish_kernel(flags_ref, mine_ref, theirs_ref, near_ref, far_ref, embed_ref, conv_ref, in_ref, mid_ref, head_ref, std_ref):
    core = flags_ref[2]
    lane1 = iota((1, 128), 1)
    total = jnp.sum(near_ref[...] + far_ref[...], axis=0, keepdims=True) * 0.125
    scales = []
    for j in range(2):
        kind = 2 * core + j
        std = jnp.zeros((1, 128), f32)
        for z in range(4):
            at = pl.ds(pl.multiple_of(8 * (4 * z + kind), 8), 8)
            std = std + near_ref[at, :][0:1] + far_ref[at, :][0:1]
        std = jnp.where((lane1 >= 32) & (lane1 < 32 + ACT), std, 0.0)
        square = jnp.sum(std * std + jnp.where(lane1 == kind, total, 0.0), axis=1, keepdims=True)
        scale = 1.0 / jnp.sqrt(square / ENTRIES + 1e-06)
        std_ref[j : j + 1, :] = (std * scale)[:, 32 : 32 + ACT]
        scales.append(scale)

    def write(encoder_ref, trunk_ref):
        for j, scale in enumerate(scales):
            for q in range(6):
                conv_ref[j, q // 2, q % 2] = encoder_ref[j, 16 * q : 16 * q + 16, :] * scale
            embed_ref[:, j, :] = encoder_ref[j, 96:99, :] * scale
            for n in range(2):
                cols = slice(256 * n, 256 * n + 256)
                in_ref[j, :, cols] = trunk_ref[j, 16 * n : 16 * n + 16, :] * scale
                mid_ref[j, :, cols] = trunk_ref[j, 32 + 32 * n : 64 + 32 * n, :] * scale
            head_ref[0:8, j, :] = trunk_ref[j, 96:104, 0:32] * scale
            head_ref[8:13, j, :] = trunk_ref[j, 96:101, 32:64] * scale

    @pl.when(core == 0)
    def _():
        write(mine_ref, theirs_ref)

    @pl.when(core == 1)
    def _():
        write(theirs_ref, mine_ref)


def finish(flags, mine, theirs, near, far):
    shapes = ((3, 2, 256), (2, 3, 2, 16, 256), (2, 16, 512), (2, 32, 512), (13, 2, 32), (2, 12))
    embed, conv, first, second, head, std = pl.pallas_call(
        finish_kernel,
        out_shape=tuple(jax.ShapeDtypeStruct(s, f32) for s in shapes),
        in_specs=[pl.BlockSpec(memory_space=pltpu.SMEM)] + [pl.BlockSpec(memory_space=pltpu.VMEM)] * 4,
        compiler_params=pltpu.CompilerParams(vmem_limit_bytes=16 * 1024 * 1024),
        name="finish",
    )(flags, mine, theirs, near, far)
    return embed.transpose(1, 0, 2), conv, first, second, head.transpose(1, 2, 0), std


def swap(value):
    return lax.ppermute(value, "core", [(0, 1), (1, 0)])


def local(observations, rollout, done_flags, member_ids, embed_weight, conv_weight, trunk_in, trunk_mid, head_weight, log_std):
    x, core = lax.axis_index("x"), lax.axis_index("core")
    own = core == x // 2
    flags = jnp.stack([x % 2, own.astype(jnp.int32), core]).astype(jnp.int32)
    packed = pack(observations, rollout, done_flags, member_ids)
    packed, flags = lax.optimization_barrier((packed, flags))
    recv = lax.all_to_all(packed, ("y", "x"), split_axis=0, concat_axis=0, tiled=True)
    weights = prepare(flags, embed_weight, conv_weight, trunk_in, trunk_mid, head_weight)
    weights = jnp.where(own, weights, swap(weights))
    keep, give, stat = member_grad(flags, recv, weights, log_std, swap(log_std))
    both = (keep.astype(f32) + swap(give).astype(f32)).astype(bf16)
    parts = lax.all_to_all(both, ("z", "x"), split_axis=0, concat_axis=0, tiled=True)
    mine, theirs, cast = reduce_parts(flags, parts, stat)
    near = lax.all_to_all(cast, ("z", "x"), split_axis=0, concat_axis=0, tiled=True)
    return finish(flags, mine, swap(theirs), near, swap(near))


def solution(mesh):
    fine = Mesh(mesh.devices.reshape(4, 2, 4, 4), ("y", "core", "z", "x"))
    member, dp = ("y", "core"), ("z", "x")
    every = member + dp
    return jax.shard_map(
        local,
        mesh=fine,
        in_specs=(P(every), P(every), P(every), P(every)) + (P(member),) * 6,
        out_specs=(
            P(member, dp),
            P(member, None, None, dp),
            P(member, dp),
            P(member, dp),
            P(member, dp),
            P(member),
        ),
        check_vma=False,
    )
```

```python
import jax
import jax.numpy as jnp
from jax import lax
from jax.experimental import pallas as pl
from jax.experimental.pallas import tpu as pltpu
from jax.sharding import Mesh, PartitionSpec as P


gamma_rate = 0.99
trace_rate = 0.95
half_log_tau = 0.9189385332046727

OBS = 48
STEPS = 24
ACT = 12
CH = 256
UNITS = 512
MEMBERS = 16
CAP = 6
SLOT = 8
REC = 64
WIDTH = STEPS * REC
ENTRIES = 805388
SOURCES = 16
SPANS = SOURCES * CAP
CHUNK_STEPS = 8
CHUNKS = STEPS // CHUNK_STEPS
ROWS = CHUNK_STEPS * SPANS
ALL_ROWS = STEPS * SPANS
PAD = 4 * SPANS
SHARDS = 16
HALF = 104
W_IN, W_MID, W_EMBED, W_HEAD, W_ROWS = 1536, 2048, 3072, 3328, 3360
f32 = jnp.float32
bf16 = jnp.bfloat16


def iota(shape, dim):
    return lax.broadcasted_iota(jnp.int32, shape, dim)


def dot(a, b):
    return jnp.dot(a, b, preferred_element_type=f32)


def dot_tn(a, b):
    return lax.dot_general(a, b, (((0,), (0,)), ((), ())), preferred_element_type=f32)


def dot_nt(a, b):
    return lax.dot_general(a, b, (((1,), (1,)), ((), ())), preferred_element_type=f32)


def onehot(cond):
    return jnp.where(cond, 1.0, 0.0).astype(bf16)


def pack_kernel(obs_ref, roll_ref, done_ref, ids_ref, out_ref):
    spans = obs_ref.shape[0]
    row, col = iota((STEPS * 16, 512), 0), iota((STEPS * 16, 512), 1)
    step = col & 127
    pick = onehot((row == 16 * step + 12 + (col >> 7)) & (step < STEPS))
    parts = dot(roll_ref[...], pick)
    reward, old_value = parts[:, 0:128], parts[:, 128:256]
    next_value, old_logp = parts[:, 256:384], parts[:, 384:512]
    widen = onehot(iota((STEPS, 128), 0) == iota((STEPS, 128), 1))
    done = dot_tn(done_ref[...].astype(f32).astype(bf16), widen)
    lane = iota((spans, 128), 1)
    alive = jnp.where(lane < STEPS, 1.0 - done, 0.0)
    advantage = reward + gamma_rate * alive * next_value - old_value
    carry = gamma_rate * trace_rate * alive
    for shift in (1, 2, 4, 8, 16):
        advantage = advantage + carry * pltpu.roll(advantage, 128 - shift, 1)
        carry = carry * pltpu.roll(carry, 128 - shift, 1)
    target = jnp.where(lane < STEPS, advantage + old_value, 0.0)
    advantage = jnp.where(lane < STEPS, advantage, 0.0)
    scalars = jnp.concatenate([target.astype(bf16), advantage.astype(bf16), old_logp.astype(bf16)], axis=1)

    col = iota((384, 512), 1)
    row = iota((384, 512), 0)
    spot, within = col & 63, col >> 6
    place_obs = onehot((row == 48 * within + spot) & (spot < 48))
    place_act = onehot((row == 16 * within + spot - 48) & (spot >= 48) & (spot < 60))[0:128]
    live = jnp.where((iota((spans, 512), 1) & 63) == 63, 1.0, 0.0)
    groups = []
    for g in range(3):
        place_scal = onehot((spot >= 60) & (spot < 63) & (row == (spot - 60) * 128 + 8 * g + within))
        placed = dot(obs_ref[:, 384 * g : 384 * g + 384], place_obs)
        placed = placed + dot(roll_ref[:, 128 * g : 128 * g + 128], place_act)
        placed = placed + dot(scalars, place_scal) + live
        groups.append(placed.astype(bf16))

    slots = MEMBERS * SLOT
    ids = ids_ref[...]
    slot, span = iota((slots, spans), 0), iota((slots, spans), 1)
    named = onehot(iota((MEMBERS, spans), 0) == ids)
    earlier = onehot(iota((spans, spans), 0) < iota((spans, spans), 1))
    rank = jnp.sum(dot(named, earlier) * named.astype(f32), axis=0, keepdims=True)
    dispatch = onehot(slot == ids * SLOT + rank.astype(jnp.int32))
    for g in range(3):
        out_ref[:, 512 * g : 512 * g + 512] = dot(dispatch, groups[g]).astype(bf16)


def pack(observations, rollout, done_flags, member_ids):
    return pl.pallas_call(
        pack_kernel,
        out_shape=jax.ShapeDtypeStruct((MEMBERS * SLOT, WIDTH), bf16),
        name="pack",
    )(observations, rollout, done_flags.T, member_ids.T)


def weights_kernel(
    which_ref, embed_hbm, conv_hbm, in_hbm, mid_hbm, head_hbm, out_ref,
    embed_ref, conv_ref, in_ref, mid_ref, head_ref, sems,
):
    which = which_ref[0]
    moves = [
        pltpu.make_async_copy(conv_hbm.at[which, layer], conv_ref.at[layer], sems.at[layer]) for layer in range(3)
    ]
    moves.append(pltpu.make_async_copy(mid_hbm.at[which], mid_ref, sems.at[3]))
    moves.append(pltpu.make_async_copy(in_hbm.at[which], in_ref, sems.at[4]))
    moves.append(pltpu.make_async_copy(embed_hbm.at[which], embed_ref, sems.at[5]))
    moves.append(pltpu.make_async_copy(head_hbm, head_ref, sems.at[6]))
    for move in moves:
        move.start()
    for layer in range(3):
        moves[layer].wait()
        for tap in range(2):
            at = CH * (2 * layer + tap)
            out_ref[at : at + CH, :] = conv_ref[layer, tap].astype(bf16)
    halves = (slice(0, 256), slice(256, 512))
    moves[3].wait()
    for n in range(2):
        out_ref[W_MID + UNITS * n : W_MID + UNITS * n + UNITS, :] = mid_ref[:, halves[n]].astype(bf16)
    moves[4].wait()
    for n in range(2):
        out_ref[W_IN + CH * n : W_IN + CH * n + CH, :] = in_ref[:, halves[n]].astype(bf16)
    moves[5].wait()
    embed = embed_ref[...].astype(bf16)
    r, k = iota((128, OBS), 0), iota((128, OBS), 1)
    for n in range(2):
        out_ref[W_EMBED + 128 * n : W_EMBED + 128 * n + 128, :] = dot(onehot(r == k + REC * n), embed).astype(bf16)
    moves[6].wait()
    head = jnp.where(which == 0, head_ref[:, 0, :], head_ref[:, 1, :]).astype(bf16)
    head = dot(onehot(iota((16, ACT + 1), 0) == iota((16, ACT + 1), 1)), head).astype(bf16)
    for n in range(2):
        out_ref[W_HEAD + 16 * n : W_HEAD + 16 * n + 16, :] = head[:, halves[n]]


def prepare(which, embed, conv, trunk_in, trunk_mid, head):
    head = head.transpose(2, 0, 1)
    v = pltpu.VMEM
    return pl.pallas_call(
        weights_kernel,
        in_specs=[pl.BlockSpec(memory_space=pltpu.SMEM)] + [pl.BlockSpec(memory_space=pltpu.HBM)] * 5,
        out_specs=pl.BlockSpec(memory_space=v),
        out_shape=jax.ShapeDtypeStruct((W_ROWS, CH), bf16),
        scratch_shapes=[v(x.shape[1:], f32) for x in (embed, conv, trunk_in, trunk_mid)]
        + [v(head.shape, f32), pltpu.SemaphoreType.DMA((7,))],
        cost_estimate=pl.CostEstimate(flops=0, bytes_accessed=5_000_000, transcendentals=0),
        compiler_params=pltpu.CompilerParams(vmem_limit_bytes=60 * 1024 * 1024),
        name="weights",
    )(which, embed, conv, trunk_in, trunk_mid, head)


def grad_kernel(
    which_ref, own_ref, core_ref, recv_ref, w_ref, scale_ref, other_ref,
    keep_ref, give_ref, stat_ref,
    xc, xt, hid, c0, c1, c2, c3, g0, g1, g2, first, second, dout, dp2, dp1, dhid, dm0, dm1, dm2, dpair,
    acc_conv, acc_in, acc_mid, acc_head, acc_stat,
):
    own = own_ref[0] == 1
    cs, gs, dms = (c0, c1, c2), (g0, g1, g2), (dm0, dm1, dm2)
    for ref in cs:
        ref[0:PAD, :] = jnp.zeros((PAD, CH), bf16)
    for ref in dms:
        ref[ALL_ROWS : ALL_ROWS + PAD, :] = jnp.zeros((PAD, CH), bf16)
    for ref in (acc_conv, acc_in, acc_mid, acc_head, acc_stat):
        ref[...] = jnp.zeros_like(ref)

    r, k = iota((SPANS, SOURCES * SLOT), 0), iota((SPANS, SOURCES * SLOT), 1)
    compact = onehot(((k & 7) < CAP) & (r == (k >> 3) * CAP + (k & 7)))
    r, k = iota((64, 128), 0), iota((64, 128), 1)
    entry = r & 31
    select = onehot((entry < 16) & (k == entry + OBS + (r >> 5) * REC))
    sub = iota((16, 1), 0)
    is_act = sub < ACT
    scale = jnp.where(own, scale_ref[...], other_ref[...])
    scale = jnp.where(which_ref[0] == 0, scale[0:1, :], scale[1:2, :])
    log_scale = jnp.sum(jnp.where(iota((16, ACT), 0) == iota((16, ACT), 1), scale, 0.0), axis=1, keepdims=True)
    conv = [w_ref.at[2 * CH * layer : 2 * CH * layer + 2 * CH] for layer in range(3)]
    in_half = [w_ref.at[W_IN + CH * n : W_IN + CH * n + CH] for n in range(2)]
    mid_half = [w_ref.at[W_MID + UNITS * n : W_MID + UNITS * n + UNITS] for n in range(2)]
    embed_half = [w_ref.at[W_EMBED + 128 * n : W_EMBED + 128 * n + 128] for n in range(2)]
    head_half = [w_ref.at[W_HEAD + 16 * n : W_HEAD + 16 * n + 16] for n in range(2)]

    def across(halves, rows):
        return jnp.concatenate([half[rows, :] for half in halves], axis=1)

    inverse = jnp.where(is_act, jnp.exp(-log_scale), 0.0)
    offset = jnp.sum(jnp.where(is_act, log_scale, 0.0), axis=0, keepdims=True) + ACT * half_log_tau
    lane = iota((1, ROWS), 1)
    odd = lane < 0
    for s in range(1, CHUNK_STEPS, 2):
        odd = odd | ((lane >= s * SPANS) & (lane < (s + 1) * SPANS))

    @pl.loop(0, CHUNKS)
    def _(i):
        base = i * ROWS
        pairs = CHUNK_STEPS // 2
        x = recv_ref[:, pl.ds(pl.multiple_of(i * (pairs * 128), 128), pairs * 128)]
        x = dot(compact, x).astype(bf16)
        half_rows = pl.ds(pl.multiple_of(i * (ROWS // 2), 16), ROWS // 2)
        for p in range(pairs):
            part = x[:, 128 * p : 128 * p + 128]
            xc[pl.ds(pl.multiple_of(i * (ROWS // 2) + p * SPANS, 16), SPANS), :] = part
            xt[2 * p * SPANS : (2 * p + 1) * SPANS, :] = part
            xt[(2 * p + 1) * SPANS : (2 * p + 2) * SPANS, :] = part
        y = [dot(xc[half_rows, :], half[...]) for half in embed_half]
        for p in range(pairs):
            for half in range(2):
                at = (2 * p + half) * SPANS
                h = y[half][p * SPANS : (p + 1) * SPANS, :]
                hid[at : at + SPANS, :] = h
                c0[pl.ds(pl.multiple_of(base + PAD + at, 16), SPANS), :] = h.astype(bf16)
        for layer in range(3):
            c, g = cs[layer], gs[layer]
            lag = SPANS * 2**layer
            both = jnp.concatenate(
                [c[pl.ds(pl.multiple_of(base + PAD, 16), ROWS), :], c[pl.ds(pl.multiple_of(base + PAD - lag, 16), ROWS), :]],
                axis=1,
            )
            mix = dot(both, conv[layer][...])
            grown = jnp.exp(mix)
            h = hid[...] + jnp.maximum(mix, jnp.minimum(grown - 1.0, 0.0))
            g[pl.ds(pl.multiple_of(base, 16), ROWS), :] = jnp.minimum(grown.astype(bf16), jnp.ones((), bf16))
            if layer < 2:
                hid[...] = h
                cs[layer + 1][pl.ds(pl.multiple_of(base + PAD, 16), ROWS), :] = h.astype(bf16)
            else:
                c3[...] = h.astype(bf16)

        def elu(x):
            below = jnp.minimum((jnp.exp(x) - 1.0).astype(bf16), jnp.zeros((), bf16))
            return jnp.maximum(x.astype(bf16), below)

        def slope(y):
            return jnp.minimum(y, jnp.zeros((), bf16)) + jnp.ones((), bf16)

        for n in range(0, UNITS, 256):
            first[:, n : n + 256] = elu(dot(c3[...], in_half[n // 256][...]))
        for n in range(0, UNITS, 256):
            second[:, n : n + 256] = elu(dot(first[...], mid_half[n // 256][...]))
        out = dot_nt(across(head_half, slice(0, 16)), second[...])
        record = dot_nt(select, xt[...])
        record = jnp.where(odd, record[32:64], record[0:32])
        diff = record[0:16] - out
        scaled = diff * inverse
        square = scaled * scaled
        advantage = record[13:14]
        old_logp = record[14:15]
        live = record[15:16]
        log_ratio = -0.5 * jnp.sum(square, axis=0, keepdims=True) - offset - old_logp
        ratio = jnp.exp(log_ratio)
        dlog = live * (0.5 * (ratio - 1.0) - ratio * advantage)
        dvalue = -0.5 * live * diff
        d = jnp.where(sub == ACT, dvalue, dlog * scaled * inverse)
        dout[...] = d.astype(bf16)
        acc_stat[...] += jnp.sum(dlog * (square - 1.0), axis=1, keepdims=True)
        acc_head[...] += dot(dout[...], second[...])
        for n in range(0, UNITS, 256):
            ds = dot_tn(dout[...], head_half[n // 256][...])
            dp2[:, n : n + 256] = ds.astype(bf16) * slope(second[:, n : n + 256])
        for n in range(0, UNITS, 256):
            df = dot_nt(dp2[...], across(mid_half, slice(n, n + 256)))
            dp1[:, n : n + 256] = df.astype(bf16) * slope(first[:, n : n + 256])
        dhid[pl.ds(pl.multiple_of(base, 16), ROWS), :] = dot_nt(dp1[...], across(in_half, slice(0, CH)))
        for n in range(0, UNITS, 256):
            acc_mid[n : n + 256, :] += dot_tn(first[:, n : n + 256], dp2[...])
        acc_in[...] += dot_tn(c3[...], dp1[...])

    @pl.loop(0, CHUNKS)
    def _(j):
        i = CHUNKS - 1 - j
        base = i * ROWS
        here = pl.ds(pl.multiple_of(base, 16), ROWS)
        for layer in (2, 1, 0):
            c, g, dm = cs[layer], gs[layer], dms[layer]
            lag = SPANS * 2**layer
            dh = dhid[here, :]
            dm[here, :] = dh.astype(bf16) * g[here, :]
            dc = dot_nt(dm[here, :], conv[layer][0:256, :])
            dc = dc + dot_nt(dm[pl.ds(pl.multiple_of(base + lag, 16), ROWS), :], conv[layer][256:512, :])
            dh = dh + dc
            if layer > 0:
                dhid[here, :] = dh
            else:
                for s in range(CHUNK_STEPS):
                    at = pl.ds(pl.multiple_of(i * (ROWS // 2) + (s // 2) * SPANS, 16), SPANS)
                    dpair[at, 256 * (s % 2) : 256 * (s % 2) + 256] = dh[s * SPANS : s * SPANS + SPANS].astype(bf16)
            acc_conv[2 * layer] += dot_tn(c[pl.ds(pl.multiple_of(base + PAD, 16), ROWS), :], dm[here, :])
            acc_conv[2 * layer + 1] += dot_tn(c[pl.ds(pl.multiple_of(base + PAD - lag, 16), ROWS), :], dm[here, :])

    dembed = dot_tn(xc[...], dpair[...])
    dembed = (dembed[0:OBS, 0:256] + dembed[REC : REC + OBS, 256:512]).astype(bf16)
    r, k = iota((SHARDS * 8, OBS), 0), iota((SHARDS * 8, OBS), 1)
    spread = onehot(((r & 7) < 3) & (k == (r >> 3) * 3 + (r & 7)))
    extra = dot(spread, dembed).astype(bf16)
    dhead = acc_head[...].astype(bf16)

    def write(encoder_ref, trunk_ref):
        for s in range(SHARDS):
            for q in range(6):
                encoder_ref[s, 16 * q : 16 * q + 16, :] = acc_conv[q, 16 * s : 16 * s + 16, :].astype(bf16)
            encoder_ref[s, 96:104, :] = extra[8 * s : 8 * s + 8, :]
            for n in range(2):
                cols = slice(256 * n, 256 * n + 256)
                trunk_ref[s, 16 * n : 16 * n + 16, :] = acc_in[16 * s : 16 * s + 16, cols].astype(bf16)
                trunk_ref[s, 32 + 32 * n : 64 + 32 * n, :] = acc_mid[32 * s : 32 * s + 32, cols].astype(bf16)
            trunk_ref[s, 96:104, :] = jnp.zeros((8, 256), bf16)
            for n in range(2):
                trunk_ref[s, 96:104, 32 * n : 32 * n + 32] = dhead[8 * n : 8 * n + 8, 32 * s : 32 * s + 32]

    @pl.when(core_ref[0] == 0)
    def _():
        write(keep_ref, give_ref)

    @pl.when(core_ref[0] == 1)
    def _():
        write(give_ref, keep_ref)

    at = (iota((16, 128), 0) == iota((16, 128), 1)) & is_act
    line = jnp.sum(jnp.where(at, acc_stat[...], 0.0), axis=0, keepdims=True)
    stat_ref[...] = jnp.broadcast_to(line, (8, 128))


def member_grad(which, own, core, recv, weights, scale, other):
    v = pltpu.VMEM
    half = ALL_ROWS // 2
    return pl.pallas_call(
        grad_kernel,
        out_shape=(
            jax.ShapeDtypeStruct((SHARDS, HALF, 256), bf16),
            jax.ShapeDtypeStruct((SHARDS, HALF, 256), bf16),
            jax.ShapeDtypeStruct((8, 128), f32),
        ),
        in_specs=[pl.BlockSpec(memory_space=pltpu.SMEM)] * 3 + [pl.BlockSpec(memory_space=v)] * 4,
        scratch_shapes=[
            v((half, 128), bf16), v((ROWS, 128), bf16), v((ROWS, CH), f32),
            v((PAD + ALL_ROWS, CH), bf16), v((PAD + ALL_ROWS, CH), bf16), v((PAD + ALL_ROWS, CH), bf16),
            v((ROWS, CH), bf16),
            v((ALL_ROWS, CH), bf16), v((ALL_ROWS, CH), bf16), v((ALL_ROWS, CH), bf16),
            v((ROWS, UNITS), bf16), v((ROWS, UNITS), bf16), v((16, ROWS), bf16),
            v((ROWS, UNITS), bf16), v((ROWS, UNITS), bf16),
            v((ALL_ROWS, CH), f32),
            v((ALL_ROWS + PAD, CH), bf16), v((ALL_ROWS + PAD, CH), bf16), v((ALL_ROWS + PAD, CH), bf16),
            v((half, 512), bf16),
            v((6, CH, CH), f32), v((CH, UNITS), f32), v((UNITS, UNITS), f32), v((16, UNITS), f32), v((16, 128), f32),
        ],
        cost_estimate=pl.CostEstimate(flops=11_200_000_000, bytes_accessed=4_000_000, transcendentals=4_000_000),
        compiler_params=pltpu.CompilerParams(vmem_limit_bytes=34 * 1024 * 1024),
        name="grad",
    )(which, own, core, recv, weights, scale, other)


def reduce_kernel(core_ref, recv_ref, stat_ref, mine_ref, theirs_ref, cast_ref):
    lane1 = iota((1, 128), 1)
    line = pltpu.roll(stat_ref[0:1, :], 32, 1)
    for whose, out_ref in ((core_ref[0], mine_ref), (1 - core_ref[0], theirs_ref)):
        for j in range(2):
            kind = 2 * whose + j
            total = recv_ref[kind].astype(f32)
            for z in range(1, 4):
                total = total + recv_ref[4 * z + kind].astype(f32)
            out_ref[j] = total
            line = line + jnp.where(lane1 == kind, jnp.sum(total * total), 0.0)
    for s in range(SHARDS):
        cast_ref[8 * s : 8 * s + 8, :] = jnp.broadcast_to(line, (8, 128))


def reduce_parts(core, recv, stat):
    part = jax.ShapeDtypeStruct((2, HALF, 256), f32)
    return pl.pallas_call(
        reduce_kernel,
        out_shape=(part, part, jax.ShapeDtypeStruct((SHARDS * 8, 128), f32)),
        in_specs=[pl.BlockSpec(memory_space=pltpu.SMEM)] + [pl.BlockSpec(memory_space=pltpu.VMEM)] * 2,
        compiler_params=pltpu.CompilerParams(vmem_limit_bytes=16 * 1024 * 1024),
        name="reduce",
    )(core, recv, stat)


def finish_kernel(core_ref, mine_ref, theirs_ref, near_ref, far_ref, embed_ref, conv_ref, in_ref, mid_ref, head_ref, std_ref):
    core = core_ref[0]
    lane1 = iota((1, 128), 1)
    total = jnp.sum(near_ref[...] + far_ref[...], axis=0, keepdims=True) * 0.125
    scales = []
    for j in range(2):
        kind = 2 * core + j
        std = jnp.zeros((1, 128), f32)
        for z in range(4):
            at = pl.ds(pl.multiple_of(8 * (4 * z + kind), 8), 8)
            std = std + near_ref[at, :][0:1] + far_ref[at, :][0:1]
        std = jnp.where((lane1 >= 32) & (lane1 < 32 + ACT), std, 0.0)
        square = jnp.sum(std * std + jnp.where(lane1 == kind, total, 0.0), axis=1, keepdims=True)
        scale = 1.0 / jnp.sqrt(square / ENTRIES + 1e-06)
        std_ref[j : j + 1, :] = (std * scale)[:, 32 : 32 + ACT]
        scales.append(scale)

    def write(encoder_ref, trunk_ref):
        for j, scale in enumerate(scales):
            for q in range(6):
                conv_ref[j, q // 2, q % 2] = encoder_ref[j, 16 * q : 16 * q + 16, :] * scale
            embed_ref[:, j, :] = encoder_ref[j, 96:99, :] * scale
            for n in range(2):
                cols = slice(256 * n, 256 * n + 256)
                in_ref[j, :, cols] = trunk_ref[j, 16 * n : 16 * n + 16, :] * scale
                mid_ref[j, :, cols] = trunk_ref[j, 32 + 32 * n : 64 + 32 * n, :] * scale
            head_ref[0:8, j, :] = trunk_ref[j, 96:104, 0:32] * scale
            head_ref[8:13, j, :] = trunk_ref[j, 96:101, 32:64] * scale

    @pl.when(core == 0)
    def _():
        write(mine_ref, theirs_ref)

    @pl.when(core == 1)
    def _():
        write(theirs_ref, mine_ref)


def finish(core, mine, theirs, near, far):
    shapes = ((3, 2, 256), (2, 3, 2, 16, 256), (2, 16, 512), (2, 32, 512), (13, 2, 32), (2, 12))
    embed, conv, first, second, head, std = pl.pallas_call(
        finish_kernel,
        out_shape=tuple(jax.ShapeDtypeStruct(s, f32) for s in shapes),
        in_specs=[pl.BlockSpec(memory_space=pltpu.SMEM)] + [pl.BlockSpec(memory_space=pltpu.VMEM)] * 4,
        compiler_params=pltpu.CompilerParams(vmem_limit_bytes=16 * 1024 * 1024),
        name="finish",
    )(core, mine, theirs, near, far)
    return embed.transpose(1, 0, 2), conv, first, second, head.transpose(1, 2, 0), std


def swap(value):
    return lax.ppermute(value, "core", [(0, 1), (1, 0)])


def local(observations, rollout, done_flags, member_ids, embed_weight, conv_weight, trunk_in, trunk_mid, head_weight, log_std):
    x, core = lax.axis_index("x"), lax.axis_index("core")
    which, own = (x % 2).reshape(1), (core == x // 2).astype(jnp.int32).reshape(1)
    core = core.reshape(1)
    packed = pack(observations, rollout, done_flags, member_ids)
    recv = lax.all_to_all(packed, ("y", "x"), split_axis=0, concat_axis=0, tiled=True)
    weights = prepare(which, embed_weight, conv_weight, trunk_in, trunk_mid, head_weight)
    weights = jnp.where(own[0] == 1, weights, swap(weights))
    keep, give, stat = member_grad(which, own, core, recv, weights, log_std, swap(log_std))
    both = (keep.astype(f32) + swap(give).astype(f32)).astype(bf16)
    parts = lax.all_to_all(both, ("z", "x"), split_axis=0, concat_axis=0, tiled=True)
    mine, theirs, cast = reduce_parts(core, parts, stat)
    near = lax.all_to_all(cast, ("z", "x"), split_axis=0, concat_axis=0, tiled=True)
    return finish(core, mine, swap(theirs), near, swap(near))


def solution(mesh):
    fine = Mesh(mesh.devices.reshape(4, 2, 4, 4), ("y", "core", "z", "x"))
    member, dp = ("y", "core"), ("z", "x")
    every = member + dp
    return jax.shard_map(
        local,
        mesh=fine,
        in_specs=(P(every), P(every), P(every), P(every)) + (P(member),) * 6,
        out_specs=(
            P(member, dp),
            P(member, None, None, dp),
            P(member, dp),
            P(member, dp),
            P(member, dp),
            P(member),
        ),
        check_vma=False,
    )
```

```python
import jax
import jax.numpy as jnp
from jax import lax
from jax.experimental import pallas as pl
from jax.experimental.pallas import tpu as pltpu
from jax.sharding import Mesh, PartitionSpec as P


gamma_rate = 0.99
trace_rate = 0.95
half_log_tau = 0.9189385332046727

OBS = 48
STEPS = 24
ACT = 12
CH = 256
UNITS = 512
MEMBERS = 16
CAP = 6
SLOT = 8
REC = 64
WIDTH = STEPS * REC
ENTRIES = 805388
SOURCES = 16
SPANS = SOURCES * CAP
CHUNK_STEPS = 8
CHUNKS = STEPS // CHUNK_STEPS
ROWS = CHUNK_STEPS * SPANS
ALL_ROWS = STEPS * SPANS
PAD = 4 * SPANS
SHARDS = 16
HALF = 104
CONV_ROWS = 1536
W_IN, W_MID, W_EMBED, W_HEAD, W_ROWS = 0, 512, 1536, 1792, 1824
f32 = jnp.float32
bf16 = jnp.bfloat16


def iota(shape, dim):
    return lax.broadcasted_iota(jnp.int32, shape, dim)


def dot(a, b):
    return jnp.dot(a, b, preferred_element_type=f32)


def dot_tn(a, b):
    return lax.dot_general(a, b, (((0,), (0,)), ((), ())), preferred_element_type=f32)


def dot_nt(a, b):
    return lax.dot_general(a, b, (((1,), (1,)), ((), ())), preferred_element_type=f32)


def onehot(cond):
    return jnp.where(cond, 1.0, 0.0).astype(bf16)


def pack_kernel(obs_ref, roll_ref, done_ref, ids_ref, out_ref):
    spans = obs_ref.shape[0]
    row, col = iota((STEPS * 16, 512), 0), iota((STEPS * 16, 512), 1)
    step = col & 127
    pick = onehot((row == 16 * step + 12 + (col >> 7)) & (step < STEPS))
    parts = dot(roll_ref[...], pick)
    reward, old_value = parts[:, 0:128], parts[:, 128:256]
    next_value, old_logp = parts[:, 256:384], parts[:, 384:512]
    widen = onehot(iota((STEPS, 128), 0) == iota((STEPS, 128), 1))
    done = dot_tn(done_ref[...].astype(f32).astype(bf16), widen)
    lane = iota((spans, 128), 1)
    alive = jnp.where(lane < STEPS, 1.0 - done, 0.0)
    advantage = reward + gamma_rate * alive * next_value - old_value
    carry = gamma_rate * trace_rate * alive
    for shift in (1, 2, 4, 8, 16):
        advantage = advantage + carry * pltpu.roll(advantage, 128 - shift, 1)
        carry = carry * pltpu.roll(carry, 128 - shift, 1)
    target = jnp.where(lane < STEPS, advantage + old_value, 0.0)
    advantage = jnp.where(lane < STEPS, advantage, 0.0)
    scalars = jnp.concatenate([target.astype(bf16), advantage.astype(bf16), old_logp.astype(bf16)], axis=1)

    col = iota((384, 512), 1)
    row = iota((384, 512), 0)
    spot, within = col & 63, col >> 6
    place_obs = onehot((row == 48 * within + spot) & (spot < 48))
    place_act = onehot((row == 16 * within + spot - 48) & (spot >= 48) & (spot < 60))[0:128]
    live = jnp.where((iota((spans, 512), 1) & 63) == 63, 1.0, 0.0)
    groups = []
    for g in range(3):
        place_scal = onehot((spot >= 60) & (spot < 63) & (row == (spot - 60) * 128 + 8 * g + within))
        placed = dot(obs_ref[:, 384 * g : 384 * g + 384], place_obs)
        placed = placed + dot(roll_ref[:, 128 * g : 128 * g + 128], place_act)
        placed = placed + dot(scalars, place_scal) + live
        groups.append(placed.astype(bf16))

    slots = MEMBERS * SLOT
    ids = ids_ref[...]
    slot, span = iota((slots, spans), 0), iota((slots, spans), 1)
    named = onehot(iota((MEMBERS, spans), 0) == ids)
    earlier = onehot(iota((spans, spans), 0) < iota((spans, spans), 1))
    rank = jnp.sum(dot(named, earlier) * named.astype(f32), axis=0, keepdims=True)
    dispatch = onehot(slot == ids * SLOT + rank.astype(jnp.int32))
    for g in range(3):
        out_ref[:, 512 * g : 512 * g + 512] = dot(dispatch, groups[g]).astype(bf16)


def pack(observations, rollout, done_flags, member_ids):
    return pl.pallas_call(
        pack_kernel,
        out_shape=jax.ShapeDtypeStruct((MEMBERS * SLOT, WIDTH), bf16),
        name="pack",
    )(observations, rollout, done_flags.T, member_ids.T)


def conv_weights_kernel(which_ref, conv_hbm, out_ref, conv_ref, sems):
    moves = [
        pltpu.make_async_copy(conv_hbm.at[which_ref[0], layer], conv_ref.at[layer], sems.at[layer]) for layer in range(3)
    ]
    for move in moves:
        move.start()
    for layer in range(3):
        moves[layer].wait()
        for tap in range(2):
            at = CH * (2 * layer + tap)
            out_ref[at : at + CH, :] = conv_ref[layer, tap].astype(bf16)


def trunk_weights_kernel(
    which_ref, embed_hbm, in_hbm, mid_hbm, head_hbm, out_ref,
    embed_ref, in_ref, mid_ref, head_ref, sems,
):
    which = which_ref[0]
    moves = [
        pltpu.make_async_copy(head_hbm, head_ref, sems.at[0]),
        pltpu.make_async_copy(embed_hbm.at[which], embed_ref, sems.at[1]),
        pltpu.make_async_copy(in_hbm.at[which], in_ref, sems.at[2]),
        pltpu.make_async_copy(mid_hbm.at[which], mid_ref, sems.at[3]),
    ]
    for move in moves:
        move.start()
    halves = (slice(0, 256), slice(256, 512))
    moves[0].wait()
    head = jnp.where(which == 0, head_ref[:, 0, :], head_ref[:, 1, :]).astype(bf16)
    head = dot(onehot(iota((16, ACT + 1), 0) == iota((16, ACT + 1), 1)), head).astype(bf16)
    for n in range(2):
        out_ref[W_HEAD + 16 * n : W_HEAD + 16 * n + 16, :] = head[:, halves[n]]
    moves[1].wait()
    embed = embed_ref[...].astype(bf16)
    r, k = iota((128, OBS), 0), iota((128, OBS), 1)
    for n in range(2):
        out_ref[W_EMBED + 128 * n : W_EMBED + 128 * n + 128, :] = dot(onehot(r == k + REC * n), embed).astype(bf16)
    moves[2].wait()
    for n in range(2):
        out_ref[W_IN + CH * n : W_IN + CH * n + CH, :] = in_ref[:, halves[n]].astype(bf16)
    moves[3].wait()
    for n in range(2):
        out_ref[W_MID + UNITS * n : W_MID + UNITS * n + UNITS, :] = mid_ref[:, halves[n]].astype(bf16)


def prepare(kernel, rows, which, arrays, shapes):
    v = pltpu.VMEM
    return pl.pallas_call(
        kernel,
        in_specs=[pl.BlockSpec(memory_space=pltpu.SMEM)] + [pl.BlockSpec(memory_space=pltpu.HBM)] * len(arrays),
        out_specs=pl.BlockSpec(memory_space=v),
        out_shape=jax.ShapeDtypeStruct((rows, CH), bf16),
        scratch_shapes=[v(shape, f32) for shape in shapes] + [pltpu.SemaphoreType.DMA((4,))],
        cost_estimate=pl.CostEstimate(flops=0, bytes_accessed=2_500_000, transcendentals=0),
        compiler_params=pltpu.CompilerParams(vmem_limit_bytes=60 * 1024 * 1024),
    )(which, *arrays)


def grad_kernel(
    which_ref, own_ref, core_ref, recv_ref, conv_ref, w_ref, scale_ref, other_ref,
    keep_ref, give_ref, stat_ref,
    xc, xt, hid, c0, c1, c2, c3, g0, g1, g2, first, second, dout, dp2, dp1, dhid, dm0, dm1, dm2, dpair,
    acc_conv, acc_in, acc_mid, acc_head, acc_stat,
):
    own = own_ref[0] == 1
    cs, gs, dms = (c0, c1, c2), (g0, g1, g2), (dm0, dm1, dm2)
    for ref in cs:
        ref[0:PAD, :] = jnp.zeros((PAD, CH), bf16)
    for ref in dms:
        ref[ALL_ROWS : ALL_ROWS + PAD, :] = jnp.zeros((PAD, CH), bf16)

    r, k = iota((SPANS, SOURCES * SLOT), 0), iota((SPANS, SOURCES * SLOT), 1)
    compact = onehot(((k & 7) < CAP) & (r == (k >> 3) * CAP + (k & 7)))
    r, k = iota((64, 128), 0), iota((64, 128), 1)
    entry = r & 31
    select = onehot((entry < 16) & (k == entry + OBS + (r >> 5) * REC))
    sub = iota((16, 1), 0)
    is_act = sub < ACT
    scale = jnp.where(own, scale_ref[...], other_ref[...])
    scale = jnp.where(which_ref[0] == 0, scale[0:1, :], scale[1:2, :])
    log_scale = jnp.sum(jnp.where(iota((16, ACT), 0) == iota((16, ACT), 1), scale, 0.0), axis=1, keepdims=True)
    conv = [conv_ref.at[2 * CH * layer : 2 * CH * layer + 2 * CH] for layer in range(3)]
    in_half = [w_ref.at[W_IN + CH * n : W_IN + CH * n + CH] for n in range(2)]
    mid_half = [w_ref.at[W_MID + UNITS * n : W_MID + UNITS * n + UNITS] for n in range(2)]
    embed_half = [w_ref.at[W_EMBED + 128 * n : W_EMBED + 128 * n + 128] for n in range(2)]
    head_half = [w_ref.at[W_HEAD + 16 * n : W_HEAD + 16 * n + 16] for n in range(2)]

    def across(halves, rows):
        return jnp.concatenate([half[rows, :] for half in halves], axis=1)

    inverse = jnp.where(is_act, jnp.exp(-log_scale), 0.0)
    offset = jnp.sum(jnp.where(is_act, log_scale, 0.0), axis=0, keepdims=True) + ACT * half_log_tau
    lane = iota((1, ROWS), 1)
    odd = lane < 0
    for s in range(1, CHUNK_STEPS, 2):
        odd = odd | ((lane >= s * SPANS) & (lane < (s + 1) * SPANS))

    pairs = CHUNK_STEPS // 2
    blocks = (0, 256)

    def rows(i, shift=0):
        return slice(i * ROWS + shift, (i + 1) * ROWS + shift)

    def add(ref, at, value, start):
        if start:
            ref[at] = value
        else:
            ref[at] += value

    def elu(x):
        below = jnp.minimum((jnp.exp(x) - 1.0).astype(bf16), jnp.zeros((), bf16))
        return jnp.maximum(x.astype(bf16), below)

    def slope(y):
        return jnp.minimum(y, jnp.zeros((), bf16)) + jnp.ones((), bf16)

    def forward(i):
        def enter():
            x = dot(compact, recv_ref[:, i * pairs * 128 : (i + 1) * pairs * 128]).astype(bf16)
            for p in range(pairs):
                part = x[:, 128 * p : 128 * p + 128]
                at = i * (ROWS // 2) + p * SPANS
                xc[at : at + SPANS, :] = part
                for half in range(2):
                    at = i * ROWS + (2 * p + half) * SPANS
                    xt[at : at + SPANS, :] = part
            y = [dot(xc[i * (ROWS // 2) : (i + 1) * (ROWS // 2), :], half[...]) for half in embed_half]
            for p in range(pairs):
                for half in range(2):
                    at = i * ROWS + (2 * p + half) * SPANS
                    h = y[half][p * SPANS : (p + 1) * SPANS, :]
                    hid[at - i * ROWS : at - i * ROWS + SPANS, :] = h
                    c0[PAD + at : PAD + at + SPANS, :] = h.astype(bf16)

        def encode(layer):
            c, lag = cs[layer], SPANS * 2**layer
            both = jnp.concatenate([c[rows(i, PAD), :], c[rows(i, PAD - lag), :]], axis=1)
            mix = dot(both, conv[layer][...])
            grown = jnp.exp(mix)
            h = hid[...] + jnp.maximum(mix, jnp.minimum(grown - 1.0, 0.0))
            gs[layer][rows(i), :] = grown.astype(bf16)
            if layer < 2:
                hid[...] = h
                cs[layer + 1][rows(i, PAD), :] = h.astype(bf16)
            else:
                c3[rows(i), :] = h.astype(bf16)

        def widen(n):
            first[rows(i), n : n + 256] = elu(dot(c3[rows(i), :], in_half[n // 256][...]))

        def deepen(n):
            second[rows(i), n : n + 256] = elu(dot(first[rows(i), :], mid_half[n // 256][...]))

        yield enter
        for layer in range(3):
            yield lambda layer=layer: encode(layer)
        for n in blocks:
            yield lambda n=n: widen(n)
        for n in blocks:
            yield lambda n=n: deepen(n)

    def backward(i):
        def loss():
            out = dot_nt(across(head_half, slice(0, 16)), second[rows(i), :])
            record = dot_nt(select, xt[rows(i), :])
            record = jnp.where(odd, record[32:64], record[0:32])
            diff = record[0:16] - out
            scaled = diff * inverse
            square = scaled * scaled
            advantage, old_logp, live = record[13:14], record[14:15], record[15:16]
            log_ratio = -0.5 * jnp.sum(square, axis=0, keepdims=True) - offset - old_logp
            ratio = jnp.exp(log_ratio)
            dlog = live * (0.5 * (ratio - 1.0) - ratio * advantage)
            dvalue = -0.5 * live * diff
            d = jnp.where(sub == ACT, dvalue, dlog * scaled * inverse)
            dout[...] = d.astype(bf16)
            total = jnp.sum(dlog * (square - 1.0), axis=1, keepdims=True)
            add(acc_stat, Ellipsis, jnp.broadcast_to(total, acc_stat.shape), i == 0)

        def down(n):
            ds = dot_tn(dout[...], head_half[n // 256][...])
            dp2[:, n : n + 256] = ds.astype(bf16) * slope(second[rows(i), n : n + 256])

        def head():
            add(acc_head, Ellipsis, dot(dout[...], second[rows(i), :]), i == 0)

        def middle(n):
            df = dot_nt(dp2[...], across(mid_half, slice(n, n + 256)))
            dp1[:, n : n + 256] = df.astype(bf16) * slope(first[rows(i), n : n + 256])

        def top():
            dhid[rows(i), :] = dot_nt(dp1[...], across(in_half, slice(0, CH)))

        def grad_mid():
            add(acc_mid, Ellipsis, dot_tn(first[rows(i), :], dp2[...]), i == 0)

        def grad_in():
            add(acc_in, Ellipsis, dot_tn(c3[rows(i), :], dp1[...]), i == 0)

        yield loss
        for n in blocks:
            yield lambda n=n: down(n)
        yield head
        for n in blocks:
            yield lambda n=n: middle(n)
        yield top
        yield grad_mid
        yield grad_in

    def decode(i):
        start = i == CHUNKS - 1
        for layer in (2, 1, 0):
            c, dm, lag = cs[layer], dms[layer], SPANS * 2**layer
            dh = dhid[rows(i), :]
            dm[rows(i), :] = dh.astype(bf16) * jnp.minimum(gs[layer][rows(i), :], jnp.ones((), bf16))
            dc = dot_nt(dm[rows(i), :], conv[layer][0:256, :])
            dc = dc + dot_nt(dm[rows(i, lag), :], conv[layer][256:512, :])
            dh = dh + dc
            if layer > 0:
                dhid[rows(i), :] = dh
            else:
                for s in range(CHUNK_STEPS):
                    at = i * (ROWS // 2) + (s // 2) * SPANS
                    part = dh[s * SPANS : s * SPANS + SPANS].astype(bf16)
                    dpair[at : at + SPANS, 256 * (s % 2) : 256 * (s % 2) + 256] = part
            both = jnp.concatenate([c[rows(i, PAD), :], c[rows(i, PAD - lag), :]], axis=1)
            add(acc_conv, layer, dot_tn(both, dm[rows(i), :]), start)

    def weave(left, right):
        left, right = list(left), list(right)
        order = [((k + 0.5) / len(left), 0, f) for k, f in enumerate(left)]
        order += [((k + 0.5) / len(right), 1, f) for k, f in enumerate(right)]
        for _, _, run in sorted(order, key=lambda item: item[:2]):
            run()

    weave(forward(0), [])
    for i in range(1, CHUNKS):
        weave(forward(i), backward(i - 1))
    weave(backward(CHUNKS - 1), [])
    for i in range(CHUNKS - 1, -1, -1):
        decode(i)

    dembed = dot_tn(xc[...], dpair[...])
    dembed = (dembed[0:OBS, 0:256] + dembed[REC : REC + OBS, 256:512]).astype(bf16)
    r, k = iota((SHARDS * 8, OBS), 0), iota((SHARDS * 8, OBS), 1)
    spread = onehot(((r & 7) < 3) & (k == (r >> 3) * 3 + (r & 7)))
    extra = dot(spread, dembed).astype(bf16)
    dhead = acc_head[...].astype(bf16)

    def write(encoder_ref, trunk_ref):
        for s in range(SHARDS):
            for q in range(6):
                encoder_ref[s, 16 * q : 16 * q + 16, :] = acc_conv[q // 2, 256 * (q % 2) + 16 * s : 256 * (q % 2) + 16 * s + 16, :].astype(bf16)
            encoder_ref[s, 96:104, :] = extra[8 * s : 8 * s + 8, :]
            for n in range(2):
                cols = slice(256 * n, 256 * n + 256)
                trunk_ref[s, 16 * n : 16 * n + 16, :] = acc_in[16 * s : 16 * s + 16, cols].astype(bf16)
                trunk_ref[s, 32 + 32 * n : 64 + 32 * n, :] = acc_mid[32 * s : 32 * s + 32, cols].astype(bf16)
            trunk_ref[s, 96:104, :] = jnp.zeros((8, 256), bf16)
            for n in range(2):
                trunk_ref[s, 96:104, 32 * n : 32 * n + 32] = dhead[8 * n : 8 * n + 8, 32 * s : 32 * s + 32]

    @pl.when(core_ref[0] == 0)
    def _():
        write(keep_ref, give_ref)

    @pl.when(core_ref[0] == 1)
    def _():
        write(give_ref, keep_ref)

    at = (iota((16, 128), 0) == iota((16, 128), 1)) & is_act
    line = jnp.sum(jnp.where(at, acc_stat[...], 0.0), axis=0, keepdims=True)
    stat_ref[...] = jnp.broadcast_to(line, (8, 128))


def member_grad(which, own, core, recv, conv, trunk, scale, other):
    v = pltpu.VMEM
    half = ALL_ROWS // 2
    return pl.pallas_call(
        grad_kernel,
        out_shape=(
            jax.ShapeDtypeStruct((SHARDS, HALF, 256), bf16),
            jax.ShapeDtypeStruct((SHARDS, HALF, 256), bf16),
            jax.ShapeDtypeStruct((8, 128), f32),
        ),
        in_specs=[pl.BlockSpec(memory_space=pltpu.SMEM)] * 3 + [pl.BlockSpec(memory_space=v)] * 5,
        scratch_shapes=[
            v((half, 128), bf16), v((ALL_ROWS, 128), bf16), v((ROWS, CH), f32),
            v((PAD + ALL_ROWS, CH), bf16), v((PAD + ALL_ROWS, CH), bf16), v((PAD + ALL_ROWS, CH), bf16),
            v((ALL_ROWS, CH), bf16),
            v((ALL_ROWS, CH), bf16), v((ALL_ROWS, CH), bf16), v((ALL_ROWS, CH), bf16),
            v((ALL_ROWS, UNITS), bf16), v((ALL_ROWS, UNITS), bf16), v((16, ROWS), bf16),
            v((ROWS, UNITS), bf16), v((ROWS, UNITS), bf16),
            v((ALL_ROWS, CH), f32),
            v((ALL_ROWS + PAD, CH), bf16), v((ALL_ROWS + PAD, CH), bf16), v((ALL_ROWS + PAD, CH), bf16),
            v((half, 512), bf16),
            v((3, 2 * CH, CH), f32), v((CH, UNITS), f32), v((UNITS, UNITS), f32), v((16, UNITS), f32), v((16, 128), f32),
        ],
        cost_estimate=pl.CostEstimate(flops=11_200_000_000, bytes_accessed=4_000_000, transcendentals=4_000_000),
        compiler_params=pltpu.CompilerParams(vmem_limit_bytes=42 * 1024 * 1024),
        name="grad",
    )(which, own, core, recv, conv, trunk, scale, other)


def reduce_kernel(core_ref, recv_ref, stat_ref, mine_ref, theirs_ref, cast_ref):
    lane1 = iota((1, 128), 1)
    line = pltpu.roll(stat_ref[0:1, :], 32, 1)
    for whose, out_ref in ((core_ref[0], mine_ref), (1 - core_ref[0], theirs_ref)):
        for j in range(2):
            kind = 2 * whose + j
            total = recv_ref[kind].astype(f32)
            for z in range(1, 4):
                total = total + recv_ref[4 * z + kind].astype(f32)
            out_ref[j] = total
            line = line + jnp.where(lane1 == kind, jnp.sum(total * total), 0.0)
    for s in range(SHARDS):
        cast_ref[8 * s : 8 * s + 8, :] = jnp.broadcast_to(line, (8, 128))


def reduce_parts(core, recv, stat):
    part = jax.ShapeDtypeStruct((2, HALF, 256), f32)
    return pl.pallas_call(
        reduce_kernel,
        out_shape=(part, part, jax.ShapeDtypeStruct((SHARDS * 8, 128), f32)),
        in_specs=[pl.BlockSpec(memory_space=pltpu.SMEM)] + [pl.BlockSpec(memory_space=pltpu.VMEM)] * 2,
        compiler_params=pltpu.CompilerParams(vmem_limit_bytes=16 * 1024 * 1024),
        name="reduce",
    )(core, recv, stat)


def finish_kernel(core_ref, mine_ref, theirs_ref, near_ref, far_ref, embed_ref, conv_ref, in_ref, mid_ref, head_ref, std_ref):
    core = core_ref[0]
    lane1 = iota((1, 128), 1)
    total = jnp.sum(near_ref[...] + far_ref[...], axis=0, keepdims=True) * 0.125
    scales = []
    for j in range(2):
        kind = 2 * core + j
        std = jnp.zeros((1, 128), f32)
        for z in range(4):
            at = pl.ds(pl.multiple_of(8 * (4 * z + kind), 8), 8)
            std = std + near_ref[at, :][0:1] + far_ref[at, :][0:1]
        std = jnp.where((lane1 >= 32) & (lane1 < 32 + ACT), std, 0.0)
        square = jnp.sum(std * std + jnp.where(lane1 == kind, total, 0.0), axis=1, keepdims=True)
        scale = 1.0 / jnp.sqrt(square / ENTRIES + 1e-06)
        std_ref[j : j + 1, :] = (std * scale)[:, 32 : 32 + ACT]
        scales.append(scale)

    def write(encoder_ref, trunk_ref):
        for j, scale in enumerate(scales):
            for q in range(6):
                conv_ref[j, q // 2, q % 2] = encoder_ref[j, 16 * q : 16 * q + 16, :] * scale
            embed_ref[:, j, :] = encoder_ref[j, 96:99, :] * scale
            for n in range(2):
                cols = slice(256 * n, 256 * n + 256)
                in_ref[j, :, cols] = trunk_ref[j, 16 * n : 16 * n + 16, :] * scale
                mid_ref[j, :, cols] = trunk_ref[j, 32 + 32 * n : 64 + 32 * n, :] * scale
            head_ref[0:8, j, :] = trunk_ref[j, 96:104, 0:32] * scale
            head_ref[8:13, j, :] = trunk_ref[j, 96:101, 32:64] * scale

    @pl.when(core == 0)
    def _():
        write(mine_ref, theirs_ref)

    @pl.when(core == 1)
    def _():
        write(theirs_ref, mine_ref)


def finish(core, mine, theirs, near, far):
    shapes = ((3, 2, 256), (2, 3, 2, 16, 256), (2, 16, 512), (2, 32, 512), (13, 2, 32), (2, 12))
    embed, conv, first, second, head, std = pl.pallas_call(
        finish_kernel,
        out_shape=tuple(jax.ShapeDtypeStruct(s, f32) for s in shapes),
        in_specs=[pl.BlockSpec(memory_space=pltpu.SMEM)] + [pl.BlockSpec(memory_space=pltpu.VMEM)] * 4,
        compiler_params=pltpu.CompilerParams(vmem_limit_bytes=16 * 1024 * 1024),
        name="finish",
    )(core, mine, theirs, near, far)
    return embed.transpose(1, 0, 2), conv, first, second, head.transpose(1, 2, 0), std


def swap(value):
    return lax.ppermute(value, "core", [(0, 1), (1, 0)])


def local(observations, rollout, done_flags, member_ids, embed_weight, conv_weight, trunk_in, trunk_mid, head_weight, log_std):
    x, core = lax.axis_index("x"), lax.axis_index("core")
    which, own = (x % 2).reshape(1), (core == x // 2).astype(jnp.int32).reshape(1)
    core = core.reshape(1)
    packed = pack(observations, rollout, done_flags, member_ids)
    recv = lax.all_to_all(packed, ("y", "x"), split_axis=0, concat_axis=0, tiled=True)
    conv = prepare(conv_weights_kernel, CONV_ROWS, which, (conv_weight,), (conv_weight.shape[1:],))
    conv_far = swap(conv)
    head = head_weight.transpose(2, 0, 1)
    arrays = (embed_weight, trunk_in, trunk_mid, head)
    shapes = tuple(x.shape[1:] for x in arrays[:3]) + (head.shape,)
    trunk = prepare(trunk_weights_kernel, W_ROWS, which, arrays, shapes)
    mine = own[0] == 1
    conv = jnp.where(mine, conv, conv_far)
    trunk = jnp.where(mine, trunk, swap(trunk))
    keep, give, stat = member_grad(which, own, core, recv, conv, trunk, log_std, swap(log_std))
    both = (keep.astype(f32) + swap(give).astype(f32)).astype(bf16)
    parts = lax.all_to_all(both, ("z", "x"), split_axis=0, concat_axis=0, tiled=True)
    mine, theirs, cast = reduce_parts(core, parts, stat)
    near = lax.all_to_all(cast, ("z", "x"), split_axis=0, concat_axis=0, tiled=True)
    return finish(core, mine, swap(theirs), near, swap(near))


def solution(mesh):
    fine = Mesh(mesh.devices.reshape(4, 2, 4, 4), ("y", "core", "z", "x"))
    member, dp = ("y", "core"), ("z", "x")
    every = member + dp
    return jax.shard_map(
        local,
        mesh=fine,
        in_specs=(P(every), P(every), P(every), P(every)) + (P(member),) * 6,
        out_specs=(
            P(member, dp),
            P(member, None, None, dp),
            P(member, dp),
            P(member, dp),
            P(member, dp),
            P(member),
        ),
        check_vma=False,
    )
```

```python
import jax
import jax.numpy as jnp
from jax import lax
from jax.experimental import pallas as pl
from jax.experimental.pallas import tpu as pltpu
from jax.sharding import Mesh, PartitionSpec as P


gamma_rate = 0.99
trace_rate = 0.95
half_log_tau = 0.9189385332046727

OBS = 48
STEPS = 24
ACT = 12
CH = 256
UNITS = 512
MEMBERS = 16
CAP = 6
SLOT = 8
REC = 64
WIDTH = STEPS * REC
ENTRIES = 805388
SOURCES = 16
SPANS = SOURCES * CAP
CHUNK_STEPS = 8
CHUNKS = STEPS // CHUNK_STEPS
ROWS = CHUNK_STEPS * SPANS
ALL_ROWS = STEPS * SPANS
PAD = 4 * SPANS
SHARDS = 16
HALF = 104
BIG_ROWS, SMALL_ROWS = 2560, 800
W_MID = 1536
W_IN, W_EMBED, W_HEAD = 0, 512, 768
f32 = jnp.float32
bf16 = jnp.bfloat16


def iota(shape, dim):
    return lax.broadcasted_iota(jnp.int32, shape, dim)


def dot(a, b):
    return jnp.dot(a, b, preferred_element_type=f32)


def dot_tn(a, b):
    return lax.dot_general(a, b, (((0,), (0,)), ((), ())), preferred_element_type=f32)


def dot_nt(a, b):
    return lax.dot_general(a, b, (((1,), (1,)), ((), ())), preferred_element_type=f32)


def onehot(cond):
    return jnp.where(cond, 1.0, 0.0).astype(bf16)


def pack_kernel(obs_hbm, roll_hbm, done_hbm, ids_hbm, out_ref, obs_ref, roll_ref, done_ref, ids_ref, pick_ref, obs_at, act_at, scal_at, sems):
    moves = [
        pltpu.make_async_copy(source, target, sems.at[k])
        for k, (source, target) in enumerate(
            ((roll_hbm, roll_ref), (done_hbm, done_ref), (obs_hbm, obs_ref), (ids_hbm, ids_ref))
        )
    ]
    for move in moves:
        move.start()
    spans = obs_ref.shape[0]
    col = iota((1, 512), 1)
    spot, within, step = col & 63, col >> 6, col & 127
    row = iota((384, 512), 0)
    obs_at[...] = onehot(row == jnp.where(spot < 48, 48 * within + spot, -1))
    act_at[...] = onehot(row[0:128] == jnp.where((spot >= 48) & (spot < 60), 16 * within + spot - 48, -1))
    scal_at[...] = onehot(row == jnp.where((spot >= 60) & (spot < 63), (spot - 60) * 128 + within, -1))
    pick_ref[...] = onehot(row == jnp.where(step < STEPS, 16 * step + 12 + (col >> 7), -1))
    for move in moves:
        move.wait()
    parts = dot(roll_ref[...], pick_ref[...])
    reward, old_value = parts[:, 0:128], parts[:, 128:256]
    next_value, old_logp = parts[:, 256:384], parts[:, 384:512]
    widen = onehot(iota((STEPS, 128), 0) == iota((STEPS, 128), 1))
    done = dot_tn(done_ref[...].astype(f32).astype(bf16), widen)
    lane = iota((spans, 128), 1)
    alive = jnp.where(lane < STEPS, 1.0 - done, 0.0)
    advantage = reward + gamma_rate * alive * next_value - old_value
    carry = gamma_rate * trace_rate * alive
    for shift in (1, 2, 4, 8, 16):
        advantage = advantage + carry * pltpu.roll(advantage, 128 - shift, 1)
        carry = carry * pltpu.roll(carry, 128 - shift, 1)
    target = jnp.where(lane < STEPS, advantage + old_value, 0.0)
    advantage = jnp.where(lane < STEPS, advantage, 0.0)
    scalars = [target, advantage, old_logp]

    live = jnp.where((iota((spans, 512), 1) & 63) == 63, 1.0, 0.0)
    groups = []
    for g in range(3):
        placed = dot(obs_ref[:, 384 * g : 384 * g + 384], obs_at[...])
        placed = placed + dot(roll_ref[:, 128 * g : 128 * g + 128], act_at[...])
        turned = [pltpu.roll(x, (128 - 8 * g) % 128, 1) if g else x for x in scalars]
        turned = jnp.concatenate([x.astype(bf16) for x in turned], axis=1)
        placed = placed + dot(turned, scal_at[...]) + live
        groups.append(placed.astype(bf16))

    slots = MEMBERS * SLOT
    ids = ids_ref[...]
    slot, span = iota((slots, spans), 0), iota((slots, spans), 1)
    named = onehot(iota((MEMBERS, spans), 0) == ids)
    earlier = onehot(iota((spans, spans), 0) < iota((spans, spans), 1))
    rank = jnp.sum(dot(named, earlier) * named.astype(f32), axis=0, keepdims=True)
    dispatch = onehot(slot == ids * SLOT + rank.astype(jnp.int32))
    for g in range(3):
        out_ref[:, 512 * g : 512 * g + 512] = dot(dispatch, groups[g]).astype(bf16)


def pack(observations, rollout, done_flags, member_ids):
    arrays = (observations, rollout, done_flags.T, member_ids.T)
    return pl.pallas_call(
        pack_kernel,
        out_shape=jax.ShapeDtypeStruct((MEMBERS * SLOT, WIDTH), bf16),
        in_specs=[pl.BlockSpec(memory_space=pltpu.HBM)] * 4,
        out_specs=pl.BlockSpec(memory_space=pltpu.VMEM),
        scratch_shapes=[pltpu.VMEM(x.shape, x.dtype) for x in arrays]
        + [pltpu.VMEM((384, 512), bf16), pltpu.VMEM((384, 512), bf16), pltpu.VMEM((128, 512), bf16)]
        + [pltpu.VMEM((384, 512), bf16), pltpu.SemaphoreType.DMA((4,))],
        compiler_params=pltpu.CompilerParams(vmem_limit_bytes=60 * 1024 * 1024),
        name="pack",
    )(*arrays)


def big_weights_kernel(which_ref, conv_hbm, mid_hbm, out_ref, conv_ref, mid_ref, sems):
    which = which_ref[0]
    moves = [pltpu.make_async_copy(conv_hbm.at[which, layer], conv_ref.at[layer], sems.at[layer]) for layer in range(3)]
    moves.append(pltpu.make_async_copy(mid_hbm.at[which], mid_ref, sems.at[3]))
    for move in moves:
        move.start()
    for layer in range(3):
        moves[layer].wait()
        for tap in range(2):
            at = CH * (2 * layer + tap)
            out_ref[at : at + CH, :] = conv_ref[layer, tap].astype(bf16)
    moves[3].wait()
    for n in range(2):
        out_ref[W_MID + UNITS * n : W_MID + UNITS * n + UNITS, :] = mid_ref[:, 256 * n : 256 * n + 256].astype(bf16)


def small_weights_kernel(which_ref, embed_hbm, in_hbm, head_hbm, out_ref, embed_ref, in_ref, head_ref, sems):
    which = which_ref[0]
    moves = [
        pltpu.make_async_copy(head_hbm, head_ref, sems.at[0]),
        pltpu.make_async_copy(embed_hbm.at[which], embed_ref, sems.at[1]),
        pltpu.make_async_copy(in_hbm.at[which], in_ref, sems.at[2]),
    ]
    for move in moves:
        move.start()
    halves = (slice(0, 256), slice(256, 512))
    moves[0].wait()
    head = jnp.where(which == 0, head_ref[:, 0, :], head_ref[:, 1, :]).astype(bf16)
    head = dot(onehot(iota((16, ACT + 1), 0) == iota((16, ACT + 1), 1)), head).astype(bf16)
    for n in range(2):
        out_ref[W_HEAD + 16 * n : W_HEAD + 16 * n + 16, :] = head[:, halves[n]]
    moves[1].wait()
    embed = embed_ref[...].astype(bf16)
    r, k = iota((128, OBS), 0), iota((128, OBS), 1)
    for n in range(2):
        out_ref[W_EMBED + 128 * n : W_EMBED + 128 * n + 128, :] = dot(onehot(r == k + REC * n), embed).astype(bf16)
    moves[2].wait()
    for n in range(2):
        out_ref[W_IN + CH * n : W_IN + CH * n + CH, :] = in_ref[:, halves[n]].astype(bf16)


def prepare(kernel, rows, which, arrays, shapes):
    v = pltpu.VMEM
    return pl.pallas_call(
        kernel,
        in_specs=[pl.BlockSpec(memory_space=pltpu.SMEM)] + [pl.BlockSpec(memory_space=pltpu.HBM)] * len(arrays),
        out_specs=pl.BlockSpec(memory_space=v),
        out_shape=jax.ShapeDtypeStruct((rows, CH), bf16),
        scratch_shapes=[v(shape, f32) for shape in shapes] + [pltpu.SemaphoreType.DMA((4,))],
        cost_estimate=pl.CostEstimate(flops=0, bytes_accessed=2_500_000, transcendentals=0),
        compiler_params=pltpu.CompilerParams(vmem_limit_bytes=60 * 1024 * 1024),
    )(which, *arrays)


def grad_kernel(
    which_ref, own_ref, core_ref, recv_ref, big_ref, w_ref, scale_ref, other_ref,
    keep_ref, give_ref, stat_ref,
    xc, xt, hid, c0, c1, c2, c3, g0, g1, g2, first, second, dout, dp2, dp1, dhid, dm0, dm1, dm2, dpair,
    acc_conv, acc_in, acc_mid, acc_head, acc_stat,
):
    own = own_ref[0] == 1
    cs, gs, dms = (c0, c1, c2), (g0, g1, g2), (dm0, dm1, dm2)
    for ref in cs:
        ref[0:PAD, :] = jnp.zeros((PAD, CH), bf16)
    for ref in dms:
        ref[ALL_ROWS : ALL_ROWS + PAD, :] = jnp.zeros((PAD, CH), bf16)

    r, k = iota((SPANS, SOURCES * SLOT), 0), iota((SPANS, SOURCES * SLOT), 1)
    compact = onehot(((k & 7) < CAP) & (r == (k >> 3) * CAP + (k & 7)))
    r, k = iota((64, 128), 0), iota((64, 128), 1)
    entry = r & 31
    select = onehot((entry < 16) & (k == entry + OBS + (r >> 5) * REC))
    sub = iota((16, 1), 0)
    is_act = sub < ACT
    scale = jnp.where(own, scale_ref[...], other_ref[...])
    scale = jnp.where(which_ref[0] == 0, scale[0:1, :], scale[1:2, :])
    log_scale = jnp.sum(jnp.where(iota((16, ACT), 0) == iota((16, ACT), 1), scale, 0.0), axis=1, keepdims=True)
    conv = [big_ref.at[2 * CH * layer : 2 * CH * layer + 2 * CH] for layer in range(3)]
    in_half = [w_ref.at[W_IN + CH * n : W_IN + CH * n + CH] for n in range(2)]
    mid_half = [big_ref.at[W_MID + UNITS * n : W_MID + UNITS * n + UNITS] for n in range(2)]
    embed_half = [w_ref.at[W_EMBED + 128 * n : W_EMBED + 128 * n + 128] for n in range(2)]
    head_half = [w_ref.at[W_HEAD + 16 * n : W_HEAD + 16 * n + 16] for n in range(2)]

    def across(halves, rows):
        return jnp.concatenate([half[rows, :] for half in halves], axis=1)

    inverse = jnp.where(is_act, jnp.exp(-log_scale), 0.0)
    offset = jnp.sum(jnp.where(is_act, log_scale, 0.0), axis=0, keepdims=True) + ACT * half_log_tau
    lane = iota((1, ROWS), 1)
    odd = lane < 0
    for s in range(1, CHUNK_STEPS, 2):
        odd = odd | ((lane >= s * SPANS) & (lane < (s + 1) * SPANS))

    pairs = CHUNK_STEPS // 2
    blocks = (0, 256)

    def rows(i, shift=0):
        return slice(i * ROWS + shift, (i + 1) * ROWS + shift)

    def add(ref, at, value, start):
        if start:
            ref[at] = value
        else:
            ref[at] += value

    def elu(x):
        below = jnp.minimum((jnp.exp(x) - 1.0).astype(bf16), jnp.zeros((), bf16))
        return jnp.maximum(x.astype(bf16), below)

    def slope(y):
        return jnp.minimum(y, jnp.zeros((), bf16)) + jnp.ones((), bf16)

    def forward(i):
        def enter():
            x = dot(compact, recv_ref[:, i * pairs * 128 : (i + 1) * pairs * 128]).astype(bf16)
            for p in range(pairs):
                part = x[:, 128 * p : 128 * p + 128]
                at = i * (ROWS // 2) + p * SPANS
                xc[at : at + SPANS, :] = part
                for half in range(2):
                    at = i * ROWS + (2 * p + half) * SPANS
                    xt[at : at + SPANS, :] = part
            y = [dot(xc[i * (ROWS // 2) : (i + 1) * (ROWS // 2), :], half[...]) for half in embed_half]
            for p in range(pairs):
                for half in range(2):
                    at = i * ROWS + (2 * p + half) * SPANS
                    h = y[half][p * SPANS : (p + 1) * SPANS, :]
                    hid[at - i * ROWS : at - i * ROWS + SPANS, :] = h
                    c0[PAD + at : PAD + at + SPANS, :] = h.astype(bf16)

        def encode(layer):
            c, lag = cs[layer], SPANS * 2**layer
            both = jnp.concatenate([c[rows(i, PAD), :], c[rows(i, PAD - lag), :]], axis=1)
            mix = dot(both, conv[layer][...])
            grown = jnp.exp(mix)
            h = hid[...] + jnp.maximum(mix, jnp.minimum(grown - 1.0, 0.0))
            gs[layer][rows(i), :] = grown.astype(bf16)
            if layer < 2:
                hid[...] = h
                cs[layer + 1][rows(i, PAD), :] = h.astype(bf16)
            else:
                c3[rows(i), :] = h.astype(bf16)

        def widen(n):
            first[rows(i), n : n + 256] = elu(dot(c3[rows(i), :], in_half[n // 256][...]))

        def deepen(n):
            second[rows(i), n : n + 256] = elu(dot(first[rows(i), :], mid_half[n // 256][...]))

        yield enter
        for layer in range(3):
            yield lambda layer=layer: encode(layer)
        for n in blocks:
            yield lambda n=n: widen(n)
        for n in blocks:
            yield lambda n=n: deepen(n)

    def backward(i):
        def loss():
            out = dot_nt(across(head_half, slice(0, 16)), second[rows(i), :])
            record = dot_nt(select, xt[rows(i), :])
            record = jnp.where(odd, record[32:64], record[0:32])
            diff = record[0:16] - out
            scaled = diff * inverse
            square = scaled * scaled
            advantage, old_logp, live = record[13:14], record[14:15], record[15:16]
            log_ratio = -0.5 * jnp.sum(square, axis=0, keepdims=True) - offset - old_logp
            ratio = jnp.exp(log_ratio)
            dlog = live * (0.5 * (ratio - 1.0) - ratio * advantage)
            dvalue = -0.5 * live * diff
            d = jnp.where(sub == ACT, dvalue, dlog * scaled * inverse)
            dout[...] = d.astype(bf16)
            total = jnp.sum(dlog * (square - 1.0), axis=1, keepdims=True)
            add(acc_stat, Ellipsis, jnp.broadcast_to(total, acc_stat.shape), i == 0)

        def down(n):
            ds = dot_tn(dout[...], head_half[n // 256][...])
            dp2[:, n : n + 256] = ds.astype(bf16) * slope(second[rows(i), n : n + 256])

        def head():
            add(acc_head, Ellipsis, dot(dout[...], second[rows(i), :]), i == 0)

        def middle(n):
            df = dot_nt(dp2[...], across(mid_half, slice(n, n + 256)))
            dp1[:, n : n + 256] = df.astype(bf16) * slope(first[rows(i), n : n + 256])

        def top():
            dhid[rows(i), :] = dot_nt(dp1[...], across(in_half, slice(0, CH)))

        def grad_mid():
            add(acc_mid, Ellipsis, dot_tn(first[rows(i), :], dp2[...]), i == 0)

        def grad_in():
            add(acc_in, Ellipsis, dot_tn(c3[rows(i), :], dp1[...]), i == 0)

        yield loss
        for n in blocks:
            yield lambda n=n: down(n)
        yield head
        for n in blocks:
            yield lambda n=n: middle(n)
        yield top
        yield grad_mid
        yield grad_in

    def decode(i):
        start = i == CHUNKS - 1
        for layer in (2, 1, 0):
            c, dm, lag = cs[layer], dms[layer], SPANS * 2**layer
            dh = dhid[rows(i), :]
            dm[rows(i), :] = dh.astype(bf16) * jnp.minimum(gs[layer][rows(i), :], jnp.ones((), bf16))
            dc = dot_nt(dm[rows(i), :], conv[layer][0:256, :])
            dc = dc + dot_nt(dm[rows(i, lag), :], conv[layer][256:512, :])
            dh = dh + dc
            if layer > 0:
                dhid[rows(i), :] = dh
            else:
                for s in range(CHUNK_STEPS):
                    at = i * (ROWS // 2) + (s // 2) * SPANS
                    part = dh[s * SPANS : s * SPANS + SPANS].astype(bf16)
                    dpair[at : at + SPANS, 256 * (s % 2) : 256 * (s % 2) + 256] = part
            both = jnp.concatenate([c[rows(i, PAD), :], c[rows(i, PAD - lag), :]], axis=1)
            add(acc_conv, layer, dot_tn(both, dm[rows(i), :]), start)

    def weave(left, right):
        left, right = list(left), list(right)
        order = [((k + 0.5) / len(left), 0, f) for k, f in enumerate(left)]
        order += [((k + 0.5) / len(right), 1, f) for k, f in enumerate(right)]
        for _, _, run in sorted(order, key=lambda item: item[:2]):
            run()

    weave(forward(0), [])
    for i in range(1, CHUNKS):
        weave(forward(i), backward(i - 1))
    weave(backward(CHUNKS - 1), [])
    for i in range(CHUNKS - 1, -1, -1):
        decode(i)

    dembed = dot_tn(xc[...], dpair[...])
    dembed = (dembed[0:OBS, 0:256] + dembed[REC : REC + OBS, 256:512]).astype(bf16)
    r, k = iota((SHARDS * 8, OBS), 0), iota((SHARDS * 8, OBS), 1)
    spread = onehot(((r & 7) < 3) & (k == (r >> 3) * 3 + (r & 7)))
    extra = dot(spread, dembed).astype(bf16)
    dhead = acc_head[...].astype(bf16)

    def write(encoder_ref, trunk_ref):
        for s in range(SHARDS):
            for q in range(6):
                encoder_ref[s, 16 * q : 16 * q + 16, :] = acc_conv[q // 2, 256 * (q % 2) + 16 * s : 256 * (q % 2) + 16 * s + 16, :].astype(bf16)
            encoder_ref[s, 96:104, :] = extra[8 * s : 8 * s + 8, :]
            for n in range(2):
                cols = slice(256 * n, 256 * n + 256)
                trunk_ref[s, 16 * n : 16 * n + 16, :] = acc_in[16 * s : 16 * s + 16, cols].astype(bf16)
                trunk_ref[s, 32 + 32 * n : 64 + 32 * n, :] = acc_mid[32 * s : 32 * s + 32, cols].astype(bf16)
            trunk_ref[s, 96:104, :] = jnp.zeros((8, 256), bf16)
            for n in range(2):
                trunk_ref[s, 96:104, 32 * n : 32 * n + 32] = dhead[8 * n : 8 * n + 8, 32 * s : 32 * s + 32]

    @pl.when(core_ref[0] == 0)
    def _():
        write(keep_ref, give_ref)

    @pl.when(core_ref[0] == 1)
    def _():
        write(give_ref, keep_ref)

    at = (iota((16, 128), 0) == iota((16, 128), 1)) & is_act
    line = jnp.sum(jnp.where(at, acc_stat[...], 0.0), axis=0, keepdims=True)
    stat_ref[...] = jnp.broadcast_to(line, (8, 128))


def member_grad(which, own, core, recv, big, small, scale, other):
    v = pltpu.VMEM
    half = ALL_ROWS // 2
    return pl.pallas_call(
        grad_kernel,
        out_shape=(
            jax.ShapeDtypeStruct((SHARDS, HALF, 256), bf16),
            jax.ShapeDtypeStruct((SHARDS, HALF, 256), bf16),
            jax.ShapeDtypeStruct((8, 128), f32),
        ),
        in_specs=[pl.BlockSpec(memory_space=pltpu.SMEM)] * 3 + [pl.BlockSpec(memory_space=v)] * 5,
        scratch_shapes=[
            v((half, 128), bf16), v((ALL_ROWS, 128), bf16), v((ROWS, CH), f32),
            v((PAD + ALL_ROWS, CH), bf16), v((PAD + ALL_ROWS, CH), bf16), v((PAD + ALL_ROWS, CH), bf16),
            v((ALL_ROWS, CH), bf16),
            v((ALL_ROWS, CH), bf16), v((ALL_ROWS, CH), bf16), v((ALL_ROWS, CH), bf16),
            v((ALL_ROWS, UNITS), bf16), v((ALL_ROWS, UNITS), bf16), v((16, ROWS), bf16),
            v((ROWS, UNITS), bf16), v((ROWS, UNITS), bf16),
            v((ALL_ROWS, CH), f32),
            v((ALL_ROWS + PAD, CH), bf16), v((ALL_ROWS + PAD, CH), bf16), v((ALL_ROWS + PAD, CH), bf16),
            v((half, 512), bf16),
            v((3, 2 * CH, CH), f32), v((CH, UNITS), f32), v((UNITS, UNITS), f32), v((16, UNITS), f32), v((16, 128), f32),
        ],
        cost_estimate=pl.CostEstimate(flops=11_200_000_000, bytes_accessed=4_000_000, transcendentals=4_000_000),
        compiler_params=pltpu.CompilerParams(vmem_limit_bytes=42 * 1024 * 1024),
        name="grad",
    )(which, own, core, recv, big, small, scale, other)


def reduce_kernel(core_ref, recv_ref, stat_ref, mine_ref, theirs_ref, cast_ref):
    lane1 = iota((1, 128), 1)
    line = pltpu.roll(stat_ref[0:1, :], 32, 1)
    for whose, out_ref in ((core_ref[0], mine_ref), (1 - core_ref[0], theirs_ref)):
        for j in range(2):
            kind = 2 * whose + j
            total = recv_ref[kind].astype(f32)
            for z in range(1, 4):
                total = total + recv_ref[4 * z + kind].astype(f32)
            out_ref[j] = total
            line = line + jnp.where(lane1 == kind, jnp.sum(total * total), 0.0)
    for s in range(SHARDS):
        cast_ref[8 * s : 8 * s + 8, :] = jnp.broadcast_to(line, (8, 128))


def reduce_parts(core, recv, stat):
    part = jax.ShapeDtypeStruct((2, HALF, 256), f32)
    return pl.pallas_call(
        reduce_kernel,
        out_shape=(part, part, jax.ShapeDtypeStruct((SHARDS * 8, 128), f32)),
        in_specs=[pl.BlockSpec(memory_space=pltpu.SMEM)] + [pl.BlockSpec(memory_space=pltpu.VMEM)] * 2,
        compiler_params=pltpu.CompilerParams(vmem_limit_bytes=16 * 1024 * 1024),
        name="reduce",
    )(core, recv, stat)


def finish_kernel(core_ref, mine_ref, theirs_ref, near_ref, far_ref, embed_ref, conv_ref, in_ref, mid_ref, head_ref, std_ref):
    core = core_ref[0]
    lane1 = iota((1, 128), 1)
    total = jnp.sum(near_ref[...] + far_ref[...], axis=0, keepdims=True) * 0.125
    scales = []
    for j in range(2):
        kind = 2 * core + j
        std = jnp.zeros((1, 128), f32)
        for z in range(4):
            at = pl.ds(pl.multiple_of(8 * (4 * z + kind), 8), 8)
            std = std + near_ref[at, :][0:1] + far_ref[at, :][0:1]
        std = jnp.where((lane1 >= 32) & (lane1 < 32 + ACT), std, 0.0)
        square = jnp.sum(std * std + jnp.where(lane1 == kind, total, 0.0), axis=1, keepdims=True)
        scale = 1.0 / jnp.sqrt(square / ENTRIES + 1e-06)
        std_ref[j : j + 1, :] = (std * scale)[:, 32 : 32 + ACT]
        scales.append(scale)

    def write(encoder_ref, trunk_ref):
        for j, scale in enumerate(scales):
            for q in range(6):
                conv_ref[j, q // 2, q % 2] = encoder_ref[j, 16 * q : 16 * q + 16, :] * scale
            embed_ref[:, j, :] = encoder_ref[j, 96:99, :] * scale
            for n in range(2):
                cols = slice(256 * n, 256 * n + 256)
                in_ref[j, :, cols] = trunk_ref[j, 16 * n : 16 * n + 16, :] * scale
                mid_ref[j, :, cols] = trunk_ref[j, 32 + 32 * n : 64 + 32 * n, :] * scale
            head_ref[0:8, j, :] = trunk_ref[j, 96:104, 0:32] * scale
            head_ref[8:13, j, :] = trunk_ref[j, 96:101, 32:64] * scale

    @pl.when(core == 0)
    def _():
        write(mine_ref, theirs_ref)

    @pl.when(core == 1)
    def _():
        write(theirs_ref, mine_ref)


def finish(core, mine, theirs, near, far):
    shapes = ((3, 2, 256), (2, 3, 2, 16, 256), (2, 16, 512), (2, 32, 512), (13, 2, 32), (2, 12))
    embed, conv, first, second, head, std = pl.pallas_call(
        finish_kernel,
        out_shape=tuple(jax.ShapeDtypeStruct(s, f32) for s in shapes),
        in_specs=[pl.BlockSpec(memory_space=pltpu.SMEM)] + [pl.BlockSpec(memory_space=pltpu.VMEM)] * 4,
        compiler_params=pltpu.CompilerParams(vmem_limit_bytes=16 * 1024 * 1024),
        name="finish",
    )(core, mine, theirs, near, far)
    return embed.transpose(1, 0, 2), conv, first, second, head.transpose(1, 2, 0), std


def swap(value):
    return lax.ppermute(value, "core", [(0, 1), (1, 0)])


def local(observations, rollout, done_flags, member_ids, embed_weight, conv_weight, trunk_in, trunk_mid, head_weight, log_std):
    x, core = lax.axis_index("x"), lax.axis_index("core")
    which, own = (x % 2).reshape(1), (core == x // 2).astype(jnp.int32).reshape(1)
    core = core.reshape(1)
    packed = pack(observations, rollout, done_flags, member_ids)
    recv = lax.all_to_all(packed, ("y", "x"), split_axis=0, concat_axis=0, tiled=True)
    arrays = (conv_weight, trunk_mid)
    shapes = tuple(x.shape[1:] for x in arrays)
    big = prepare(big_weights_kernel, BIG_ROWS, which, arrays, shapes)
    big_far = swap(big)
    head = head_weight.transpose(2, 0, 1)
    arrays = (embed_weight, trunk_in, head)
    shapes = tuple(x.shape[1:] for x in arrays[:2]) + (head.shape,)
    small = prepare(small_weights_kernel, SMALL_ROWS, which, arrays, shapes)
    mine = own[0] == 1
    big = jnp.where(mine, big, big_far)
    small = jnp.where(mine, small, swap(small))
    keep, give, stat = member_grad(which, own, core, recv, big, small, log_std, swap(log_std))
    both = (keep.astype(f32) + swap(give).astype(f32)).astype(bf16)
    parts = lax.all_to_all(both, ("z", "x"), split_axis=0, concat_axis=0, tiled=True)
    mine, theirs, cast = reduce_parts(core, parts, stat)
    near = lax.all_to_all(cast, ("z", "x"), split_axis=0, concat_axis=0, tiled=True)
    theirs, near = lax.optimization_barrier((theirs, near))
    return finish(core, mine, swap(theirs), near, swap(near))


def solution(mesh):
    fine = Mesh(mesh.devices.reshape(4, 2, 4, 4), ("y", "core", "z", "x"))
    member, dp = ("y", "core"), ("z", "x")
    every = member + dp
    return jax.shard_map(
        local,
        mesh=fine,
        in_specs=(P(every), P(every), P(every), P(every)) + (P(member),) * 6,
        out_specs=(
            P(member, dp),
            P(member, None, None, dp),
            P(member, dp),
            P(member, dp),
            P(member, dp),
            P(member),
        ),
        check_vma=False,
    )
```

```python
import jax
import jax.numpy as jnp
from jax import lax
from jax.experimental import pallas as pl
from jax.experimental.pallas import tpu as pltpu
from jax.sharding import Mesh, PartitionSpec as P


gamma_rate = 0.99
trace_rate = 0.95
half_log_tau = 0.9189385332046727

OBS = 48
STEPS = 24
ACT = 12
CH = 256
UNITS = 512
MEMBERS = 16
CAP = 6
SLOT = 8
REC = 64
WIDTH = STEPS * REC
ENTRIES = 805388
SOURCES = 16
SPANS = SOURCES * CAP
CHUNK_STEPS = 8
CHUNKS = STEPS // CHUNK_STEPS
ROWS = CHUNK_STEPS * SPANS
ALL_ROWS = STEPS * SPANS
PAD = 4 * SPANS
SHARDS = 16
HALF = 104
W_MID, W_IN, W_EMBED, W_HEAD, W_ROWS = 1536, 2560, 3072, 3328, 3360
f32 = jnp.float32
bf16 = jnp.bfloat16


def iota(shape, dim):
    return lax.broadcasted_iota(jnp.int32, shape, dim)


def dot(a, b):
    return jnp.dot(a, b, preferred_element_type=f32)


def dot_tn(a, b):
    return lax.dot_general(a, b, (((0,), (0,)), ((), ())), preferred_element_type=f32)


def dot_nt(a, b):
    return lax.dot_general(a, b, (((1,), (1,)), ((), ())), preferred_element_type=f32)


def onehot(cond):
    return jnp.where(cond, 1.0, 0.0).astype(bf16)


def pack_kernel(
    which_ref, obs_hbm, roll_hbm, done_hbm, ids_hbm, embed_hbm, conv_hbm, in_hbm, mid_hbm, head_hbm,
    out_ref, w_ref,
    obs_ref, roll_ref, done_ref, ids_ref, embed_ref, conv_ref, in_ref, mid_ref, head_ref,
    pick_ref, obs_at, act_at, scal_at, sems,
):
    which = which_ref[0]
    sources = [roll_hbm, done_hbm, obs_hbm, ids_hbm, head_hbm]
    sources += [conv_hbm.at[which], mid_hbm.at[which], in_hbm.at[which], embed_hbm.at[which]]
    targets = [roll_ref, done_ref, obs_ref, ids_ref, head_ref, conv_ref, mid_ref, in_ref, embed_ref]
    copies = [
        pltpu.make_async_copy(source, target, sems.at[k]) for k, (source, target) in enumerate(zip(sources, targets))
    ]
    moves, head_move, (conv_move, mid_move, in_move, embed_move) = copies[:4], copies[4], copies[5:]
    for move in copies:
        move.start()
    spans = obs_ref.shape[0]
    col = iota((1, 512), 1)
    spot, within, step = col & 63, col >> 6, col & 127
    row = iota((384, 512), 0)
    obs_at[...] = onehot(row == jnp.where(spot < 48, 48 * within + spot, -1))
    act_at[...] = onehot(row[0:128] == jnp.where((spot >= 48) & (spot < 60), 16 * within + spot - 48, -1))
    scal_at[...] = onehot(row == jnp.where((spot >= 60) & (spot < 63), (spot - 60) * 128 + within, -1))
    pick_ref[...] = onehot(row == jnp.where(step < STEPS, 16 * step + 12 + (col >> 7), -1))
    for move in moves:
        move.wait()
    parts = dot(roll_ref[...], pick_ref[...])
    reward, old_value = parts[:, 0:128], parts[:, 128:256]
    next_value, old_logp = parts[:, 256:384], parts[:, 384:512]
    widen = onehot(iota((STEPS, 128), 0) == iota((STEPS, 128), 1))
    done = dot_tn(done_ref[...].astype(f32).astype(bf16), widen)
    lane = iota((spans, 128), 1)
    alive = jnp.where(lane < STEPS, 1.0 - done, 0.0)
    advantage = reward + gamma_rate * alive * next_value - old_value
    carry = gamma_rate * trace_rate * alive
    for shift in (1, 2, 4, 8, 16):
        advantage = advantage + carry * pltpu.roll(advantage, 128 - shift, 1)
        carry = carry * pltpu.roll(carry, 128 - shift, 1)
    target = jnp.where(lane < STEPS, advantage + old_value, 0.0)
    advantage = jnp.where(lane < STEPS, advantage, 0.0)
    scalars = [target, advantage, old_logp]

    live = jnp.where((iota((spans, 512), 1) & 63) == 63, 1.0, 0.0)
    groups = []
    for g in range(3):
        placed = dot(obs_ref[:, 384 * g : 384 * g + 384], obs_at[...])
        placed = placed + dot(roll_ref[:, 128 * g : 128 * g + 128], act_at[...])
        turned = [pltpu.roll(x, (128 - 8 * g) % 128, 1) if g else x for x in scalars]
        turned = jnp.concatenate([x.astype(bf16) for x in turned], axis=1)
        placed = placed + dot(turned, scal_at[...]) + live
        groups.append(placed.astype(bf16))

    slots = MEMBERS * SLOT
    ids = ids_ref[...]
    slot, span = iota((slots, spans), 0), iota((slots, spans), 1)
    named = onehot(iota((MEMBERS, spans), 0) == ids)
    earlier = onehot(iota((spans, spans), 0) < iota((spans, spans), 1))
    rank = jnp.sum(dot(named, earlier) * named.astype(f32), axis=0, keepdims=True)
    dispatch = onehot(slot == ids * SLOT + rank.astype(jnp.int32))
    for g in range(3):
        out_ref[:, 512 * g : 512 * g + 512] = dot(dispatch, groups[g]).astype(bf16)

    halves = (slice(0, 256), slice(256, 512))
    head_move.wait()
    head = jnp.where(which == 0, head_ref[:, 0, :], head_ref[:, 1, :]).astype(bf16)
    head = dot(onehot(iota((16, ACT + 1), 0) == iota((16, ACT + 1), 1)), head).astype(bf16)
    for n in range(2):
        w_ref[W_HEAD + 16 * n : W_HEAD + 16 * n + 16, :] = head[:, halves[n]]
    conv_move.wait()
    for layer in range(3):
        for tap in range(2):
            at = CH * (2 * layer + tap)
            w_ref[at : at + CH, :] = conv_ref[layer, tap].astype(bf16)
    mid_move.wait()
    for n in range(2):
        w_ref[W_MID + UNITS * n : W_MID + UNITS * n + UNITS, :] = mid_ref[:, halves[n]].astype(bf16)
    in_move.wait()
    for n in range(2):
        w_ref[W_IN + CH * n : W_IN + CH * n + CH, :] = in_ref[:, halves[n]].astype(bf16)
    embed_move.wait()
    embed = embed_ref[...].astype(bf16)
    r, k = iota((128, OBS), 0), iota((128, OBS), 1)
    for n in range(2):
        w_ref[W_EMBED + 128 * n : W_EMBED + 128 * n + 128, :] = dot(onehot(r == k + REC * n), embed).astype(bf16)


def pack(which, observations, rollout, done_flags, member_ids, embed, conv, trunk_in, trunk_mid, head):
    v = pltpu.VMEM
    spans = (observations, rollout, done_flags.T, member_ids.T)
    weights = (embed, conv, trunk_in, trunk_mid)
    head = head.transpose(2, 0, 1)
    return pl.pallas_call(
        pack_kernel,
        out_shape=(jax.ShapeDtypeStruct((MEMBERS * SLOT, WIDTH), bf16), jax.ShapeDtypeStruct((W_ROWS, CH), bf16)),
        in_specs=[pl.BlockSpec(memory_space=pltpu.SMEM)] + [pl.BlockSpec(memory_space=pltpu.HBM)] * 9,
        out_specs=(pl.BlockSpec(memory_space=v), pl.BlockSpec(memory_space=v)),
        scratch_shapes=[v(x.shape, x.dtype) for x in spans]
        + [v(x.shape[1:], f32) for x in weights]
        + [v(head.shape, f32)]
        + [v((384, 512), bf16), v((384, 512), bf16), v((128, 512), bf16), v((384, 512), bf16)]
        + [pltpu.SemaphoreType.DMA((9,))],
        compiler_params=pltpu.CompilerParams(vmem_limit_bytes=60 * 1024 * 1024),
        name="pack",
    )(which, *spans, *weights, head)


def grad_kernel(
    which_ref, own_ref, core_ref, recv_ref, w_ref, scale_ref, other_ref,
    keep_ref, give_ref, stat_ref,
    xc, xt, hid, c0, c1, c2, c3, g0, g1, g2, first, second, dout, dp2, dp1, dhid, dm0, dm1, dm2, dpair,
    acc_conv, acc_in, acc_mid, acc_head, acc_stat,
):
    own = own_ref[0] == 1
    cs, gs, dms = (c0, c1, c2), (g0, g1, g2), (dm0, dm1, dm2)
    for ref in cs:
        ref[0:PAD, :] = jnp.zeros((PAD, CH), bf16)
    for ref in dms:
        ref[ALL_ROWS : ALL_ROWS + PAD, :] = jnp.zeros((PAD, CH), bf16)

    r, k = iota((SPANS, SOURCES * SLOT), 0), iota((SPANS, SOURCES * SLOT), 1)
    compact = onehot(((k & 7) < CAP) & (r == (k >> 3) * CAP + (k & 7)))
    r, k = iota((64, 128), 0), iota((64, 128), 1)
    entry = r & 31
    select = onehot((entry < 16) & (k == entry + OBS + (r >> 5) * REC))
    sub = iota((16, 1), 0)
    is_act = sub < ACT
    scale = jnp.where(own, scale_ref[...], other_ref[...])
    scale = jnp.where(which_ref[0] == 0, scale[0:1, :], scale[1:2, :])
    log_scale = jnp.sum(jnp.where(iota((16, ACT), 0) == iota((16, ACT), 1), scale, 0.0), axis=1, keepdims=True)
    conv = [w_ref.at[2 * CH * layer : 2 * CH * layer + 2 * CH] for layer in range(3)]
    in_half = [w_ref.at[W_IN + CH * n : W_IN + CH * n + CH] for n in range(2)]
    mid_half = [w_ref.at[W_MID + UNITS * n : W_MID + UNITS * n + UNITS] for n in range(2)]
    embed_half = [w_ref.at[W_EMBED + 128 * n : W_EMBED + 128 * n + 128] for n in range(2)]
    head_half = [w_ref.at[W_HEAD + 16 * n : W_HEAD + 16 * n + 16] for n in range(2)]

    def across(halves, rows):
        return jnp.concatenate([half[rows, :] for half in halves], axis=1)

    inverse = jnp.where(is_act, jnp.exp(-log_scale), 0.0)
    offset = jnp.sum(jnp.where(is_act, log_scale, 0.0), axis=0, keepdims=True) + ACT * half_log_tau
    lane = iota((1, ROWS), 1)
    odd = lane < 0
    for s in range(1, CHUNK_STEPS, 2):
        odd = odd | ((lane >= s * SPANS) & (lane < (s + 1) * SPANS))

    pairs = CHUNK_STEPS // 2
    blocks = (0, 256)

    def rows(i, shift=0):
        return slice(i * ROWS + shift, (i + 1) * ROWS + shift)

    def add(ref, at, value, start):
        if start:
            ref[at] = value
        else:
            ref[at] += value

    def elu(x):
        below = jnp.minimum((jnp.exp(x) - 1.0).astype(bf16), jnp.zeros((), bf16))
        return jnp.maximum(x.astype(bf16), below)

    def slope(y):
        return jnp.minimum(y, jnp.zeros((), bf16)) + jnp.ones((), bf16)

    def forward(i):
        def enter():
            x = dot(compact, recv_ref[:, i * pairs * 128 : (i + 1) * pairs * 128]).astype(bf16)
            for p in range(pairs):
                part = x[:, 128 * p : 128 * p + 128]
                at = i * (ROWS // 2) + p * SPANS
                xc[at : at + SPANS, :] = part
                for half in range(2):
                    at = i * ROWS + (2 * p + half) * SPANS
                    xt[at : at + SPANS, :] = part
            y = [dot(xc[i * (ROWS // 2) : (i + 1) * (ROWS // 2), :], half[...]) for half in embed_half]
            for p in range(pairs):
                for half in range(2):
                    at = i * ROWS + (2 * p + half) * SPANS
                    h = y[half][p * SPANS : (p + 1) * SPANS, :]
                    hid[at - i * ROWS : at - i * ROWS + SPANS, :] = h
                    c0[PAD + at : PAD + at + SPANS, :] = h.astype(bf16)

        def encode(layer):
            c, lag = cs[layer], SPANS * 2**layer
            both = jnp.concatenate([c[rows(i, PAD), :], c[rows(i, PAD - lag), :]], axis=1)
            mix = dot(both, conv[layer][...])
            grown = jnp.exp(mix)
            h = hid[...] + jnp.maximum(mix, jnp.minimum(grown - 1.0, 0.0))
            gs[layer][rows(i), :] = grown.astype(bf16)
            if layer < 2:
                hid[...] = h
                cs[layer + 1][rows(i, PAD), :] = h.astype(bf16)
            else:
                c3[rows(i), :] = h.astype(bf16)

        def widen(n):
            first[rows(i), n : n + 256] = elu(dot(c3[rows(i), :], in_half[n // 256][...]))

        def deepen(n):
            second[rows(i), n : n + 256] = elu(dot(first[rows(i), :], mid_half[n // 256][...]))

        yield enter
        for layer in range(3):
            yield lambda layer=layer: encode(layer)
        for n in blocks:
            yield lambda n=n: widen(n)
        for n in blocks:
            yield lambda n=n: deepen(n)

    def backward(i):
        def loss():
            out = dot_nt(across(head_half, slice(0, 16)), second[rows(i), :])
            record = dot_nt(select, xt[rows(i), :])
            record = jnp.where(odd, record[32:64], record[0:32])
            diff = record[0:16] - out
            scaled = diff * inverse
            square = scaled * scaled
            advantage, old_logp, live = record[13:14], record[14:15], record[15:16]
            log_ratio = -0.5 * jnp.sum(square, axis=0, keepdims=True) - offset - old_logp
            ratio = jnp.exp(log_ratio)
            dlog = live * (0.5 * (ratio - 1.0) - ratio * advantage)
            dvalue = -0.5 * live * diff
            d = jnp.where(sub == ACT, dvalue, dlog * scaled * inverse)
            dout[...] = d.astype(bf16)
            total = jnp.sum(dlog * (square - 1.0), axis=1, keepdims=True)
            add(acc_stat, Ellipsis, jnp.broadcast_to(total, acc_stat.shape), i == 0)

        def down(n):
            ds = dot_tn(dout[...], head_half[n // 256][...])
            dp2[:, n : n + 256] = ds.astype(bf16) * slope(second[rows(i), n : n + 256])

        def head():
            add(acc_head, Ellipsis, dot(dout[...], second[rows(i), :]), i == 0)

        def middle(n):
            df = dot_nt(dp2[...], across(mid_half, slice(n, n + 256)))
            dp1[:, n : n + 256] = df.astype(bf16) * slope(first[rows(i), n : n + 256])

        def top():
            dhid[rows(i), :] = dot_nt(dp1[...], across(in_half, slice(0, CH)))

        def grad_mid():
            add(acc_mid, Ellipsis, dot_tn(first[rows(i), :], dp2[...]), i == 0)

        def grad_in():
            add(acc_in, Ellipsis, dot_tn(c3[rows(i), :], dp1[...]), i == 0)

        yield loss
        for n in blocks:
            yield lambda n=n: down(n)
        yield head
        for n in blocks:
            yield lambda n=n: middle(n)
        yield top
        yield grad_mid
        yield grad_in

    def decode(i):
        start = i == CHUNKS - 1
        for layer in (2, 1, 0):
            c, dm, lag = cs[layer], dms[layer], SPANS * 2**layer
            dh = dhid[rows(i), :]
            dm[rows(i), :] = dh.astype(bf16) * jnp.minimum(gs[layer][rows(i), :], jnp.ones((), bf16))
            dc = dot_nt(dm[rows(i), :], conv[layer][0:256, :])
            dc = dc + dot_nt(dm[rows(i, lag), :], conv[layer][256:512, :])
            dh = dh + dc
            if layer > 0:
                dhid[rows(i), :] = dh
            else:
                for s in range(CHUNK_STEPS):
                    at = i * (ROWS // 2) + (s // 2) * SPANS
                    part = dh[s * SPANS : s * SPANS + SPANS].astype(bf16)
                    dpair[at : at + SPANS, 256 * (s % 2) : 256 * (s % 2) + 256] = part
            both = jnp.concatenate([c[rows(i, PAD), :], c[rows(i, PAD - lag), :]], axis=1)
            add(acc_conv, layer, dot_tn(both, dm[rows(i), :]), start)

    def weave(left, right):
        left, right = list(left), list(right)
        order = [((k + 0.5) / len(left), 0, f) for k, f in enumerate(left)]
        order += [((k + 0.5) / len(right), 1, f) for k, f in enumerate(right)]
        for _, _, run in sorted(order, key=lambda item: item[:2]):
            run()

    weave(forward(0), [])
    for i in range(1, CHUNKS):
        weave(forward(i), backward(i - 1))
    weave(backward(CHUNKS - 1), [])
    for i in range(CHUNKS - 1, -1, -1):
        decode(i)

    dembed = dot_tn(xc[...], dpair[...])
    dembed = (dembed[0:OBS, 0:256] + dembed[REC : REC + OBS, 256:512]).astype(bf16)
    r, k = iota((SHARDS * 8, OBS), 0), iota((SHARDS * 8, OBS), 1)
    spread = onehot(((r & 7) < 3) & (k == (r >> 3) * 3 + (r & 7)))
    extra = dot(spread, dembed).astype(bf16)
    dhead = acc_head[...].astype(bf16)

    def write(encoder_ref, trunk_ref):
        for s in range(SHARDS):
            for q in range(6):
                encoder_ref[s, 16 * q : 16 * q + 16, :] = acc_conv[q // 2, 256 * (q % 2) + 16 * s : 256 * (q % 2) + 16 * s + 16, :].astype(bf16)
            encoder_ref[s, 96:104, :] = extra[8 * s : 8 * s + 8, :]
            for n in range(2):
                cols = slice(256 * n, 256 * n + 256)
                trunk_ref[s, 16 * n : 16 * n + 16, :] = acc_in[16 * s : 16 * s + 16, cols].astype(bf16)
                trunk_ref[s, 32 + 32 * n : 64 + 32 * n, :] = acc_mid[32 * s : 32 * s + 32, cols].astype(bf16)
            trunk_ref[s, 96:104, :] = jnp.zeros((8, 256), bf16)
            for n in range(2):
                trunk_ref[s, 96:104, 32 * n : 32 * n + 32] = dhead[8 * n : 8 * n + 8, 32 * s : 32 * s + 32]

    @pl.when(core_ref[0] == 0)
    def _():
        write(keep_ref, give_ref)

    @pl.when(core_ref[0] == 1)
    def _():
        write(give_ref, keep_ref)

    at = (iota((16, 128), 0) == iota((16, 128), 1)) & is_act
    line = jnp.sum(jnp.where(at, acc_stat[...], 0.0), axis=0, keepdims=True)
    stat_ref[...] = jnp.broadcast_to(line, (8, 128))


def member_grad(which, own, core, recv, weights, scale, other):
    v = pltpu.VMEM
    half = ALL_ROWS // 2
    return pl.pallas_call(
        grad_kernel,
        out_shape=(
            jax.ShapeDtypeStruct((SHARDS, HALF, 256), bf16),
            jax.ShapeDtypeStruct((SHARDS, HALF, 256), bf16),
            jax.ShapeDtypeStruct((8, 128), f32),
        ),
        in_specs=[pl.BlockSpec(memory_space=pltpu.SMEM)] * 3 + [pl.BlockSpec(memory_space=v)] * 4,
        scratch_shapes=[
            v((half, 128), bf16), v((ALL_ROWS, 128), bf16), v((ROWS, CH), f32),
            v((PAD + ALL_ROWS, CH), bf16), v((PAD + ALL_ROWS, CH), bf16), v((PAD + ALL_ROWS, CH), bf16),
            v((ALL_ROWS, CH), bf16),
            v((ALL_ROWS, CH), bf16), v((ALL_ROWS, CH), bf16), v((ALL_ROWS, CH), bf16),
            v((ALL_ROWS, UNITS), bf16), v((ALL_ROWS, UNITS), bf16), v((16, ROWS), bf16),
            v((ROWS, UNITS), bf16), v((ROWS, UNITS), bf16),
            v((ALL_ROWS, CH), f32),
            v((ALL_ROWS + PAD, CH), bf16), v((ALL_ROWS + PAD, CH), bf16), v((ALL_ROWS + PAD, CH), bf16),
            v((half, 512), bf16),
            v((3, 2 * CH, CH), f32), v((CH, UNITS), f32), v((UNITS, UNITS), f32), v((16, UNITS), f32), v((16, 128), f32),
        ],
        cost_estimate=pl.CostEstimate(flops=11_200_000_000, bytes_accessed=4_000_000, transcendentals=4_000_000),
        compiler_params=pltpu.CompilerParams(vmem_limit_bytes=42 * 1024 * 1024),
        name="grad",
    )(which, own, core, recv, weights, scale, other)


def reduce_kernel(core_ref, recv_ref, stat_ref, mine_ref, theirs_ref, cast_ref):
    lane1 = iota((1, 128), 1)
    line = pltpu.roll(stat_ref[0:1, :], 32, 1)
    for whose, out_ref in ((core_ref[0], mine_ref), (1 - core_ref[0], theirs_ref)):
        for j in range(2):
            kind = 2 * whose + j
            total = recv_ref[kind].astype(f32)
            for z in range(1, 4):
                total = total + recv_ref[4 * z + kind].astype(f32)
            out_ref[j] = total
            line = line + jnp.where(lane1 == kind, jnp.sum(total * total), 0.0)
    for s in range(2 * SHARDS):
        cast_ref[8 * s : 8 * s + 8, :] = jnp.broadcast_to(line, (8, 128))


def reduce_parts(core, recv, stat):
    part = jax.ShapeDtypeStruct((2, HALF, 256), f32)
    return pl.pallas_call(
        reduce_kernel,
        out_shape=(part, part, jax.ShapeDtypeStruct((2 * SHARDS * 8, 128), f32)),
        in_specs=[pl.BlockSpec(memory_space=pltpu.SMEM)] + [pl.BlockSpec(memory_space=pltpu.VMEM)] * 2,
        compiler_params=pltpu.CompilerParams(vmem_limit_bytes=16 * 1024 * 1024),
        name="reduce",
    )(core, recv, stat)


def finish_kernel(core_ref, mine_ref, theirs_ref, lines_ref, embed_ref, conv_ref, in_ref, mid_ref, head_ref, std_ref):
    core = core_ref[0]
    lane1 = iota((1, 128), 1)
    total = jnp.sum(lines_ref[...], axis=0, keepdims=True) * 0.125
    scales = []
    for j in range(2):
        kind = 2 * core + j
        std = jnp.zeros((1, 128), f32)
        for z in range(8):
            at = pl.ds(pl.multiple_of(8 * (4 * z + kind), 8), 8)
            std = std + lines_ref[at, :][0:1]
        std = jnp.where((lane1 >= 32) & (lane1 < 32 + ACT), std, 0.0)
        square = jnp.sum(std * std + jnp.where(lane1 == kind, total, 0.0), axis=1, keepdims=True)
        scale = 1.0 / jnp.sqrt(square / ENTRIES + 1e-06)
        std_ref[j : j + 1, :] = (std * scale)[:, 32 : 32 + ACT]
        scales.append(scale)

    def write(encoder_ref, trunk_ref):
        for j, scale in enumerate(scales):
            for q in range(6):
                conv_ref[j, q // 2, q % 2] = encoder_ref[j, 16 * q : 16 * q + 16, :] * scale
            embed_ref[:, j, :] = encoder_ref[j, 96:99, :] * scale
            for n in range(2):
                cols = slice(256 * n, 256 * n + 256)
                in_ref[j, :, cols] = trunk_ref[j, 16 * n : 16 * n + 16, :] * scale
                mid_ref[j, :, cols] = trunk_ref[j, 32 + 32 * n : 64 + 32 * n, :] * scale
            head_ref[0:8, j, :] = trunk_ref[j, 96:104, 0:32] * scale
            head_ref[8:13, j, :] = trunk_ref[j, 96:101, 32:64] * scale

    @pl.when(core == 0)
    def _():
        write(mine_ref, theirs_ref)

    @pl.when(core == 1)
    def _():
        write(theirs_ref, mine_ref)


def finish(core, mine, theirs, lines):
    shapes = ((3, 2, 256), (2, 3, 2, 16, 256), (2, 16, 512), (2, 32, 512), (13, 2, 32), (2, 12))
    embed, conv, first, second, head, std = pl.pallas_call(
        finish_kernel,
        out_shape=tuple(jax.ShapeDtypeStruct(s, f32) for s in shapes),
        in_specs=[pl.BlockSpec(memory_space=pltpu.SMEM)] + [pl.BlockSpec(memory_space=pltpu.VMEM)] * 3,
        compiler_params=pltpu.CompilerParams(vmem_limit_bytes=16 * 1024 * 1024),
        name="finish",
    )(core, mine, theirs, lines)
    return embed.transpose(1, 0, 2), conv, first, second, head.transpose(1, 2, 0), std


def swap(value):
    return lax.ppermute(value, "core", [(0, 1), (1, 0)])


def local(observations, rollout, done_flags, member_ids, embed_weight, conv_weight, trunk_in, trunk_mid, head_weight, log_std):
    x, core = lax.axis_index("x"), lax.axis_index("core")
    which, own = (x % 2).reshape(1), (core == x // 2).astype(jnp.int32).reshape(1)
    core = core.reshape(1)
    packed, weights = pack(
        which, observations, rollout, done_flags, member_ids, embed_weight, conv_weight, trunk_in, trunk_mid, head_weight
    )
    far = swap(weights)
    recv = lax.all_to_all(packed, ("y", "x"), split_axis=0, concat_axis=0, tiled=True)
    other = swap(log_std)
    weights = jnp.where(own[0] == 1, weights, far)
    keep, give, stat = member_grad(which, own, core, recv, weights, log_std, other)
    both = (keep.astype(f32) + swap(give).astype(f32)).astype(bf16)
    parts = lax.all_to_all(both, ("z", "x"), split_axis=0, concat_axis=0, tiled=True)
    mine, theirs, cast = reduce_parts(core, parts, stat)
    lines = lax.all_to_all(cast, ("core", "z", "x"), split_axis=0, concat_axis=0, tiled=True)
    return finish(core, mine, swap(theirs), lines)


def solution(mesh):
    fine = Mesh(mesh.devices.reshape(4, 2, 4, 4), ("y", "core", "z", "x"))
    member, dp = ("y", "core"), ("z", "x")
    every = member + dp
    return jax.shard_map(
        local,
        mesh=fine,
        in_specs=(P(every), P(every), P(every), P(every)) + (P(member),) * 6,
        out_specs=(
            P(member, dp),
            P(member, None, None, dp),
            P(member, dp),
            P(member, dp),
            P(member, dp),
            P(member),
        ),
        check_vma=False,
    )
```

```python
import jax
import jax.numpy as jnp
from jax import lax
from jax.experimental import pallas as pl
from jax.experimental.pallas import tpu as pltpu
from jax.sharding import Mesh, PartitionSpec as P


gamma_rate = 0.99
trace_rate = 0.95
half_log_tau = 0.9189385332046727

OBS = 48
STEPS = 24
ACT = 12
CH = 256
UNITS = 512
MEMBERS = 16
CAP = 6
SLOT = 8
REC = 64
WIDTH = STEPS * REC
ENTRIES = 805388
SOURCES = 16
SPANS = SOURCES * CAP
CHUNK_STEPS = 8
CHUNKS = STEPS // CHUNK_STEPS
ROWS = CHUNK_STEPS * SPANS
ALL_ROWS = STEPS * SPANS
PAD = 4 * SPANS
SHARDS = 16
HALF = 104
W_MID, W_IN, W_EMBED, W_HEAD, W_ROWS = 1536, 2560, 3072, 3328, 3360
f32 = jnp.float32
bf16 = jnp.bfloat16


def iota(shape, dim):
    return lax.broadcasted_iota(jnp.int32, shape, dim)


def dot(a, b):
    return jnp.dot(a, b, preferred_element_type=f32)


def dot_tn(a, b):
    return lax.dot_general(a, b, (((0,), (0,)), ((), ())), preferred_element_type=f32)


def dot_nt(a, b):
    return lax.dot_general(a, b, (((1,), (1,)), ((), ())), preferred_element_type=f32)


def onehot(cond):
    return jnp.where(cond, 1.0, 0.0).astype(bf16)


def pack_kernel(
    which_ref, obs_hbm, roll_hbm, done_hbm, ids_hbm, embed_hbm, conv_hbm, in_hbm, mid_hbm, head_hbm,
    out_hbm, w_hbm,
    out_ref, w_ref, obs_ref, roll_ref, done_ref, ids_ref, embed_ref, conv_ref, in_ref, mid_ref, head_ref,
    pick_ref, obs_at, act_at, scal_at, sems,
):
    which = which_ref[0]
    sources = [roll_hbm, done_hbm, obs_hbm, ids_hbm, head_hbm]
    sources += [conv_hbm.at[which], mid_hbm.at[which], in_hbm.at[which], embed_hbm.at[which]]
    targets = [roll_ref, done_ref, obs_ref, ids_ref, head_ref, conv_ref, mid_ref, in_ref, embed_ref]
    copies = [
        pltpu.make_async_copy(source, target, sems.at[k]) for k, (source, target) in enumerate(zip(sources, targets))
    ]
    moves, head_move, (conv_move, mid_move, in_move, embed_move) = copies[:4], copies[4], copies[5:]
    for move in copies:
        move.start()

    def store(k, start, stop):
        return pltpu.make_async_copy(w_ref.at[start:stop], w_hbm.at[start:stop], sems.at[k])

    stores = [pltpu.make_async_copy(out_ref, out_hbm, sems.at[9])]
    stores += [store(10, 0, W_MID), store(11, W_MID, W_IN), store(12, W_IN, W_ROWS)]
    spans = obs_ref.shape[0]
    col = iota((1, 512), 1)
    spot, within, step = col & 63, col >> 6, col & 127
    row = iota((384, 512), 0)
    obs_at[...] = onehot(row == jnp.where(spot < 48, 48 * within + spot, -1))
    act_at[...] = onehot(row[0:128] == jnp.where((spot >= 48) & (spot < 60), 16 * within + spot - 48, -1))
    scal_at[...] = onehot(row == jnp.where((spot >= 60) & (spot < 63), (spot - 60) * 128 + within, -1))
    pick_ref[...] = onehot(row == jnp.where(step < STEPS, 16 * step + 12 + (col >> 7), -1))
    for move in moves:
        move.wait()
    parts = dot(roll_ref[...], pick_ref[...])
    reward, old_value = parts[:, 0:128], parts[:, 128:256]
    next_value, old_logp = parts[:, 256:384], parts[:, 384:512]
    widen = onehot(iota((STEPS, 128), 0) == iota((STEPS, 128), 1))
    done = dot_tn(done_ref[...].astype(f32).astype(bf16), widen)
    lane = iota((spans, 128), 1)
    alive = jnp.where(lane < STEPS, 1.0 - done, 0.0)
    advantage = reward + gamma_rate * alive * next_value - old_value
    carry = gamma_rate * trace_rate * alive
    for shift in (1, 2, 4, 8, 16):
        advantage = advantage + carry * pltpu.roll(advantage, 128 - shift, 1)
        carry = carry * pltpu.roll(carry, 128 - shift, 1)
    target = jnp.where(lane < STEPS, advantage + old_value, 0.0)
    advantage = jnp.where(lane < STEPS, advantage, 0.0)
    scalars = [target, advantage, old_logp]

    live = jnp.where((iota((spans, 512), 1) & 63) == 63, 1.0, 0.0)
    groups = []
    for g in range(3):
        placed = dot(obs_ref[:, 384 * g : 384 * g + 384], obs_at[...])
        placed = placed + dot(roll_ref[:, 128 * g : 128 * g + 128], act_at[...])
        turned = [pltpu.roll(x, (128 - 8 * g) % 128, 1) if g else x for x in scalars]
        turned = jnp.concatenate([x.astype(bf16) for x in turned], axis=1)
        placed = placed + dot(turned, scal_at[...]) + live
        groups.append(placed.astype(bf16))

    slots = MEMBERS * SLOT
    ids = ids_ref[...]
    slot, span = iota((slots, spans), 0), iota((slots, spans), 1)
    named = onehot(iota((MEMBERS, spans), 0) == ids)
    earlier = onehot(iota((spans, spans), 0) < iota((spans, spans), 1))
    rank = jnp.sum(dot(named, earlier) * named.astype(f32), axis=0, keepdims=True)
    dispatch = onehot(slot == ids * SLOT + rank.astype(jnp.int32))
    for g in range(3):
        out_ref[:, 512 * g : 512 * g + 512] = dot(dispatch, groups[g]).astype(bf16)
    stores[0].start()

    halves = (slice(0, 256), slice(256, 512))
    head_move.wait()
    head = jnp.where(which == 0, head_ref[:, 0, :], head_ref[:, 1, :]).astype(bf16)
    head = dot(onehot(iota((16, ACT + 1), 0) == iota((16, ACT + 1), 1)), head).astype(bf16)
    for n in range(2):
        w_ref[W_HEAD + 16 * n : W_HEAD + 16 * n + 16, :] = head[:, halves[n]]
    conv_move.wait()
    for layer in range(3):
        for tap in range(2):
            at = CH * (2 * layer + tap)
            w_ref[at : at + CH, :] = conv_ref[layer, tap].astype(bf16)
    stores[1].start()
    mid_move.wait()
    for n in range(2):
        w_ref[W_MID + UNITS * n : W_MID + UNITS * n + UNITS, :] = mid_ref[:, halves[n]].astype(bf16)
    stores[2].start()
    in_move.wait()
    for n in range(2):
        w_ref[W_IN + CH * n : W_IN + CH * n + CH, :] = in_ref[:, halves[n]].astype(bf16)
    embed_move.wait()
    embed = embed_ref[...].astype(bf16)
    r, k = iota((128, OBS), 0), iota((128, OBS), 1)
    for n in range(2):
        w_ref[W_EMBED + 128 * n : W_EMBED + 128 * n + 128, :] = dot(onehot(r == k + REC * n), embed).astype(bf16)
    stores[3].start()
    for move in stores:
        move.wait()


def pack(which, observations, rollout, done_flags, member_ids, embed, conv, trunk_in, trunk_mid, head):
    v = pltpu.VMEM
    spans = (observations, rollout, done_flags.T, member_ids.T)
    weights = (embed, conv, trunk_in, trunk_mid)
    head = head.transpose(2, 0, 1)
    return pl.pallas_call(
        pack_kernel,
        out_shape=(jax.ShapeDtypeStruct((MEMBERS * SLOT, WIDTH), bf16), jax.ShapeDtypeStruct((W_ROWS, CH), bf16)),
        in_specs=[pl.BlockSpec(memory_space=pltpu.SMEM)] + [pl.BlockSpec(memory_space=pltpu.HBM)] * 9,
        out_specs=(pl.BlockSpec(memory_space=pltpu.HBM), pl.BlockSpec(memory_space=pltpu.HBM)),
        scratch_shapes=[v((MEMBERS * SLOT, WIDTH), bf16), v((W_ROWS, CH), bf16)]
        + [v(x.shape, x.dtype) for x in spans]
        + [v(x.shape[1:], f32) for x in weights]
        + [v(head.shape, f32)]
        + [v((384, 512), bf16), v((384, 512), bf16), v((128, 512), bf16), v((384, 512), bf16)]
        + [pltpu.SemaphoreType.DMA((13,))],
        compiler_params=pltpu.CompilerParams(vmem_limit_bytes=60 * 1024 * 1024),
        name="pack",
    )(which, *spans, *weights, head)


def grad_kernel(
    which_ref, own_ref, core_ref, recv_ref, w_ref, scale_ref, other_ref,
    keep_ref, give_ref, stat_ref,
    xc, xt, hid, c0, c1, c2, c3, g0, g1, g2, first, second, dout, dp2, dp1, dhid, dm0, dm1, dm2, dpair,
    acc_conv, acc_in, acc_mid, acc_head, acc_stat,
):
    own = own_ref[0] == 1
    cs, gs, dms = (c0, c1, c2), (g0, g1, g2), (dm0, dm1, dm2)
    for ref in cs:
        ref[0:PAD, :] = jnp.zeros((PAD, CH), bf16)
    for ref in dms:
        ref[ALL_ROWS : ALL_ROWS + PAD, :] = jnp.zeros((PAD, CH), bf16)

    r, k = iota((SPANS, SOURCES * SLOT), 0), iota((SPANS, SOURCES * SLOT), 1)
    compact = onehot(((k & 7) < CAP) & (r == (k >> 3) * CAP + (k & 7)))
    r, k = iota((64, 128), 0), iota((64, 128), 1)
    entry = r & 31
    select = onehot((entry < 16) & (k == entry + OBS + (r >> 5) * REC))
    sub = iota((16, 1), 0)
    is_act = sub < ACT
    scale = jnp.where(own, scale_ref[...], other_ref[...])
    scale = jnp.where(which_ref[0] == 0, scale[0:1, :], scale[1:2, :])
    log_scale = jnp.sum(jnp.where(iota((16, ACT), 0) == iota((16, ACT), 1), scale, 0.0), axis=1, keepdims=True)
    conv = [w_ref.at[2 * CH * layer : 2 * CH * layer + 2 * CH] for layer in range(3)]
    in_half = [w_ref.at[W_IN + CH * n : W_IN + CH * n + CH] for n in range(2)]
    mid_half = [w_ref.at[W_MID + UNITS * n : W_MID + UNITS * n + UNITS] for n in range(2)]
    embed_half = [w_ref.at[W_EMBED + 128 * n : W_EMBED + 128 * n + 128] for n in range(2)]
    head_half = [w_ref.at[W_HEAD + 16 * n : W_HEAD + 16 * n + 16] for n in range(2)]

    def across(halves, rows):
        return jnp.concatenate([half[rows, :] for half in halves], axis=1)

    inverse = jnp.where(is_act, jnp.exp(-log_scale), 0.0)
    offset = jnp.sum(jnp.where(is_act, log_scale, 0.0), axis=0, keepdims=True) + ACT * half_log_tau
    lane = iota((1, ROWS), 1)
    odd = lane < 0
    for s in range(1, CHUNK_STEPS, 2):
        odd = odd | ((lane >= s * SPANS) & (lane < (s + 1) * SPANS))

    pairs = CHUNK_STEPS // 2
    blocks = (0, 256)

    def rows(i, shift=0):
        return slice(i * ROWS + shift, (i + 1) * ROWS + shift)

    def add(ref, at, value, start):
        if start:
            ref[at] = value
        else:
            ref[at] += value

    def elu(x):
        below = jnp.minimum((jnp.exp(x) - 1.0).astype(bf16), jnp.zeros((), bf16))
        return jnp.maximum(x.astype(bf16), below)

    def slope(y):
        return jnp.minimum(y, jnp.zeros((), bf16)) + jnp.ones((), bf16)

    def forward(i):
        def enter():
            x = dot(compact, recv_ref[:, i * pairs * 128 : (i + 1) * pairs * 128]).astype(bf16)
            for p in range(pairs):
                part = x[:, 128 * p : 128 * p + 128]
                at = i * (ROWS // 2) + p * SPANS
                xc[at : at + SPANS, :] = part
                for half in range(2):
                    at = i * ROWS + (2 * p + half) * SPANS
                    xt[at : at + SPANS, :] = part
            y = [dot(xc[i * (ROWS // 2) : (i + 1) * (ROWS // 2), :], half[...]) for half in embed_half]
            for p in range(pairs):
                for half in range(2):
                    at = i * ROWS + (2 * p + half) * SPANS
                    h = y[half][p * SPANS : (p + 1) * SPANS, :]
                    hid[at - i * ROWS : at - i * ROWS + SPANS, :] = h
                    c0[PAD + at : PAD + at + SPANS, :] = h.astype(bf16)

        def encode(layer):
            c, lag = cs[layer], SPANS * 2**layer
            both = jnp.concatenate([c[rows(i, PAD), :], c[rows(i, PAD - lag), :]], axis=1)
            mix = dot(both, conv[layer][...])
            grown = jnp.exp(mix)
            h = hid[...] + jnp.maximum(mix, jnp.minimum(grown - 1.0, 0.0))
            gs[layer][rows(i), :] = grown.astype(bf16)
            if layer < 2:
                hid[...] = h
                cs[layer + 1][rows(i, PAD), :] = h.astype(bf16)
            else:
                c3[rows(i), :] = h.astype(bf16)

        def widen(n):
            first[rows(i), n : n + 256] = elu(dot(c3[rows(i), :], in_half[n // 256][...]))

        def deepen(n):
            second[rows(i), n : n + 256] = elu(dot(first[rows(i), :], mid_half[n // 256][...]))

        yield enter
        for layer in range(3):
            yield lambda layer=layer: encode(layer)
        for n in blocks:
            yield lambda n=n: widen(n)
        for n in blocks:
            yield lambda n=n: deepen(n)

    def backward(i):
        def loss():
            out = dot_nt(across(head_half, slice(0, 16)), second[rows(i), :])
            record = dot_nt(select, xt[rows(i), :])
            record = jnp.where(odd, record[32:64], record[0:32])
            diff = record[0:16] - out
            scaled = diff * inverse
            square = scaled * scaled
            advantage, old_logp, live = record[13:14], record[14:15], record[15:16]
            log_ratio = -0.5 * jnp.sum(square, axis=0, keepdims=True) - offset - old_logp
            ratio = jnp.exp(log_ratio)
            dlog = live * (0.5 * (ratio - 1.0) - ratio * advantage)
            dvalue = -0.5 * live * diff
            d = jnp.where(sub == ACT, dvalue, dlog * scaled * inverse)
            dout[...] = d.astype(bf16)
            total = jnp.sum(dlog * (square - 1.0), axis=1, keepdims=True)
            add(acc_stat, Ellipsis, jnp.broadcast_to(total, acc_stat.shape), i == 0)

        def down(n):
            ds = dot_tn(dout[...], head_half[n // 256][...])
            dp2[:, n : n + 256] = ds.astype(bf16) * slope(second[rows(i), n : n + 256])

        def head():
            add(acc_head, Ellipsis, dot(dout[...], second[rows(i), :]), i == 0)

        def middle(n):
            df = dot_nt(dp2[...], across(mid_half, slice(n, n + 256)))
            dp1[:, n : n + 256] = df.astype(bf16) * slope(first[rows(i), n : n + 256])

        def top():
            dhid[rows(i), :] = dot_nt(dp1[...], across(in_half, slice(0, CH)))

        def grad_mid():
            add(acc_mid, Ellipsis, dot_tn(first[rows(i), :], dp2[...]), i == 0)

        def grad_in():
            add(acc_in, Ellipsis, dot_tn(c3[rows(i), :], dp1[...]), i == 0)

        yield loss
        for n in blocks:
            yield lambda n=n: down(n)
        yield head
        for n in blocks:
            yield lambda n=n: middle(n)
        yield top
        yield grad_mid
        yield grad_in

    def decode(i):
        start = i == CHUNKS - 1
        for layer in (2, 1, 0):
            c, dm, lag = cs[layer], dms[layer], SPANS * 2**layer
            dh = dhid[rows(i), :]
            dm[rows(i), :] = dh.astype(bf16) * jnp.minimum(gs[layer][rows(i), :], jnp.ones((), bf16))
            dc = dot_nt(dm[rows(i), :], conv[layer][0:256, :])
            dc = dc + dot_nt(dm[rows(i, lag), :], conv[layer][256:512, :])
            dh = dh + dc
            if layer > 0:
                dhid[rows(i), :] = dh
            else:
                for s in range(CHUNK_STEPS):
                    at = i * (ROWS // 2) + (s // 2) * SPANS
                    part = dh[s * SPANS : s * SPANS + SPANS].astype(bf16)
                    dpair[at : at + SPANS, 256 * (s % 2) : 256 * (s % 2) + 256] = part
            both = jnp.concatenate([c[rows(i, PAD), :], c[rows(i, PAD - lag), :]], axis=1)
            add(acc_conv, layer, dot_tn(both, dm[rows(i), :]), start)

    def weave(left, right):
        left, right = list(left), list(right)
        order = [((k + 0.5) / len(left), 0, f) for k, f in enumerate(left)]
        order += [((k + 0.5) / len(right), 1, f) for k, f in enumerate(right)]
        for _, _, run in sorted(order, key=lambda item: item[:2]):
            run()

    weave(forward(0), [])
    for i in range(1, CHUNKS):
        weave(forward(i), backward(i - 1))
    weave(backward(CHUNKS - 1), [])
    for i in range(CHUNKS - 1, -1, -1):
        decode(i)

    dembed = dot_tn(xc[...], dpair[...])
    dembed = (dembed[0:OBS, 0:256] + dembed[REC : REC + OBS, 256:512]).astype(bf16)
    r, k = iota((SHARDS * 8, OBS), 0), iota((SHARDS * 8, OBS), 1)
    spread = onehot(((r & 7) < 3) & (k == (r >> 3) * 3 + (r & 7)))
    extra = dot(spread, dembed).astype(bf16)
    dhead = acc_head[...].astype(bf16)

    def write(encoder_ref, trunk_ref):
        for s in range(SHARDS):
            for q in range(6):
                encoder_ref[s, 16 * q : 16 * q + 16, :] = acc_conv[q // 2, 256 * (q % 2) + 16 * s : 256 * (q % 2) + 16 * s + 16, :].astype(bf16)
            encoder_ref[s, 96:104, :] = extra[8 * s : 8 * s + 8, :]
            for n in range(2):
                cols = slice(256 * n, 256 * n + 256)
                trunk_ref[s, 16 * n : 16 * n + 16, :] = acc_in[16 * s : 16 * s + 16, cols].astype(bf16)
                trunk_ref[s, 32 + 32 * n : 64 + 32 * n, :] = acc_mid[32 * s : 32 * s + 32, cols].astype(bf16)
            trunk_ref[s, 96:104, :] = jnp.zeros((8, 256), bf16)
            for n in range(2):
                trunk_ref[s, 96:104, 32 * n : 32 * n + 32] = dhead[8 * n : 8 * n + 8, 32 * s : 32 * s + 32]

    @pl.when(core_ref[0] == 0)
    def _():
        write(keep_ref, give_ref)

    @pl.when(core_ref[0] == 1)
    def _():
        write(give_ref, keep_ref)

    at = (iota((16, 128), 0) == iota((16, 128), 1)) & is_act
    line = jnp.sum(jnp.where(at, acc_stat[...], 0.0), axis=0, keepdims=True)
    stat_ref[...] = jnp.broadcast_to(line, (8, 128))


def member_grad(which, own, core, recv, weights, scale, other):
    v = pltpu.VMEM
    half = ALL_ROWS // 2
    return pl.pallas_call(
        grad_kernel,
        out_shape=(
            jax.ShapeDtypeStruct((SHARDS, HALF, 256), bf16),
            jax.ShapeDtypeStruct((SHARDS, HALF, 256), bf16),
            jax.ShapeDtypeStruct((8, 128), f32),
        ),
        in_specs=[pl.BlockSpec(memory_space=pltpu.SMEM)] * 3 + [pl.BlockSpec(memory_space=v)] * 4,
        scratch_shapes=[
            v((half, 128), bf16), v((ALL_ROWS, 128), bf16), v((ROWS, CH), f32),
            v((PAD + ALL_ROWS, CH), bf16), v((PAD + ALL_ROWS, CH), bf16), v((PAD + ALL_ROWS, CH), bf16),
            v((ALL_ROWS, CH), bf16),
            v((ALL_ROWS, CH), bf16), v((ALL_ROWS, CH), bf16), v((ALL_ROWS, CH), bf16),
            v((ALL_ROWS, UNITS), bf16), v((ALL_ROWS, UNITS), bf16), v((16, ROWS), bf16),
            v((ROWS, UNITS), bf16), v((ROWS, UNITS), bf16),
            v((ALL_ROWS, CH), f32),
            v((ALL_ROWS + PAD, CH), bf16), v((ALL_ROWS + PAD, CH), bf16), v((ALL_ROWS + PAD, CH), bf16),
            v((half, 512), bf16),
            v((3, 2 * CH, CH), f32), v((CH, UNITS), f32), v((UNITS, UNITS), f32), v((16, UNITS), f32), v((16, 128), f32),
        ],
        cost_estimate=pl.CostEstimate(flops=11_200_000_000, bytes_accessed=4_000_000, transcendentals=4_000_000),
        compiler_params=pltpu.CompilerParams(vmem_limit_bytes=42 * 1024 * 1024),
        name="grad",
    )(which, own, core, recv, weights, scale, other)


def reduce_kernel(core_ref, recv_ref, stat_ref, mine_ref, theirs_ref, cast_ref):
    lane1 = iota((1, 128), 1)
    line = pltpu.roll(stat_ref[0:1, :], 32, 1)
    for whose, out_ref in ((core_ref[0], mine_ref), (1 - core_ref[0], theirs_ref)):
        for j in range(2):
            kind = 2 * whose + j
            total = recv_ref[kind].astype(f32)
            for z in range(1, 4):
                total = total + recv_ref[4 * z + kind].astype(f32)
            out_ref[j] = total
            line = line + jnp.where(lane1 == kind, jnp.sum(total * total), 0.0)
    for s in range(2 * SHARDS):
        cast_ref[8 * s : 8 * s + 8, :] = jnp.broadcast_to(line, (8, 128))


def reduce_parts(core, recv, stat):
    part = jax.ShapeDtypeStruct((2, HALF, 256), f32)
    return pl.pallas_call(
        reduce_kernel,
        out_shape=(part, part, jax.ShapeDtypeStruct((2 * SHARDS * 8, 128), f32)),
        in_specs=[pl.BlockSpec(memory_space=pltpu.SMEM)] + [pl.BlockSpec(memory_space=pltpu.VMEM)] * 2,
        compiler_params=pltpu.CompilerParams(vmem_limit_bytes=16 * 1024 * 1024),
        name="reduce",
    )(core, recv, stat)


def finish_kernel(core_ref, mine_ref, theirs_ref, lines_ref, embed_ref, conv_ref, in_ref, mid_ref, head_ref, std_ref):
    core = core_ref[0]
    lane1 = iota((1, 128), 1)
    total = jnp.sum(lines_ref[...], axis=0, keepdims=True) * 0.125
    scales = []
    for j in range(2):
        kind = 2 * core + j
        std = jnp.zeros((1, 128), f32)
        for z in range(8):
            at = pl.ds(pl.multiple_of(8 * (4 * z + kind), 8), 8)
            std = std + lines_ref[at, :][0:1]
        std = jnp.where((lane1 >= 32) & (lane1 < 32 + ACT), std, 0.0)
        square = jnp.sum(std * std + jnp.where(lane1 == kind, total, 0.0), axis=1, keepdims=True)
        scale = 1.0 / jnp.sqrt(square / ENTRIES + 1e-06)
        std_ref[j : j + 1, :] = (std * scale)[:, 32 : 32 + ACT]
        scales.append(scale)

    def write(encoder_ref, trunk_ref):
        for j, scale in enumerate(scales):
            for q in range(6):
                conv_ref[j, q // 2, q % 2] = encoder_ref[j, 16 * q : 16 * q + 16, :] * scale
            embed_ref[:, j, :] = encoder_ref[j, 96:99, :] * scale
            for n in range(2):
                cols = slice(256 * n, 256 * n + 256)
                in_ref[j, :, cols] = trunk_ref[j, 16 * n : 16 * n + 16, :] * scale
                mid_ref[j, :, cols] = trunk_ref[j, 32 + 32 * n : 64 + 32 * n, :] * scale
            head_ref[0:8, j, :] = trunk_ref[j, 96:104, 0:32] * scale
            head_ref[8:13, j, :] = trunk_ref[j, 96:101, 32:64] * scale

    @pl.when(core == 0)
    def _():
        write(mine_ref, theirs_ref)

    @pl.when(core == 1)
    def _():
        write(theirs_ref, mine_ref)


def finish(core, mine, theirs, lines):
    shapes = ((3, 2, 256), (2, 3, 2, 16, 256), (2, 16, 512), (2, 32, 512), (13, 2, 32), (2, 12))
    embed, conv, first, second, head, std = pl.pallas_call(
        finish_kernel,
        out_shape=tuple(jax.ShapeDtypeStruct(s, f32) for s in shapes),
        in_specs=[pl.BlockSpec(memory_space=pltpu.SMEM)] + [pl.BlockSpec(memory_space=pltpu.VMEM)] * 3,
        compiler_params=pltpu.CompilerParams(vmem_limit_bytes=16 * 1024 * 1024),
        name="finish",
    )(core, mine, theirs, lines)
    return embed.transpose(1, 0, 2), conv, first, second, head.transpose(1, 2, 0), std


def swap(value):
    return lax.ppermute(value, "core", [(0, 1), (1, 0)])


def local(observations, rollout, done_flags, member_ids, embed_weight, conv_weight, trunk_in, trunk_mid, head_weight, log_std):
    x, core = lax.axis_index("x"), lax.axis_index("core")
    which, own = (x % 2).reshape(1), (core == x // 2).astype(jnp.int32).reshape(1)
    core = core.reshape(1)
    packed, weights = pack(
        which, observations, rollout, done_flags, member_ids, embed_weight, conv_weight, trunk_in, trunk_mid, head_weight
    )
    far = swap(weights)
    recv = lax.all_to_all(packed, ("y", "x"), split_axis=0, concat_axis=0, tiled=True)
    other = swap(log_std)
    weights = jnp.where(own[0] == 1, weights, far)
    keep, give, stat = member_grad(which, own, core, recv, weights, log_std, other)
    both = (keep.astype(f32) + swap(give).astype(f32)).astype(bf16)
    parts = lax.all_to_all(both, ("z", "x"), split_axis=0, concat_axis=0, tiled=True)
    mine, theirs, cast = reduce_parts(core, parts, stat)
    lines = lax.all_to_all(cast, ("core", "z", "x"), split_axis=0, concat_axis=0, tiled=True)
    theirs = swap(theirs)
    return finish(core, mine, theirs, lines)


def solution(mesh):
    fine = Mesh(mesh.devices.reshape(4, 2, 4, 4), ("y", "core", "z", "x"))
    member, dp = ("y", "core"), ("z", "x")
    every = member + dp
    return jax.shard_map(
        local,
        mesh=fine,
        in_specs=(P(every), P(every), P(every), P(every)) + (P(member),) * 6,
        out_specs=(
            P(member, dp),
            P(member, None, None, dp),
            P(member, dp),
            P(member, dp),
            P(member, dp),
            P(member),
        ),
        check_vma=False,
    )
```

```python
import jax
import jax.numpy as jnp
from jax import lax
from jax.experimental import pallas as pl
from jax.experimental.pallas import tpu as pltpu
from jax.sharding import Mesh, PartitionSpec as P


gamma_rate = 0.99
trace_rate = 0.95
half_log_tau = 0.9189385332046727

OBS = 48
STEPS = 24
ACT = 12
CH = 256
UNITS = 512
MEMBERS = 16
CAP = 6
SLOT = 8
REC = 64
WIDTH = STEPS * REC
ENTRIES = 805388
SOURCES = 16
SPANS = SOURCES * CAP
CHUNK_STEPS = 8
CHUNKS = STEPS // CHUNK_STEPS
ROWS = CHUNK_STEPS * SPANS
ALL_ROWS = STEPS * SPANS
PAD = 4 * SPANS
SHARDS = 16
HALF = 104
W_MID, W_IN, W_EMBED, W_HEAD, W_ROWS = 1536, 2560, 3072, 3328, 3360
f32 = jnp.float32
bf16 = jnp.bfloat16


def iota(shape, dim):
    return lax.broadcasted_iota(jnp.int32, shape, dim)


def dot(a, b):
    return jnp.dot(a, b, preferred_element_type=f32)


def dot_tn(a, b):
    return lax.dot_general(a, b, (((0,), (0,)), ((), ())), preferred_element_type=f32)


def dot_nt(a, b):
    return lax.dot_general(a, b, (((1,), (1,)), ((), ())), preferred_element_type=f32)


def onehot(cond):
    return jnp.where(cond, 1.0, 0.0).astype(bf16)


def pack_kernel(
    which_ref, obs_hbm, roll_hbm, done_hbm, ids_hbm, embed_hbm, conv_hbm, in_hbm, mid_hbm, head_hbm,
    out_hbm, w_hbm,
    out_ref, w_ref, obs_ref, roll_ref, done_ref, ids_ref, embed_ref, conv_ref, in_ref, mid_ref, head_ref,
    pick_ref, obs_at, act_at, scal_at, sems,
):
    which = which_ref[0]
    sources = [roll_hbm, done_hbm, obs_hbm, ids_hbm, head_hbm]
    sources += [conv_hbm.at[which], mid_hbm.at[which], in_hbm.at[which], embed_hbm.at[which]]
    targets = [roll_ref, done_ref, obs_ref, ids_ref, head_ref, conv_ref, mid_ref, in_ref, embed_ref]
    copies = [
        pltpu.make_async_copy(source, target, sems.at[k]) for k, (source, target) in enumerate(zip(sources, targets))
    ]
    moves, head_move, (conv_move, mid_move, in_move, embed_move) = copies[:4], copies[4], copies[5:]
    for move in copies:
        move.start()

    def store(k, start, stop):
        return pltpu.make_async_copy(w_ref.at[start:stop], w_hbm.at[start:stop], sems.at[k])

    stores = [pltpu.make_async_copy(out_ref, out_hbm, sems.at[9])]
    stores += [store(10, 0, W_MID), store(11, W_MID, W_IN), store(12, W_IN, W_ROWS)]
    spans = obs_ref.shape[0]
    col = iota((1, 512), 1)
    spot, within, step = col & 63, col >> 6, col & 127
    row = iota((384, 512), 0)
    obs_at[...] = onehot(row == jnp.where(spot < 48, 48 * within + spot, -1))
    act_at[...] = onehot(row[0:128] == jnp.where((spot >= 48) & (spot < 60), 16 * within + spot - 48, -1))
    scal_at[...] = onehot(row == jnp.where((spot >= 60) & (spot < 63), (spot - 60) * 128 + within, -1))
    pick_ref[...] = onehot(row == jnp.where(step < STEPS, 16 * step + 12 + (col >> 7), -1))
    for move in moves:
        move.wait()
    parts = dot(roll_ref[...], pick_ref[...])
    reward, old_value = parts[:, 0:128], parts[:, 128:256]
    next_value, old_logp = parts[:, 256:384], parts[:, 384:512]
    widen = onehot(iota((STEPS, 128), 0) == iota((STEPS, 128), 1))
    done = dot_tn(done_ref[...].astype(f32).astype(bf16), widen)
    lane = iota((spans, 128), 1)
    alive = jnp.where(lane < STEPS, 1.0 - done, 0.0)
    advantage = reward + gamma_rate * alive * next_value - old_value
    carry = gamma_rate * trace_rate * alive
    for shift in (1, 2, 4, 8, 16):
        advantage = advantage + carry * pltpu.roll(advantage, 128 - shift, 1)
        carry = carry * pltpu.roll(carry, 128 - shift, 1)
    target = jnp.where(lane < STEPS, advantage + old_value, 0.0)
    advantage = jnp.where(lane < STEPS, advantage, 0.0)
    scalars = [target, advantage, old_logp]

    live = jnp.where((iota((spans, 512), 1) & 63) == 63, 1.0, 0.0)
    groups = []
    for g in range(3):
        placed = dot(obs_ref[:, 384 * g : 384 * g + 384], obs_at[...])
        placed = placed + dot(roll_ref[:, 128 * g : 128 * g + 128], act_at[...])
        turned = [pltpu.roll(x, (128 - 8 * g) % 128, 1) if g else x for x in scalars]
        turned = jnp.concatenate([x.astype(bf16) for x in turned], axis=1)
        placed = placed + dot(turned, scal_at[...]) + live
        groups.append(placed.astype(bf16))

    slots = MEMBERS * SLOT
    ids = ids_ref[...]
    slot, span = iota((slots, spans), 0), iota((slots, spans), 1)
    named = onehot(iota((MEMBERS, spans), 0) == ids)
    earlier = onehot(iota((spans, spans), 0) < iota((spans, spans), 1))
    rank = jnp.sum(dot(named, earlier) * named.astype(f32), axis=0, keepdims=True)
    dispatch = onehot(slot == ids * SLOT + rank.astype(jnp.int32))
    for g in range(3):
        out_ref[:, 512 * g : 512 * g + 512] = dot(dispatch, groups[g]).astype(bf16)
    stores[0].start()

    halves = (slice(0, 256), slice(256, 512))
    head_move.wait()
    head = jnp.where(which == 0, head_ref[:, 0, :], head_ref[:, 1, :]).astype(bf16)
    head = dot(onehot(iota((16, ACT + 1), 0) == iota((16, ACT + 1), 1)), head).astype(bf16)
    for n in range(2):
        w_ref[W_HEAD + 16 * n : W_HEAD + 16 * n + 16, :] = head[:, halves[n]]
    conv_move.wait()
    for layer in range(3):
        for tap in range(2):
            at = CH * (2 * layer + tap)
            w_ref[at : at + CH, :] = conv_ref[layer, tap].astype(bf16)
    stores[1].start()
    mid_move.wait()
    for n in range(2):
        w_ref[W_MID + UNITS * n : W_MID + UNITS * n + UNITS, :] = mid_ref[:, halves[n]].astype(bf16)
    stores[2].start()
    in_move.wait()
    for n in range(2):
        w_ref[W_IN + CH * n : W_IN + CH * n + CH, :] = in_ref[:, halves[n]].astype(bf16)
    embed_move.wait()
    embed = embed_ref[...].astype(bf16)
    r, k = iota((128, OBS), 0), iota((128, OBS), 1)
    for n in range(2):
        w_ref[W_EMBED + 128 * n : W_EMBED + 128 * n + 128, :] = dot(onehot(r == k + REC * n), embed).astype(bf16)
    stores[3].start()
    for move in stores:
        move.wait()


def pack(which, observations, rollout, done_flags, member_ids, embed, conv, trunk_in, trunk_mid, head):
    v = pltpu.VMEM
    spans = (observations, rollout, done_flags.T, member_ids.T)
    weights = (embed, conv, trunk_in, trunk_mid)
    head = head.transpose(2, 0, 1)
    return pl.pallas_call(
        pack_kernel,
        out_shape=(jax.ShapeDtypeStruct((MEMBERS * SLOT, WIDTH), bf16), jax.ShapeDtypeStruct((W_ROWS, CH), bf16)),
        in_specs=[pl.BlockSpec(memory_space=pltpu.SMEM)] + [pl.BlockSpec(memory_space=pltpu.HBM)] * 9,
        out_specs=(pl.BlockSpec(memory_space=pltpu.HBM), pl.BlockSpec(memory_space=pltpu.HBM)),
        scratch_shapes=[v((MEMBERS * SLOT, WIDTH), bf16), v((W_ROWS, CH), bf16)]
        + [v(x.shape, x.dtype) for x in spans]
        + [v(x.shape[1:], f32) for x in weights]
        + [v(head.shape, f32)]
        + [v((384, 512), bf16), v((384, 512), bf16), v((128, 512), bf16), v((384, 512), bf16)]
        + [pltpu.SemaphoreType.DMA((13,))],
        compiler_params=pltpu.CompilerParams(vmem_limit_bytes=60 * 1024 * 1024),
        name="pack",
    )(which, *spans, *weights, head)


def grad_kernel(
    which_ref, own_ref, core_ref, recv_ref, w_ref, scale_ref, other_ref,
    keep_ref, give_ref, stat_ref,
    xc, xt, hid, c0, c1, c2, c3, g0, g1, g2, first, second, dout, dp2, dp1, dhid, dm0, dm1, dm2, dpair,
    acc_conv, acc_in, acc_mid, acc_head, acc_stat,
):
    own = own_ref[0] == 1
    cs, gs, dms = (c0, c1, c2), (g0, g1, g2), (dm0, dm1, dm2)
    for ref in cs:
        ref[0:PAD, :] = jnp.zeros((PAD, CH), bf16)
    for ref in dms:
        ref[ALL_ROWS : ALL_ROWS + PAD, :] = jnp.zeros((PAD, CH), bf16)

    r, k = iota((SPANS, SOURCES * SLOT), 0), iota((SPANS, SOURCES * SLOT), 1)
    compact = onehot(((k & 7) < CAP) & (r == (k >> 3) * CAP + (k & 7)))
    r, k = iota((64, 128), 0), iota((64, 128), 1)
    entry = r & 31
    select = onehot((entry < 16) & (k == entry + OBS + (r >> 5) * REC))
    sub = iota((16, 1), 0)
    is_act = sub < ACT
    scale = jnp.where(own, scale_ref[...], other_ref[...])
    scale = jnp.where(which_ref[0] == 0, scale[0:1, :], scale[1:2, :])
    log_scale = jnp.sum(jnp.where(iota((16, ACT), 0) == iota((16, ACT), 1), scale, 0.0), axis=1, keepdims=True)
    conv = [w_ref.at[2 * CH * layer : 2 * CH * layer + 2 * CH] for layer in range(3)]
    in_half = [w_ref.at[W_IN + CH * n : W_IN + CH * n + CH] for n in range(2)]
    mid_half = [w_ref.at[W_MID + UNITS * n : W_MID + UNITS * n + UNITS] for n in range(2)]
    embed_half = [w_ref.at[W_EMBED + 128 * n : W_EMBED + 128 * n + 128] for n in range(2)]
    head_half = [w_ref.at[W_HEAD + 16 * n : W_HEAD + 16 * n + 16] for n in range(2)]

    def across(halves, rows):
        return jnp.concatenate([half[rows, :] for half in halves], axis=1)

    inverse = jnp.where(is_act, jnp.exp(-log_scale), 0.0)
    offset = jnp.sum(jnp.where(is_act, log_scale, 0.0), axis=0, keepdims=True) + ACT * half_log_tau
    lane = iota((1, ROWS), 1)
    odd = lane < 0
    for s in range(1, CHUNK_STEPS, 2):
        odd = odd | ((lane >= s * SPANS) & (lane < (s + 1) * SPANS))

    pairs = CHUNK_STEPS // 2
    blocks = (0, 256)

    def rows(i, shift=0):
        return slice(i * ROWS + shift, (i + 1) * ROWS + shift)

    def add(ref, at, value, start):
        if start:
            ref[at] = value
        else:
            ref[at] += value

    def elu(x):
        below = jnp.minimum((jnp.exp(x) - 1.0).astype(bf16), jnp.zeros((), bf16))
        return jnp.maximum(x.astype(bf16), below)

    def slope(y):
        return jnp.minimum(y, jnp.zeros((), bf16)) + jnp.ones((), bf16)

    def forward(i):
        def enter():
            x = dot(compact, recv_ref[:, i * pairs * 128 : (i + 1) * pairs * 128]).astype(bf16)
            for p in range(pairs):
                part = x[:, 128 * p : 128 * p + 128]
                at = i * (ROWS // 2) + p * SPANS
                xc[at : at + SPANS, :] = part
                for half in range(2):
                    at = i * ROWS + (2 * p + half) * SPANS
                    xt[at : at + SPANS, :] = part
            y = [dot(xc[i * (ROWS // 2) : (i + 1) * (ROWS // 2), :], half[...]) for half in embed_half]
            for p in range(pairs):
                for half in range(2):
                    at = i * ROWS + (2 * p + half) * SPANS
                    h = y[half][p * SPANS : (p + 1) * SPANS, :]
                    hid[at - i * ROWS : at - i * ROWS + SPANS, :] = h
                    c0[PAD + at : PAD + at + SPANS, :] = h.astype(bf16)

        def encode(layer):
            c, lag = cs[layer], SPANS * 2**layer
            both = jnp.concatenate([c[rows(i, PAD), :], c[rows(i, PAD - lag), :]], axis=1)
            mix = dot(both, conv[layer][...])
            grown = jnp.exp(mix)
            h = hid[...] + jnp.maximum(mix, jnp.minimum(grown - 1.0, 0.0))
            gs[layer][rows(i), :] = grown.astype(bf16)
            if layer < 2:
                hid[...] = h
                cs[layer + 1][rows(i, PAD), :] = h.astype(bf16)
            else:
                c3[rows(i), :] = h.astype(bf16)

        def widen(n):
            first[rows(i), n : n + 256] = elu(dot(c3[rows(i), :], in_half[n // 256][...]))

        def deepen(n):
            second[rows(i), n : n + 256] = elu(dot(first[rows(i), :], mid_half[n // 256][...]))

        yield enter
        for layer in range(3):
            yield lambda layer=layer: encode(layer)
        for n in blocks:
            yield lambda n=n: widen(n)
        for n in blocks:
            yield lambda n=n: deepen(n)

    def backward(i):
        def loss():
            out = dot_nt(across(head_half, slice(0, 16)), second[rows(i), :])
            record = dot_nt(select, xt[rows(i), :])
            record = jnp.where(odd, record[32:64], record[0:32])
            diff = record[0:16] - out
            scaled = diff * inverse
            square = scaled * scaled
            advantage, old_logp, live = record[13:14], record[14:15], record[15:16]
            log_ratio = -0.5 * jnp.sum(square, axis=0, keepdims=True) - offset - old_logp
            ratio = jnp.exp(log_ratio)
            dlog = live * (0.5 * (ratio - 1.0) - ratio * advantage)
            dvalue = -0.5 * live * diff
            d = jnp.where(sub == ACT, dvalue, dlog * scaled * inverse)
            dout[...] = d.astype(bf16)
            total = jnp.sum(dlog * (square - 1.0), axis=1, keepdims=True)
            add(acc_stat, Ellipsis, jnp.broadcast_to(total, acc_stat.shape), i == 0)

        def down(n):
            ds = dot_tn(dout[...], head_half[n // 256][...])
            dp2[:, n : n + 256] = ds.astype(bf16) * slope(second[rows(i), n : n + 256])

        def head():
            add(acc_head, Ellipsis, dot(dout[...], second[rows(i), :]), i == 0)

        def middle(n):
            df = dot_nt(dp2[...], across(mid_half, slice(n, n + 256)))
            dp1[:, n : n + 256] = df.astype(bf16) * slope(first[rows(i), n : n + 256])

        def top():
            dhid[rows(i), :] = dot_nt(dp1[...], across(in_half, slice(0, CH)))

        def grad_mid():
            add(acc_mid, Ellipsis, dot_tn(first[rows(i), :], dp2[...]), i == 0)

        def grad_in():
            add(acc_in, Ellipsis, dot_tn(c3[rows(i), :], dp1[...]), i == 0)

        yield loss
        for n in blocks:
            yield lambda n=n: down(n)
        yield head
        for n in blocks:
            yield lambda n=n: middle(n)
        yield top
        yield grad_mid
        yield grad_in

    def decode(i):
        start = i == CHUNKS - 1
        for layer in (2, 1, 0):
            c, dm, lag = cs[layer], dms[layer], SPANS * 2**layer
            dh = dhid[rows(i), :]
            dm[rows(i), :] = dh.astype(bf16) * jnp.minimum(gs[layer][rows(i), :], jnp.ones((), bf16))
            dc = dot_nt(dm[rows(i), :], conv[layer][0:256, :])
            dc = dc + dot_nt(dm[rows(i, lag), :], conv[layer][256:512, :])
            dh = dh + dc
            if layer > 0:
                dhid[rows(i), :] = dh
            else:
                for s in range(CHUNK_STEPS):
                    at = i * (ROWS // 2) + (s // 2) * SPANS
                    part = dh[s * SPANS : s * SPANS + SPANS].astype(bf16)
                    dpair[at : at + SPANS, 256 * (s % 2) : 256 * (s % 2) + 256] = part
            both = jnp.concatenate([c[rows(i, PAD), :], c[rows(i, PAD - lag), :]], axis=1)
            add(acc_conv, layer, dot_tn(both, dm[rows(i), :]), start)

    def weave(left, right):
        left, right = list(left), list(right)
        order = [((k + 0.5) / len(left), 0, f) for k, f in enumerate(left)]
        order += [((k + 0.5) / len(right), 1, f) for k, f in enumerate(right)]
        for _, _, run in sorted(order, key=lambda item: item[:2]):
            run()

    weave(forward(0), [])
    for i in range(1, CHUNKS):
        weave(forward(i), backward(i - 1))
    weave(backward(CHUNKS - 1), [])
    for i in range(CHUNKS - 1, -1, -1):
        decode(i)

    dembed = dot_tn(xc[...], dpair[...])
    dembed = (dembed[0:OBS, 0:256] + dembed[REC : REC + OBS, 256:512]).astype(bf16)
    r, k = iota((SHARDS * 8, OBS), 0), iota((SHARDS * 8, OBS), 1)
    spread = onehot(((r & 7) < 3) & (k == (r >> 3) * 3 + (r & 7)))
    extra = dot(spread, dembed).astype(bf16)
    dhead = acc_head[...].astype(bf16)

    def write(encoder_ref, trunk_ref):
        for s in range(SHARDS):
            for q in range(6):
                encoder_ref[s, 16 * q : 16 * q + 16, :] = acc_conv[q // 2, 256 * (q % 2) + 16 * s : 256 * (q % 2) + 16 * s + 16, :].astype(bf16)
            encoder_ref[s, 96:104, :] = extra[8 * s : 8 * s + 8, :]
            for n in range(2):
                cols = slice(256 * n, 256 * n + 256)
                trunk_ref[s, 16 * n : 16 * n + 16, :] = acc_in[16 * s : 16 * s + 16, cols].astype(bf16)
                trunk_ref[s, 32 + 32 * n : 64 + 32 * n, :] = acc_mid[32 * s : 32 * s + 32, cols].astype(bf16)
            trunk_ref[s, 96:104, :] = jnp.zeros((8, 256), bf16)
            for n in range(2):
                trunk_ref[s, 96:104, 32 * n : 32 * n + 32] = dhead[8 * n : 8 * n + 8, 32 * s : 32 * s + 32]

    @pl.when(core_ref[0] == 0)
    def _():
        write(keep_ref, give_ref)

    @pl.when(core_ref[0] == 1)
    def _():
        write(give_ref, keep_ref)

    at = (iota((16, 128), 0) == iota((16, 128), 1)) & is_act
    line = jnp.sum(jnp.where(at, acc_stat[...], 0.0), axis=0, keepdims=True)
    stat_ref[...] = jnp.broadcast_to(line, (8, 128))


def member_grad(which, own, core, recv, weights, scale, other):
    v = pltpu.VMEM
    half = ALL_ROWS // 2
    return pl.pallas_call(
        grad_kernel,
        out_shape=(
            jax.ShapeDtypeStruct((SHARDS, HALF, 256), bf16),
            jax.ShapeDtypeStruct((SHARDS, HALF, 256), bf16),
            jax.ShapeDtypeStruct((8, 128), f32),
        ),
        in_specs=[pl.BlockSpec(memory_space=pltpu.SMEM)] * 3 + [pl.BlockSpec(memory_space=v)] * 4,
        scratch_shapes=[
            v((half, 128), bf16), v((ALL_ROWS, 128), bf16), v((ROWS, CH), f32),
            v((PAD + ALL_ROWS, CH), bf16), v((PAD + ALL_ROWS, CH), bf16), v((PAD + ALL_ROWS, CH), bf16),
            v((ALL_ROWS, CH), bf16),
            v((ALL_ROWS, CH), bf16), v((ALL_ROWS, CH), bf16), v((ALL_ROWS, CH), bf16),
            v((ALL_ROWS, UNITS), bf16), v((ALL_ROWS, UNITS), bf16), v((16, ROWS), bf16),
            v((ROWS, UNITS), bf16), v((ROWS, UNITS), bf16),
            v((ALL_ROWS, CH), f32),
            v((ALL_ROWS + PAD, CH), bf16), v((ALL_ROWS + PAD, CH), bf16), v((ALL_ROWS + PAD, CH), bf16),
            v((half, 512), bf16),
            v((3, 2 * CH, CH), f32), v((CH, UNITS), f32), v((UNITS, UNITS), f32), v((16, UNITS), f32), v((16, 128), f32),
        ],
        cost_estimate=pl.CostEstimate(flops=11_200_000_000, bytes_accessed=4_000_000, transcendentals=4_000_000),
        compiler_params=pltpu.CompilerParams(vmem_limit_bytes=42 * 1024 * 1024),
        name="grad",
    )(which, own, core, recv, weights, scale, other)


def reduce_kernel(core_ref, recv_ref, stat_ref, mine_ref, theirs_ref, cast_ref):
    lane1 = iota((1, 128), 1)
    line = pltpu.roll(stat_ref[0:1, :], 32, 1)
    for whose, out_ref in ((core_ref[0], mine_ref), (1 - core_ref[0], theirs_ref)):
        for j in range(2):
            kind = 2 * whose + j
            total = recv_ref[kind].astype(f32)
            for z in range(1, 4):
                total = total + recv_ref[4 * z + kind].astype(f32)
            out_ref[j] = total
            line = line + jnp.where(lane1 == kind, jnp.sum(total * total), 0.0)
    for s in range(2 * SHARDS):
        cast_ref[s] = line


def reduce_parts(core, recv, stat):
    part = jax.ShapeDtypeStruct((2, HALF, 256), f32)
    return pl.pallas_call(
        reduce_kernel,
        out_shape=(part, part, jax.ShapeDtypeStruct((2 * SHARDS, 1, 128), f32)),
        in_specs=[pl.BlockSpec(memory_space=pltpu.SMEM)] + [pl.BlockSpec(memory_space=pltpu.VMEM)] * 2,
        compiler_params=pltpu.CompilerParams(vmem_limit_bytes=16 * 1024 * 1024),
        name="reduce",
    )(core, recv, stat)


def finish_kernel(core_ref, mine_ref, theirs_ref, lines_ref, embed_ref, conv_ref, in_ref, mid_ref, head_ref, std_ref):
    core = core_ref[0]
    lane1 = iota((1, 128), 1)
    total = jnp.sum(lines_ref[...], axis=0)
    scales = []
    for j in range(2):
        kind = 2 * core + j
        std = jnp.zeros((1, 128), f32)
        for z in range(8):
            std = std + lines_ref[4 * z + kind]
        std = jnp.where((lane1 >= 32) & (lane1 < 32 + ACT), std, 0.0)
        square = jnp.sum(std * std + jnp.where(lane1 == kind, total, 0.0), axis=1, keepdims=True)
        scale = 1.0 / jnp.sqrt(square / ENTRIES + 1e-06)
        std_ref[j : j + 1, :] = (std * scale)[:, 32 : 32 + ACT]
        scales.append(scale)

    def write(encoder_ref, trunk_ref):
        for j, scale in enumerate(scales):
            for q in range(6):
                conv_ref[j, q // 2, q % 2] = encoder_ref[j, 16 * q : 16 * q + 16, :] * scale
            embed_ref[:, j, :] = encoder_ref[j, 96:99, :] * scale
            for n in range(2):
                cols = slice(256 * n, 256 * n + 256)
                in_ref[j, :, cols] = trunk_ref[j, 16 * n : 16 * n + 16, :] * scale
                mid_ref[j, :, cols] = trunk_ref[j, 32 + 32 * n : 64 + 32 * n, :] * scale
            head_ref[0:8, j, :] = trunk_ref[j, 96:104, 0:32] * scale
            head_ref[8:13, j, :] = trunk_ref[j, 96:101, 32:64] * scale

    @pl.when(core == 0)
    def _():
        write(mine_ref, theirs_ref)

    @pl.when(core == 1)
    def _():
        write(theirs_ref, mine_ref)


def finish(core, mine, theirs, lines):
    shapes = ((3, 2, 256), (2, 3, 2, 16, 256), (2, 16, 512), (2, 32, 512), (13, 2, 32), (2, 12))
    embed, conv, first, second, head, std = pl.pallas_call(
        finish_kernel,
        out_shape=tuple(jax.ShapeDtypeStruct(s, f32) for s in shapes),
        in_specs=[pl.BlockSpec(memory_space=pltpu.SMEM)] + [pl.BlockSpec(memory_space=pltpu.VMEM)] * 3,
        compiler_params=pltpu.CompilerParams(vmem_limit_bytes=16 * 1024 * 1024),
        name="finish",
    )(core, mine, theirs, lines)
    return embed.transpose(1, 0, 2), conv, first, second, head.transpose(1, 2, 0), std


def swap(value):
    return lax.ppermute(value, "core", [(0, 1), (1, 0)])


def local(observations, rollout, done_flags, member_ids, embed_weight, conv_weight, trunk_in, trunk_mid, head_weight, log_std):
    x, core = lax.axis_index("x"), lax.axis_index("core")
    which, own = (x % 2).reshape(1), (core == x // 2).astype(jnp.int32).reshape(1)
    core = core.reshape(1)
    packed, weights = pack(
        which, observations, rollout, done_flags, member_ids, embed_weight, conv_weight, trunk_in, trunk_mid, head_weight
    )
    far = swap(weights)
    recv = lax.all_to_all(packed, ("y", "x"), split_axis=0, concat_axis=0, tiled=True)
    other = swap(log_std)
    weights = jnp.where(own[0] == 1, weights, far)
    keep, give, stat = member_grad(which, own, core, recv, weights, log_std, other)
    both = (keep.astype(f32) + swap(give).astype(f32)).astype(bf16)
    parts = lax.all_to_all(both, ("z", "x"), split_axis=0, concat_axis=0, tiled=True)
    mine, theirs, cast = reduce_parts(core, parts, stat)
    lines = lax.all_to_all(cast, ("core", "z", "x"), split_axis=0, concat_axis=0, tiled=True)
    return finish(core, mine, swap(theirs), lines)


def solution(mesh):
    fine = Mesh(mesh.devices.reshape(4, 2, 4, 4), ("y", "core", "z", "x"))
    member, dp = ("y", "core"), ("z", "x")
    every = member + dp
    return jax.shard_map(
        local,
        mesh=fine,
        in_specs=(P(every), P(every), P(every), P(every)) + (P(member),) * 6,
        out_specs=(
            P(member, dp),
            P(member, None, None, dp),
            P(member, dp),
            P(member, dp),
            P(member, dp),
            P(member),
        ),
        check_vma=False,
    )
```
